32 devices in a mesh: ht: 4 (over x, core), wt: 8 (over z, y).
Axes of the slice: x: 2, y: 2, z: 4, core: 2. Of those that a mesh axis runs over, the one named last changes fastest.
Arguments:
- queries: bfloat16 [64, 64, 1024], P('ht', 'wt'), may hold values from -30 to 30
- keys_new: bfloat16 [64, 64, 1024], P('ht', 'wt'), may hold values from -10 to 10, as said below
- values_new: bfloat16 [64, 64, 1024], P('ht', 'wt'), may hold values from -6 to 6
- keys_cache: bfloat16 [1, 64, 64, 1024], P(None, 'ht', 'wt'), may hold values from -10 to 10, as said below
- values_cache: bfloat16 [1, 64, 64, 1024], P(None, 'ht', 'wt'), may hold values from -6 to 6
- conv_weight: float32 [3, 3, 1024], replicated, may hold values from -2 to 2
- conv_bias: float32 [1024], replicated, may hold values from -2.5 to 2.5
Outputs:
- block_out: bfloat16 [64, 64, 1024], P('ht', 'wt')
The draws below stay inside these ranges and needn't reach their ends.
Inputs may be any that keep to these rules, and one draw needn't show every extreme that they name: `keys_new`: key features. `keys_cache`: key features.
All inputs are finite; a program needn't handle non-finite values.
Results may differ from the reference program's by a relative error of at most 0.003.
Values may be sent and summed in bfloat16 or wider, within the bound.
No kernel may reach another device: no remote copies, remote signals or barrier semaphores. Data moves between devices by JAX's collectives and lax.ppermute only.
A program may use at most 64 MiB of HBM per device.

```python
import jax
import jax.numpy as jnp
from jax import lax

HD = 128
WIN = 32
CACHED = 1
CHANNELS = 1024
FRAME_H = 64
FRAME_W = 64


def draw_queries(key, part):
    noise_key = jax.random.fold_in(key, 5)
    drawn = 2.5 * jnp.clip(jax.random.normal(noise_key, (FRAME_H, FRAME_W, CHANNELS), jnp.float32), -6.0, 6.0)
    return drawn.astype(jnp.bfloat16)


def draw_keys_new(key, part):
    noise_key = jax.random.fold_in(key, 6)
    drawn = jnp.clip(jax.random.normal(noise_key, (FRAME_H, FRAME_W, CHANNELS), jnp.float32), -6.0, 6.0)
    return drawn.astype(jnp.bfloat16)


def draw_keys_cache(key, part):
    noise_key = jax.random.fold_in(key, 7)
    drawn = jnp.clip(jax.random.normal(noise_key, (CACHED, FRAME_H, FRAME_W, CHANNELS), jnp.float32), -6.0, 6.0)
    return drawn.astype(jnp.bfloat16)


def levels(rng, shape, shards, least, high):
    gain = 1.0
    for dim, blocks in shards:
        steps = jax.random.uniform(jax.random.fold_in(jax.random.fold_in(rng, 6), dim), (blocks,), jnp.float32, least / len(shards), high / len(shards))
        gain = gain * jnp.repeat(jnp.exp(steps), shape[dim] // blocks).reshape((-1,) + (1,) * (len(shape) - 1 - dim))
    return gain


def centred(rng, shape, scale, reach, pieces=(), kind=jnp.bfloat16):
    entries = jax.random.normal(rng, shape, jnp.float32) * scale
    if len(pieces) > 0:
        entries = levels(rng, shape, pieces, -0.22, 0.18) * entries
    return jnp.clip(entries, min=-reach, max=reach).astype(kind)


def setup_inputs(seed: int = 0) -> dict:
    key_list = jax.random.split(jax.random.key(seed), 8)
    return {
        "queries": draw_queries(jax.random.fold_in(key_list[7], 71), 0),
        "keys_new": draw_keys_new(jax.random.fold_in(key_list[7], 71), 0),
        "values_new": centred(key_list[2], (FRAME_H, FRAME_W, CHANNELS), 1.0, 6.0, ((0, 4), (1, 8))),
        "keys_cache": draw_keys_cache(jax.random.fold_in(key_list[7], 71), 0),
        "values_cache": centred(key_list[4], (CACHED, FRAME_H, FRAME_W, CHANNELS), 1.0, 6.0, ((1, 4), (2, 8))),
        "conv_weight": centred(key_list[5], (3, 3, CHANNELS), 0.35, 2.0, (), jnp.float32),
        "conv_bias": centred(key_list[6], (CHANNELS,), 0.5, 2.5, (), jnp.float32),
    }


def window_allowed(row_start, col_start, frame_rows, frame_cols, tile_rows, tile_cols, half_win):
    ext_rows = jnp.arange(tile_rows + 2 * half_win, dtype=jnp.int32) - half_win
    ext_cols = jnp.arange(tile_cols + 2 * half_win, dtype=jnp.int32) - half_win
    query_rows = jnp.arange(tile_rows, dtype=jnp.int32)
    query_cols = jnp.arange(tile_cols, dtype=jnp.int32)
    row_delta = ext_rows[None, :] - query_rows[:, None]
    col_delta = ext_cols[None, :] - query_cols[:, None]
    global_rows = row_start + ext_rows
    global_cols = col_start + ext_cols
    row_valid = (row_delta >= -half_win) & (row_delta < half_win) & ((global_rows >= 0) & (global_rows < frame_rows))[None, :]
    col_valid = (col_delta >= -half_win) & (col_delta < half_win) & ((global_cols >= 0) & (global_cols < frame_cols))[None, :]
    allowed = row_valid[:, None, :, None] & col_valid[None, :, None, :]
    return allowed.reshape(tile_rows * tile_cols, (tile_rows + 2 * half_win) * (tile_cols + 2 * half_win))


def attend(query_rows, keys_flat, values_flat, allowed, heads, head_dim):
    score_scale = head_dim ** -0.5

    def one_head(head_index):
        lane_start = head_index * head_dim
        query_head = lax.dynamic_slice_in_dim(query_rows, lane_start, head_dim, 1).astype(jnp.float32)
        key_head = lax.dynamic_slice_in_dim(keys_flat, lane_start, head_dim, 1).astype(jnp.float32)
        value_head = lax.dynamic_slice_in_dim(values_flat, lane_start, head_dim, 1)
        scores = jnp.einsum("qd,kd->qk", query_head, key_head) * score_scale
        scores = jnp.where(allowed, scores, -1e30)
        row_top = jnp.max(scores, axis=1, keepdims=True)
        weights_f = jnp.exp(scores - row_top)
        denominator = jnp.sum(weights_f, axis=1, keepdims=True)
        numerator = jnp.dot(weights_f.astype(jnp.bfloat16), value_head, preferred_element_type=jnp.float32)
        return numerator / denominator

    outputs = lax.map(one_head, jnp.arange(heads, dtype=jnp.int32))
    return outputs.transpose(1, 0, 2).reshape(query_rows.shape[0], heads * head_dim)


def local_conv(padded, conv_weight, conv_bias, tile_rows, tile_cols):
    enhanced = jnp.zeros((tile_rows, tile_cols, padded.shape[2]), jnp.float32) + conv_bias
    for row_shift in range(3):
        for col_shift in range(3):
            enhanced = enhanced + padded[row_shift:row_shift + tile_rows, col_shift:col_shift + tile_cols].astype(jnp.float32) * conv_weight[row_shift, col_shift]
    return enhanced


def reference(queries, keys_new, values_new, keys_cache, values_cache, conv_weight, conv_bias):
    frame_rows, frame_cols, channels = queries.shape
    frames = keys_cache.shape[0] + 1
    half_win = WIN // 2
    stacked = jnp.concatenate([keys_cache, keys_new[None], values_cache, values_new[None]], axis=0)
    padded_all = jnp.pad(stacked, ((0, 0), (half_win, half_win), (half_win, half_win), (0, 0)))
    padded_values = jnp.pad(values_new, ((1, 1), (1, 1), (0, 0)))
    block_cols = frame_cols // WIN
    block_count = (frame_rows // WIN) * block_cols
    zero_index = jnp.int32(0)

    def one_block(block):
        row_start = ((block // block_cols) * WIN).astype(jnp.int32)
        col_start = ((block % block_cols) * WIN).astype(jnp.int32)
        query_block = lax.dynamic_slice(queries, (row_start, col_start, zero_index), (WIN, WIN, channels))
        region = lax.dynamic_slice(padded_all, (zero_index, row_start, col_start, zero_index), (2 * frames, 2 * WIN, 2 * WIN, channels))
        keys_flat = region[:frames].reshape(frames * 4 * WIN * WIN, channels)
        values_flat = region[frames:].reshape(frames * 4 * WIN * WIN, channels)
        allowed = jnp.tile(window_allowed(row_start, col_start, frame_rows, frame_cols, WIN, WIN, half_win), (1, frames))
        attended = attend(query_block.reshape(WIN * WIN, channels), keys_flat, values_flat, allowed, channels // HD, HD)
        beside_all = lax.dynamic_slice(padded_values, (row_start, col_start, zero_index), (WIN + 2, WIN + 2, channels))
        enhanced = local_conv(beside_all, conv_weight, conv_bias, WIN, WIN)
        return (attended.reshape(WIN, WIN, channels) + enhanced).astype(jnp.bfloat16)

    blocks = lax.map(one_block, jnp.arange(block_count, dtype=jnp.int32))
    blocks = blocks.reshape(frame_rows // WIN, block_cols, WIN, WIN, channels)
    return blocks.transpose(0, 2, 1, 3, 4).reshape(frame_rows, frame_cols, channels)
```

```python
import functools

import jax
import jax.numpy as jnp
from jax import lax
from jax.experimental import pallas as pl
from jax.experimental.pallas import tpu as pltpu
from jax.sharding import Mesh, PartitionSpec as P

HD = 128
WIN = 32


def with_halo(block, sides, width):
    for axis, dim in sides:
        count = lax.axis_size(axis)
        forward = [(i, i + 1) for i in range(count - 1)]
        backward = [(target, source) for source, target in forward]
        low = lax.ppermute(
            lax.slice_in_dim(block, block.shape[dim] - width, None, axis=dim), axis, forward
        )
        high = lax.ppermute(lax.slice_in_dim(block, 0, width, axis=dim), axis, backward)
        block = jnp.concatenate([low, block, high], axis=dim)
    return block


def window_allowed(row_start, col_start, frame_rows, frame_cols, tile_rows, tile_cols, half_win):
    ext_rows = jnp.arange(tile_rows + 2 * half_win, dtype=jnp.int32) - half_win
    ext_cols = jnp.arange(tile_cols + 2 * half_win, dtype=jnp.int32) - half_win
    query_rows = jnp.arange(tile_rows, dtype=jnp.int32)
    query_cols = jnp.arange(tile_cols, dtype=jnp.int32)
    row_delta = ext_rows[None, :] - query_rows[:, None]
    col_delta = ext_cols[None, :] - query_cols[:, None]
    global_rows = row_start + ext_rows
    global_cols = col_start + ext_cols
    row_valid = (
        (row_delta >= -half_win)
        & (row_delta < half_win)
        & ((global_rows >= 0) & (global_rows < frame_rows))[None, :]
    )
    col_valid = (
        (col_delta >= -half_win)
        & (col_delta < half_win)
        & ((global_cols >= 0) & (global_cols < frame_cols))[None, :]
    )
    allowed = row_valid[:, None, :, None] & col_valid[None, :, None, :]
    return allowed.reshape(
        tile_rows * tile_cols, (tile_rows + 2 * half_win) * (tile_cols + 2 * half_win)
    )


def attend(query_rows, keys_flat, values_flat, allowed, heads, head_dim):
    score_scale = head_dim ** (-0.5)

    def one_head(head_index):
        scores = (
            jnp.einsum("qd,kd->qk", query_rows, keys_flat, preferred_element_type=jnp.float32)
            * score_scale
        )
        scores = jnp.where(allowed, scores, -1e30)
        row_top = jnp.max(scores, axis=1, keepdims=True)
        weights_f = jnp.exp(scores - row_top)
        denominator = jnp.sum(weights_f, axis=1, keepdims=True)
        numerator = jnp.dot(
            weights_f.astype(jnp.bfloat16), values_flat, preferred_element_type=jnp.float32
        )
        return numerator / denominator

    outputs = lax.map(one_head, jnp.arange(heads, dtype=jnp.int32))
    return outputs.transpose(1, 0, 2).reshape(query_rows.shape[0], heads * head_dim)


def local_conv(padded, conv_weight, conv_bias, tile_rows, tile_cols):
    enhanced = jnp.zeros((tile_rows, tile_cols, padded.shape[2]), jnp.float32) + conv_bias
    for row_shift in range(3):
        for col_shift in range(3):
            enhanced = (
                enhanced
                + padded[
                    row_shift : row_shift + tile_rows, col_shift : col_shift + tile_cols
                ].astype(jnp.float32)
                * conv_weight[row_shift, col_shift]
            )
    return enhanced


def cycle_conv(values_new, conv_weight, conv_bias):
    tile_rows, tile_cols, channels = values_new.shape
    padded = with_halo(values_new, (("ht", 0), ("wt", 1)), 1)
    return local_conv(padded, conv_weight, conv_bias, tile_rows, tile_cols)


def shards(queries, keys_new, values_new, keys_cache, values_cache, conv_weight, conv_bias):
    tile_rows, tile_cols, channels = queries.shape
    frames = keys_cache.shape[0] + 1
    half_win = WIN // 2
    stacked = jnp.concatenate([keys_cache, keys_new[None], values_cache, values_new[None]], axis=0)
    row_start = lax.axis_index("ht") * tile_rows
    frame_rows = tile_rows * lax.axis_size("ht")
    frame_cols = tile_cols * lax.axis_size("wt")
    heads = channels // HD
    copies = lax.axis_size("wt") // heads
    bundle = jnp.concatenate([stacked, queries[None]], axis=0)
    members = bundle.shape[0]
    spread = bundle.reshape(members, tile_rows, tile_cols, 1, heads, HD)
    spread = jnp.broadcast_to(spread, (members, tile_rows, tile_cols, copies, heads, HD))
    spread = spread.reshape(members, tile_rows, tile_cols, copies * heads, HD)
    strips = lax.all_to_all(spread, "wt", split_axis=3, concat_axis=2, tiled=True)
    strips = strips.reshape(members, tile_rows, frame_cols, HD)
    device_index = lax.axis_index("wt")
    my_group = device_index // heads
    block_width = tile_cols * heads
    block_start = my_group * block_width
    padded_cols = jnp.pad(strips, ((0, 0), (0, 0), (half_win, half_win), (0, 0)))
    window = lax.dynamic_slice_in_dim(padded_cols, block_start, block_width + 2 * half_win, 2)
    query_part = window[2 * frames, :, half_win : half_win + block_width]
    region = with_halo(window[: 2 * frames], (("ht", 1),), half_win)

    def one_block(step):
        offset = step * tile_cols
        query_block = lax.dynamic_slice_in_dim(query_part, offset, tile_cols, 1).reshape(
            tile_rows * tile_cols, HD
        )
        sub = lax.dynamic_slice_in_dim(region, offset, tile_cols + 2 * half_win, 2)
        keys_flat = sub[:frames].reshape(-1, HD)
        values_flat = sub[frames:].reshape(-1, HD)
        allowed = window_allowed(
            row_start, block_start + offset, frame_rows, frame_cols, tile_rows, tile_cols, half_win
        )
        allowed = jnp.tile(allowed, (1, frames))
        result = attend(query_block, keys_flat, values_flat, allowed, 1, HD)
        return result.reshape(tile_rows, tile_cols, HD)

    blocks = lax.map(one_block, jnp.arange(heads, dtype=jnp.int32))
    payload = blocks.transpose(1, 0, 2, 3)
    payload = jnp.broadcast_to(payload[:, None], (tile_rows, copies, heads, tile_cols, HD))
    payload = payload.reshape(tile_rows, copies * heads, tile_cols, HD)
    returned = lax.all_to_all(
        payload.astype(jnp.bfloat16), "wt", split_axis=1, concat_axis=1, tiled=True
    ).astype(payload.dtype)
    own = lax.dynamic_slice_in_dim(returned, my_group * heads, heads, 1)
    combined = own.transpose(0, 2, 1, 3).reshape(tile_rows, tile_cols, channels)
    combined = combined + cycle_conv(values_new, conv_weight, conv_bias)
    return combined.astype(jnp.bfloat16)


LOG2E = 1.4426950408889634
NEG = -1e30
VMEM = pl.BlockSpec(memory_space=pltpu.VMEM)
SMEM = pl.BlockSpec(memory_space=pltpu.SMEM)


def index_of(position, shape, dim):
    return lax.broadcasted_iota(jnp.int32, shape, dim) if position is None else position


def tile_masks(tile_rows, tile_cols):
    size = tile_rows * tile_cols
    query = lax.broadcasted_iota(jnp.int32, (size, size), 0)
    key = lax.broadcasted_iota(jnp.int32, (size, size), 1)
    upper = key // tile_cols >= query // tile_cols
    left = key % tile_cols >= query % tile_cols
    return upper, left


def attend_kernel(grid_rows, grid_cols, tile_rows, tile_cols, info_ref, weight_ref, bias_ref, q_ref, *refs):
    out_ref = refs[-1]
    frames = [refs[3 * f : 3 * f + 3] for f in range((len(refs) - 1) // 3)]
    size = tile_rows * tile_cols
    scale = HD ** (-0.5) * LOG2E
    bias_left = jnp.where(info_ref[0] > 0, 0.0, NEG).astype(jnp.float32)
    bias_right = jnp.where(info_ref[1] > 0, 0.0, NEG).astype(jnp.float32)
    upper, left = tile_masks(tile_rows, tile_cols)
    upper_one = upper.astype(jnp.float32).astype(jnp.bfloat16)
    left_one = left.astype(jnp.float32).astype(jnp.bfloat16)
    lower_one = 1 - upper_one
    right_one = 1 - left_one
    ones = jnp.ones((size, HD), jnp.bfloat16)

    def slot(row, col):
        return info_ref[2 + row * grid_cols + col]

    def tile(frame, part, row, col):
        side = 1 if col < 0 else (2 if col >= grid_cols else 0)
        return frames[frame][side][slot(row, col % grid_cols), part].reshape(size, HD)

    def piece(row, col):
        query = q_ref[slot(row, col)].reshape(size, HD)

        def score(frame, key_row, key_col):
            raw = lax.dot_general(
                query, tile(frame, 0, key_row, key_col), (((1,), (1,)), ((), ())),
                preferred_element_type=jnp.float32,
            )
            if key_col < 0:
                raw = raw + bias_left
            elif key_col >= grid_cols:
                raw = raw + bias_right
            return raw

        up, down = row > 0, row + 1 < grid_rows

        def beside(frame, key_col):
            if up and down:
                return jnp.where(upper, score(frame, row - 1, key_col), score(frame, row + 1, key_col))
            if down:
                return jnp.where(upper, NEG, score(frame, row + 1, key_col))
            return jnp.where(upper, score(frame, row - 1, key_col), NEG)

        blocks = []
        for frame in range(len(frames)):
            for step in (-1, 0, 1):
                blocks.append((frame, False, step, score(frame, row, col + step)))
                blocks.append((frame, True, step, beside(frame, col + step)))
            blocks.append((frame, False, 2, jnp.where(left, score(frame, row, col - 2), score(frame, row, col + 2))))
            blocks.append((frame, True, 2, jnp.where(left, beside(frame, col - 2), beside(frame, col + 2))))
        top = blocks[0][3]
        for entry in blocks[1:]:
            top = jnp.maximum(top, entry[3])
        top = jnp.max(top, axis=1, keepdims=True)
        total = jnp.zeros((size, 2 * HD), jnp.float32)
        for frame, off_row, step, raw in blocks:
            weights = jnp.exp2((raw - top) * scale).astype(jnp.bfloat16)
            if off_row and up and down:
                by_row = [(row - 1, weights * upper_one), (row + 1, weights * lower_one)]
            elif off_row:
                by_row = [(row + 1 if down else row - 1, weights)]
            else:
                by_row = [(row, weights)]
            parts = []
            for key_row, part in by_row:
                if step == 2:
                    parts.append((key_row, col - 2, part * left_one))
                    parts.append((key_row, col + 2, part * right_one))
                else:
                    parts.append((key_row, col + step, part))
            for key_row, key_col, part in parts:
                wide = jnp.concatenate([tile(frame, 1, key_row, key_col), ones], axis=1)
                total = total + jnp.dot(part, wide, preferred_element_type=jnp.float32)
        return total[:, :HD] / total[:, HD:]

    last = len(frames) - 1
    sub = lax.broadcasted_iota(jnp.int32, (tile_cols, HD), 0)
    taps = [[weight_ref[a, pl.ds(b, 1), :] for b in range(3)] for a in range(3)]

    def enhanced(row, col):
        lines = []
        for key_row in range(row * tile_rows - 1, (row + 1) * tile_rows + 1):
            tile_row, line = key_row // tile_rows, key_row % tile_rows
            if tile_row < 0 or tile_row >= grid_rows:
                lines.append(None)
                continue

            def values(key_col):
                side = 1 if key_col < 0 else (2 if key_col >= grid_cols else 0)
                return frames[last][side][slot(tile_row, key_col % grid_cols), 1, line].astype(jnp.float32)

            here, before, after = values(col), values(col - 1), values(col + 1)
            low = jnp.where(sub == 0, pltpu.roll(before, 1, 0), pltpu.roll(here, 1, 0))
            high = jnp.where(sub == tile_cols - 1, pltpu.roll(after, tile_cols - 1, 0), pltpu.roll(here, tile_cols - 1, 0))
            lines.append((low, here, high))
        sums = []
        for line in range(tile_rows):
            total = jnp.broadcast_to(bias_ref[...], (tile_cols, HD))
            for a in range(3):
                if lines[line + a] is not None:
                    for b in range(3):
                        total = total + lines[line + a][b] * taps[a][b]
            sums.append(total)
        return jnp.stack(sums, axis=0)

    for row in range(grid_rows):
        for col in range(grid_cols):
            attended = piece(row, col).reshape(tile_rows, tile_cols, HD)
            out_ref[slot(row, col)] = (attended + enhanced(row, col)).astype(jnp.bfloat16)


def pack_kernel(heads, q_ref, kn_ref, vn_ref, kc_ref, vc_ref, first_ref, second_ref):
    for head in range(heads):
        lanes = pl.ds(head * HD, HD)
        first_ref[head, 0] = kc_ref[0, :, :, lanes]
        first_ref[head, 1] = vc_ref[0, :, :, lanes]
        second_ref[head, 0] = kn_ref[:, :, lanes]
        second_ref[head, 1] = vn_ref[:, :, lanes]
        second_ref[head, 2] = q_ref[:, :, lanes]


def head_shards(shape, queries, keys_new, values_new, keys_cache, values_cache, conv_weight, conv_bias):
    group_rows, group_cols, far = shape
    tile_rows, tile_cols, channels = queries.shape
    heads = channels // HD
    group = ("ht", "near")
    block = (tile_rows, tile_cols, HD)
    first, second = pl.pallas_call(
        functools.partial(pack_kernel, heads),
        out_shape=(
            jax.ShapeDtypeStruct((heads, 2) + block, jnp.bfloat16),
            jax.ShapeDtypeStruct((heads, 3) + block, jnp.bfloat16),
        ),
        in_specs=[VMEM] * 5,
        out_specs=(VMEM, VMEM),
    )(queries, keys_new, values_new, keys_cache, values_cache)

    def exchange(x):
        return lax.all_to_all(x, group, split_axis=0, concat_axis=0, tiled=True)

    up = [(i, i + 1) for i in range(far - 1)]
    down = [(i + 1, i) for i in range(far - 1)]

    def halo(x):
        return lax.ppermute(x, "far", up), lax.ppermute(x, "far", down)

    cached = exchange(first)
    cached_left, cached_right = halo(cached)
    second, _ = lax.optimization_barrier((second, cached))
    current = exchange(second)
    new, query = current[:, :2], current[:, 2]
    new_left, new_right = halo(new)
    far_index = lax.axis_index("far")
    head = lax.axis_index("ht") * group_cols + lax.axis_index("near")
    info = jnp.concatenate(
        [
            jnp.stack([far_index > 0, far_index < far - 1]).astype(jnp.int32),
            jnp.arange(heads, dtype=jnp.int32),
        ]
    )
    weight = lax.dynamic_slice_in_dim(conv_weight, head * HD, HD, 2)
    bias = lax.dynamic_slice_in_dim(conv_bias.reshape(1, channels), head * HD, HD, 1)
    result = pl.pallas_call(
        functools.partial(attend_kernel, group_rows, group_cols, tile_rows, tile_cols),
        out_shape=jax.ShapeDtypeStruct((heads,) + block, jnp.bfloat16),
        in_specs=[SMEM] + [VMEM] * 9,
        out_specs=VMEM,
        compiler_params=pltpu.CompilerParams(vmem_limit_bytes=48 * 1024 * 1024),
    )(info, weight, bias, query, cached, cached_left, cached_right, new, new_left, new_right)
    returned = exchange(result)
    return returned.transpose(1, 2, 0, 3).reshape(tile_rows, tile_cols, channels)


def grouping(mesh, heads):
    rows, cols = mesh.shape["ht"], mesh.shape["wt"]
    group_rows = rows
    group_cols = heads // group_rows if heads % group_rows == 0 else 0
    if group_cols != 2 or cols % group_cols:
        return None
    return group_rows, group_cols, cols // group_cols


def solution(mesh):
    def program(queries, *rest):
        heads = queries.shape[2] // HD
        shape = grouping(mesh, heads)
        if shape is None or queries.shape[0] != mesh.shape["ht"] * (WIN // 2) or queries.shape[1] != mesh.shape["wt"] * (WIN // 4):
            placed = (P("ht", "wt", None),) * 3 + (P(None, "ht", "wt", None),) * 2 + (P(), P())
            return jax.shard_map(
                shards, mesh=mesh, in_specs=placed, out_specs=P("ht", "wt", None), check_vma=False
            )(queries, *rest)
        devices = mesh.devices.reshape(shape[0], shape[2], shape[1])
        split = Mesh(devices, ("ht", "far", "near"))
        tile = P("ht", ("far", "near"), None)
        past = P(None, "ht", ("far", "near"), None)
        return jax.shard_map(
            functools.partial(head_shards, shape),
            mesh=split,
            in_specs=(tile, tile, tile, past, past, P(), P()),
            out_specs=tile,
            check_vma=False,
        )(queries, *rest)

    return program
```

```python
import functools

import jax
import jax.numpy as jnp
from jax import lax
from jax.experimental import pallas as pl
from jax.experimental.pallas import tpu as pltpu
from jax.sharding import Mesh, PartitionSpec as P


HD = 128
WIN = 32


def with_halo(block, sides, width):
    for axis, dim in sides:
        count = lax.axis_size(axis)
        forward = [(i, i + 1) for i in range(count - 1)]
        backward = [(target, source) for source, target in forward]
        low = lax.ppermute(
            lax.slice_in_dim(block, block.shape[dim] - width, None, axis=dim), axis, forward
        )
        high = lax.ppermute(lax.slice_in_dim(block, 0, width, axis=dim), axis, backward)
        block = jnp.concatenate([low, block, high], axis=dim)
    return block


def window_allowed(row_start, col_start, frame_rows, frame_cols, tile_rows, tile_cols, half_win):
    ext_rows = jnp.arange(tile_rows + 2 * half_win, dtype=jnp.int32) - half_win
    ext_cols = jnp.arange(tile_cols + 2 * half_win, dtype=jnp.int32) - half_win
    query_rows = jnp.arange(tile_rows, dtype=jnp.int32)
    query_cols = jnp.arange(tile_cols, dtype=jnp.int32)
    row_delta = ext_rows[None, :] - query_rows[:, None]
    col_delta = ext_cols[None, :] - query_cols[:, None]
    global_rows = row_start + ext_rows
    global_cols = col_start + ext_cols
    row_valid = (
        (row_delta >= -half_win)
        & (row_delta < half_win)
        & ((global_rows >= 0) & (global_rows < frame_rows))[None, :]
    )
    col_valid = (
        (col_delta >= -half_win)
        & (col_delta < half_win)
        & ((global_cols >= 0) & (global_cols < frame_cols))[None, :]
    )
    allowed = row_valid[:, None, :, None] & col_valid[None, :, None, :]
    return allowed.reshape(
        tile_rows * tile_cols, (tile_rows + 2 * half_win) * (tile_cols + 2 * half_win)
    )


def attend(query_rows, keys_flat, values_flat, allowed, heads, head_dim):
    score_scale = head_dim ** (-0.5)

    def one_head(head_index):
        scores = (
            jnp.einsum("qd,kd->qk", query_rows, keys_flat, preferred_element_type=jnp.float32)
            * score_scale
        )
        scores = jnp.where(allowed, scores, -1e30)
        row_top = jnp.max(scores, axis=1, keepdims=True)
        weights_f = jnp.exp(scores - row_top)
        denominator = jnp.sum(weights_f, axis=1, keepdims=True)
        numerator = jnp.dot(
            weights_f.astype(jnp.bfloat16), values_flat, preferred_element_type=jnp.float32
        )
        return numerator / denominator

    outputs = lax.map(one_head, jnp.arange(heads, dtype=jnp.int32))
    return outputs.transpose(1, 0, 2).reshape(query_rows.shape[0], heads * head_dim)


def local_conv(padded, conv_weight, conv_bias, tile_rows, tile_cols):
    enhanced = jnp.zeros((tile_rows, tile_cols, padded.shape[2]), jnp.float32) + conv_bias
    for row_shift in range(3):
        for col_shift in range(3):
            enhanced = (
                enhanced
                + padded[
                    row_shift : row_shift + tile_rows, col_shift : col_shift + tile_cols
                ].astype(jnp.float32)
                * conv_weight[row_shift, col_shift]
            )
    return enhanced


def cycle_conv(values_new, conv_weight, conv_bias):
    tile_rows, tile_cols, _ = values_new.shape
    padded = with_halo(values_new, (("ht", 0), ("wt", 1)), 1)
    return local_conv(padded, conv_weight, conv_bias, tile_rows, tile_cols)


def shards(queries, keys_new, values_new, keys_cache, values_cache, conv_weight, conv_bias):
    tile_rows, tile_cols, channels = queries.shape
    frames = keys_cache.shape[0] + 1
    half_win = WIN // 2
    stacked = jnp.concatenate([keys_cache, keys_new[None], values_cache, values_new[None]], axis=0)
    row_start = lax.axis_index("ht") * tile_rows
    frame_rows = tile_rows * lax.axis_size("ht")
    frame_cols = tile_cols * lax.axis_size("wt")
    heads = channels // HD
    copies = lax.axis_size("wt") // heads
    bundle = jnp.concatenate([stacked, queries[None]], axis=0)
    members = bundle.shape[0]
    spread = bundle.reshape(members, tile_rows, tile_cols, 1, heads, HD)
    spread = jnp.broadcast_to(spread, (members, tile_rows, tile_cols, copies, heads, HD))
    spread = spread.reshape(members, tile_rows, tile_cols, copies * heads, HD)
    strips = lax.all_to_all(spread, "wt", split_axis=3, concat_axis=2, tiled=True)
    strips = strips.reshape(members, tile_rows, frame_cols, HD)
    device_index = lax.axis_index("wt")
    my_group = device_index // heads
    block_width = tile_cols * heads
    block_start = my_group * block_width
    padded_cols = jnp.pad(strips, ((0, 0), (0, 0), (half_win, half_win), (0, 0)))
    window = lax.dynamic_slice_in_dim(padded_cols, block_start, block_width + 2 * half_win, 2)
    query_part = window[2 * frames, :, half_win : half_win + block_width]
    region = with_halo(window[: 2 * frames], (("ht", 1),), half_win)

    def one_block(step):
        offset = step * tile_cols
        query_block = lax.dynamic_slice_in_dim(query_part, offset, tile_cols, 1).reshape(
            tile_rows * tile_cols, HD
        )
        sub = lax.dynamic_slice_in_dim(region, offset, tile_cols + 2 * half_win, 2)
        keys_flat = sub[:frames].reshape(-1, HD)
        values_flat = sub[frames:].reshape(-1, HD)
        allowed = window_allowed(
            row_start, block_start + offset, frame_rows, frame_cols, tile_rows, tile_cols, half_win
        )
        allowed = jnp.tile(allowed, (1, frames))
        result = attend(query_block, keys_flat, values_flat, allowed, 1, HD)
        return result.reshape(tile_rows, tile_cols, HD)

    blocks = lax.map(one_block, jnp.arange(heads, dtype=jnp.int32))
    payload = blocks.transpose(1, 0, 2, 3)
    payload = jnp.broadcast_to(payload[:, None], (tile_rows, copies, heads, tile_cols, HD))
    payload = payload.reshape(tile_rows, copies * heads, tile_cols, HD)
    returned = lax.all_to_all(
        payload.astype(jnp.bfloat16), "wt", split_axis=1, concat_axis=1, tiled=True
    ).astype(payload.dtype)
    own = lax.dynamic_slice_in_dim(returned, my_group * heads, heads, 1)
    combined = own.transpose(0, 2, 1, 3).reshape(tile_rows, tile_cols, channels)
    combined = combined + cycle_conv(values_new, conv_weight, conv_bias)
    return combined.astype(jnp.bfloat16)


LOG2E = 1.4426950408889634
NEG = -1e30
VMEM = pl.BlockSpec(memory_space=pltpu.VMEM)
SMEM = pl.BlockSpec(memory_space=pltpu.SMEM)
LIMIT = pltpu.CompilerParams(vmem_limit_bytes=48 * 1024 * 1024)


def tile_masks(tile_rows, tile_cols):
    size = tile_rows * tile_cols
    query = lax.broadcasted_iota(jnp.int32, (size, size), 0)
    key = lax.broadcasted_iota(jnp.int32, (size, size), 1)
    upper = key // tile_cols >= query // tile_cols
    left = key % tile_cols >= query % tile_cols
    return upper, left


class Window:
    def __init__(self, grid, tile, info_ref, q_ref, sides):
        self.grid_rows, self.grid_cols = grid
        self.tile_rows, self.tile_cols = tile
        self.size = self.tile_rows * self.tile_cols
        self.info, self.q, self.sides = info_ref, q_ref, sides
        self.scale = HD ** (-0.5) * LOG2E
        self.bias_left = jnp.where(info_ref[0] > 0, 0.0, NEG).astype(jnp.float32)
        self.bias_right = jnp.where(info_ref[1] > 0, 0.0, NEG).astype(jnp.float32)
        self.upper, self.left = tile_masks(self.tile_rows, self.tile_cols)
        self.upper_one = self.upper.astype(jnp.float32).astype(jnp.bfloat16)
        self.left_one = self.left.astype(jnp.float32).astype(jnp.bfloat16)
        self.ones = jnp.ones((self.size, HD), jnp.bfloat16)

    def slot(self, row, col):
        return self.info[2 + row * self.grid_cols + col]

    def side(self, col):
        return 1 if col < 0 else (2 if col >= self.grid_cols else 0)

    def tile(self, frame, part, row, col):
        ref = self.sides[frame][self.side(col)]
        return ref[self.slot(row, col % self.grid_cols), part].reshape(self.size, HD)

    def score(self, query, frame, row, col):
        raw = lax.dot_general(
            query, self.tile(frame, 0, row, col), (((1,), (1,)), ((), ())),
            preferred_element_type=jnp.float32,
        )
        if self.side(col) == 1:
            raw = raw + self.bias_left
        elif self.side(col) == 2:
            raw = raw + self.bias_right
        return raw

    def attend(self, row, col, wanted):
        query = self.q[self.slot(row, col)].reshape(self.size, HD)
        up, down = row > 0, row + 1 < self.grid_rows

        def beside(frame, key_col):
            if up and down:
                above = self.score(query, frame, row - 1, key_col)
                return jnp.where(self.upper, above, self.score(query, frame, row + 1, key_col))
            if down:
                return jnp.where(self.upper, NEG, self.score(query, frame, row + 1, key_col))
            return jnp.where(self.upper, self.score(query, frame, row - 1, key_col), NEG)

        def level(frame, key_col):
            return self.score(query, frame, row, key_col)

        blocks = []
        for frame, step in wanted:
            for off_row, make in ((False, level), (True, beside)):
                if off_row and not (up or down):
                    continue
                if step == 2:
                    raw = jnp.where(self.left, make(frame, col - 2), make(frame, col + 2))
                else:
                    raw = make(frame, col + step)
                blocks.append((frame, off_row, step, raw))
        top = blocks[0][3]
        for entry in blocks[1:]:
            top = jnp.maximum(top, entry[3])
        return blocks, jnp.max(top, axis=1, keepdims=True)

    def weigh(self, row, col, blocks, top):
        up, down = row > 0, row + 1 < self.grid_rows
        total = jnp.zeros((self.size, 2 * HD), jnp.float32)
        for frame, off_row, step, raw in blocks:
            weights = jnp.exp2((raw - top) * self.scale).astype(jnp.bfloat16)
            if off_row and up and down:
                by_row = [(row - 1, weights * self.upper_one), (row + 1, weights * (1 - self.upper_one))]
            elif off_row:
                by_row = [(row + 1 if down else row - 1, weights)]
            else:
                by_row = [(row, weights)]
            for key_row, part in by_row:
                if step == 2:
                    pair = [(col - 2, part * self.left_one), (col + 2, part * (1 - self.left_one))]
                else:
                    pair = [(col + step, part)]
                for key_col, one in pair:
                    wide = jnp.concatenate([self.tile(frame, 1, key_row, key_col), self.ones], axis=1)
                    total = total + jnp.dot(one, wide, preferred_element_type=jnp.float32)
        return total

    def inner_steps(self, col):
        near = [step for step in (-1, 0, 1) if 0 <= col + step < self.grid_cols]
        return near, [step for step in (-1, 0, 1, 2) if step not in near]


def early_kernel(grid, tile, info_ref, q_ref, c_ref, cl_ref, cr_ref, n_ref, sum_ref, top_ref):
    window = Window(grid, tile, info_ref, q_ref, [[c_ref, cl_ref, cr_ref], [n_ref, None, None]])
    for row in range(grid[0]):
        for col in range(grid[1]):
            near, _ = window.inner_steps(col)
            wanted = [(0, step) for step in (-1, 0, 1, 2)] + [(1, step) for step in near]
            blocks, top = window.attend(row, col, wanted)
            sum_ref[row * grid[1] + col] = window.weigh(row, col, blocks, top)
            top_ref[row * grid[1] + col] = jnp.broadcast_to(top, (window.size, HD))


def late_kernel(
    grid, tile, info_ref, weight_ref, bias_ref, q_ref, n_ref, nl_ref, nr_ref, sum_ref, top_ref, out_ref
):
    window = Window(grid, tile, info_ref, q_ref, [None, [n_ref, nl_ref, nr_ref]])
    grid_rows, grid_cols = grid
    tile_rows, tile_cols = tile
    sub = lax.broadcasted_iota(jnp.int32, (tile_cols, HD), 0)
    taps = [[weight_ref[a, pl.ds(b, 1), :] for b in range(3)] for a in range(3)]

    def enhanced(row, col):
        lines = []
        for key_row in range(row * tile_rows - 1, (row + 1) * tile_rows + 1):
            tile_row, line = key_row // tile_rows, key_row % tile_rows
            if tile_row < 0 or tile_row >= grid_rows:
                lines.append(None)
                continue

            def values(key_col):
                ref = window.sides[1][window.side(key_col)]
                return ref[window.slot(tile_row, key_col % grid_cols), 1, line].astype(jnp.float32)

            here, before, after = values(col), values(col - 1), values(col + 1)
            low = jnp.where(sub == 0, pltpu.roll(before, 1, 0), pltpu.roll(here, 1, 0))
            high = jnp.where(
                sub == tile_cols - 1, pltpu.roll(after, tile_cols - 1, 0), pltpu.roll(here, tile_cols - 1, 0)
            )
            lines.append((low, here, high))
        sums = []
        for line in range(tile_rows):
            total = jnp.broadcast_to(bias_ref[...], (tile_cols, HD))
            for a in range(3):
                if lines[line + a] is not None:
                    for b in range(3):
                        total = total + lines[line + a][b] * taps[a][b]
            sums.append(total)
        return jnp.stack(sums, axis=0)

    for row in range(grid_rows):
        for col in range(grid_cols):
            _, wanted = window.inner_steps(col)
            blocks, top = window.attend(row, col, [(1, step) for step in wanted])
            before = top_ref[row * grid_cols + col][:, :1]
            best = jnp.maximum(top, before)
            total = window.weigh(row, col, blocks, best)
            total = total + sum_ref[row * grid_cols + col] * jnp.exp2((before - best) * window.scale)
            attended = (total[:, :HD] / total[:, HD:]).reshape(tile_rows, tile_cols, HD)
            place = info_ref[2 + grid_rows * grid_cols + row * grid_cols + col]
            out_ref[place // 2, place % 2] = (attended + enhanced(row, col)).astype(jnp.bfloat16)


def lanes(head):
    return pl.ds(pl.multiple_of(head * HD, HD), HD)


def pack_kernel(members, flips, side, me_ref, *refs):
    sources, buffers = refs[:members], refs[members:]
    for buffer, flip in zip(buffers, flips):
        for other in range(2):
            head = me_ref[0] ^ (flip ^ (side if other else 0))
            for member, source in enumerate(sources):
                buffer[other, member] = source[:, :, lanes(head)]


def unpack_kernel(flips, side, me_ref, *refs):
    out_ref, beside_ref = refs[-1], refs[-2]
    for i, flip in enumerate(flips):
        out_ref[:, :, lanes(me_ref[0] ^ flip)] = refs[i][0]
        out_ref[:, :, lanes(me_ref[0] ^ (flip ^ side))] = beside_ref[i]


def head_step(shape, queries, keys_new, values_new, keys_cache, values_cache, conv_weight, conv_bias):
    group_rows, group_cols, far = shape
    tile_rows, tile_cols, channels = queries.shape
    heads = channels // HD
    grid, tile = (group_rows, group_cols), (tile_rows, tile_cols)
    axes = ("ht", "near")
    block = (tile_rows, tile_cols, HD)
    side = group_cols
    flips = [flip for flip in range(heads) if not flip & side]
    me = lax.axis_index("ht") * group_cols + lax.axis_index("near")
    me = me.astype(jnp.int32)
    me_ref = me.reshape(1)

    def swap(x, flip):
        return lax.ppermute(x, axes, [(s, s ^ flip) for s in range(heads)])

    def pack(*arrays):
        return pl.pallas_call(
            functools.partial(pack_kernel, len(arrays), flips, side),
            out_shape=[jax.ShapeDtypeStruct((2, len(arrays)) + block, jnp.bfloat16)] * len(flips),
            in_specs=[SMEM] + [VMEM] * len(arrays),
            out_specs=[VMEM] * len(flips),
            cost_estimate=pl.CostEstimate(flops=0, bytes_accessed=len(arrays) << 20, transcendentals=0),
        )(me_ref, *arrays)

    def gather(buffers):
        got = [buffers[0]] + [swap(b, flip) for b, flip in zip(buffers[1:], flips[1:])]
        forward = jnp.stack([b[1] for b in got])
        beside = swap(forward, side)
        return jnp.concatenate([jnp.stack([b[0] for b in got]), beside], axis=0)

    up = [(i, i + 1) for i in range(far - 1)]
    down = [(i + 1, i) for i in range(far - 1)]

    def halo(x):
        return lax.ppermute(x, "far", up), lax.ppermute(x, "far", down)

    packed_cached = pack(keys_cache[0], values_cache[0])
    packed_current = pack(keys_new, values_new, queries)
    cached = gather(packed_cached)
    cached_left, cached_right = halo(cached)
    current = gather(packed_current)
    new, query = current[:, :2], current[:, 2]
    new_left, new_right = halo(new)
    far_index = lax.axis_index("far")
    flip = me ^ jnp.arange(heads, dtype=jnp.int32)
    beside = (flip // side) % 2
    order = flip % side + flip // (2 * side) * side
    info = jnp.concatenate(
        [
            jnp.stack([far_index > 0, far_index < far - 1]).astype(jnp.int32),
            beside * len(flips) + order,
            order * 2 + beside,
        ]
    )
    weight = lax.dynamic_slice_in_dim(conv_weight, me * HD, HD, 2)
    bias = lax.dynamic_slice_in_dim(conv_bias.reshape(1, channels), me * HD, HD, 1)
    size = tile_rows * tile_cols
    sums, tops = pl.pallas_call(
        functools.partial(early_kernel, grid, tile),
        out_shape=(
            jax.ShapeDtypeStruct((heads, size, 2 * HD), jnp.float32),
            jax.ShapeDtypeStruct((heads, size, HD), jnp.float32),
        ),
        in_specs=[SMEM] + [VMEM] * 5,
        out_specs=(VMEM, VMEM),
        compiler_params=LIMIT,
        cost_estimate=pl.CostEstimate(flops=2**32, bytes_accessed=2**22, transcendentals=2**21),
    )(info, query, cached, cached_left, cached_right, new)
    result = pl.pallas_call(
        functools.partial(late_kernel, grid, tile),
        out_shape=jax.ShapeDtypeStruct((len(flips), 2) + block, jnp.bfloat16),
        in_specs=[SMEM] + [VMEM] * 8,
        out_specs=VMEM,
        compiler_params=LIMIT,
        cost_estimate=pl.CostEstimate(flops=2**30, bytes_accessed=2**22, transcendentals=2**19),
    )(info, weight, bias, query, new, new_left, new_right, sums, tops)
    got = [result[0]] + [swap(result[i], flips[i]) for i in range(1, len(flips))]
    other = swap(jnp.stack([b[1] for b in got]), side)
    return pl.pallas_call(
        functools.partial(unpack_kernel, flips, side),
        out_shape=jax.ShapeDtypeStruct(queries.shape, jnp.bfloat16),
        in_specs=[SMEM] + [VMEM] * (len(flips) + 1),
        out_specs=VMEM,
    )(me_ref, *got, other)


def grouping(mesh, heads):
    rows, cols = mesh.shape["ht"], mesh.shape["wt"]
    group_rows = rows
    group_cols = heads // group_rows if heads % group_rows == 0 else 0
    if group_cols != 2 or cols % group_cols:
        return None
    return group_rows, group_cols, cols // group_cols


def solution(mesh):
    def program(queries, *rest):
        heads = queries.shape[2] // HD
        shape = grouping(mesh, heads)
        if shape is None or queries.shape[0] != mesh.shape["ht"] * (WIN // 2) or queries.shape[1] != mesh.shape["wt"] * (WIN // 4):
            placed = (P("ht", "wt", None),) * 3 + (P(None, "ht", "wt", None),) * 2 + (P(), P())
            return jax.shard_map(
                shards, mesh=mesh, in_specs=placed, out_specs=P("ht", "wt", None), check_vma=False
            )(queries, *rest)
        devices = mesh.devices.reshape(shape[0], shape[2], shape[1])
        split = Mesh(devices, ("ht", "far", "near"))
        tile = P("ht", ("far", "near"), None)
        past = P(None, "ht", ("far", "near"), None)
        step = jax.shard_map(
            functools.partial(head_step, shape),
            mesh=split,
            in_specs=(tile, tile, tile, past, past, P(), P()),
            out_specs=tile,
            check_vma=False,
        )
        return step(queries, *rest)

    return program
```

```python
import functools

import jax
import jax.numpy as jnp
from jax import lax
from jax.experimental import pallas as pl
from jax.experimental.pallas import tpu as pltpu
from jax.sharding import Mesh, PartitionSpec as P


HD = 128
WIN = 32


def with_halo(block, sides, width):
    for axis, dim in sides:
        count = lax.axis_size(axis)
        forward = [(i, i + 1) for i in range(count - 1)]
        backward = [(target, source) for source, target in forward]
        low = lax.ppermute(
            lax.slice_in_dim(block, block.shape[dim] - width, None, axis=dim), axis, forward
        )
        high = lax.ppermute(lax.slice_in_dim(block, 0, width, axis=dim), axis, backward)
        block = jnp.concatenate([low, block, high], axis=dim)
    return block


def window_allowed(row_start, col_start, frame_rows, frame_cols, tile_rows, tile_cols, half_win):
    ext_rows = jnp.arange(tile_rows + 2 * half_win, dtype=jnp.int32) - half_win
    ext_cols = jnp.arange(tile_cols + 2 * half_win, dtype=jnp.int32) - half_win
    query_rows = jnp.arange(tile_rows, dtype=jnp.int32)
    query_cols = jnp.arange(tile_cols, dtype=jnp.int32)
    row_delta = ext_rows[None, :] - query_rows[:, None]
    col_delta = ext_cols[None, :] - query_cols[:, None]
    global_rows = row_start + ext_rows
    global_cols = col_start + ext_cols
    row_valid = (
        (row_delta >= -half_win)
        & (row_delta < half_win)
        & ((global_rows >= 0) & (global_rows < frame_rows))[None, :]
    )
    col_valid = (
        (col_delta >= -half_win)
        & (col_delta < half_win)
        & ((global_cols >= 0) & (global_cols < frame_cols))[None, :]
    )
    allowed = row_valid[:, None, :, None] & col_valid[None, :, None, :]
    return allowed.reshape(
        tile_rows * tile_cols, (tile_rows + 2 * half_win) * (tile_cols + 2 * half_win)
    )


def attend(query_rows, keys_flat, values_flat, allowed, heads, head_dim):
    score_scale = head_dim ** (-0.5)

    def one_head(head_index):
        scores = (
            jnp.einsum("qd,kd->qk", query_rows, keys_flat, preferred_element_type=jnp.float32)
            * score_scale
        )
        scores = jnp.where(allowed, scores, -1e30)
        row_top = jnp.max(scores, axis=1, keepdims=True)
        weights_f = jnp.exp(scores - row_top)
        denominator = jnp.sum(weights_f, axis=1, keepdims=True)
        numerator = jnp.dot(
            weights_f.astype(jnp.bfloat16), values_flat, preferred_element_type=jnp.float32
        )
        return numerator / denominator

    outputs = lax.map(one_head, jnp.arange(heads, dtype=jnp.int32))
    return outputs.transpose(1, 0, 2).reshape(query_rows.shape[0], heads * head_dim)


def local_conv(padded, conv_weight, conv_bias, tile_rows, tile_cols):
    enhanced = jnp.zeros((tile_rows, tile_cols, padded.shape[2]), jnp.float32) + conv_bias
    for row_shift in range(3):
        for col_shift in range(3):
            enhanced = (
                enhanced
                + padded[
                    row_shift : row_shift + tile_rows, col_shift : col_shift + tile_cols
                ].astype(jnp.float32)
                * conv_weight[row_shift, col_shift]
            )
    return enhanced


def cycle_conv(values_new, conv_weight, conv_bias):
    tile_rows, tile_cols, _ = values_new.shape
    padded = with_halo(values_new, (("ht", 0), ("wt", 1)), 1)
    return local_conv(padded, conv_weight, conv_bias, tile_rows, tile_cols)


def shards(queries, keys_new, values_new, keys_cache, values_cache, conv_weight, conv_bias):
    tile_rows, tile_cols, channels = queries.shape
    frames = keys_cache.shape[0] + 1
    half_win = WIN // 2
    stacked = jnp.concatenate([keys_cache, keys_new[None], values_cache, values_new[None]], axis=0)
    row_start = lax.axis_index("ht") * tile_rows
    frame_rows = tile_rows * lax.axis_size("ht")
    frame_cols = tile_cols * lax.axis_size("wt")
    heads = channels // HD
    copies = lax.axis_size("wt") // heads
    bundle = jnp.concatenate([stacked, queries[None]], axis=0)
    members = bundle.shape[0]
    spread = bundle.reshape(members, tile_rows, tile_cols, 1, heads, HD)
    spread = jnp.broadcast_to(spread, (members, tile_rows, tile_cols, copies, heads, HD))
    spread = spread.reshape(members, tile_rows, tile_cols, copies * heads, HD)
    strips = lax.all_to_all(spread, "wt", split_axis=3, concat_axis=2, tiled=True)
    strips = strips.reshape(members, tile_rows, frame_cols, HD)
    device_index = lax.axis_index("wt")
    my_group = device_index // heads
    block_width = tile_cols * heads
    block_start = my_group * block_width
    padded_cols = jnp.pad(strips, ((0, 0), (0, 0), (half_win, half_win), (0, 0)))
    window = lax.dynamic_slice_in_dim(padded_cols, block_start, block_width + 2 * half_win, 2)
    query_part = window[2 * frames, :, half_win : half_win + block_width]
    region = with_halo(window[: 2 * frames], (("ht", 1),), half_win)

    def one_block(step):
        offset = step * tile_cols
        query_block = lax.dynamic_slice_in_dim(query_part, offset, tile_cols, 1).reshape(
            tile_rows * tile_cols, HD
        )
        sub = lax.dynamic_slice_in_dim(region, offset, tile_cols + 2 * half_win, 2)
        keys_flat = sub[:frames].reshape(-1, HD)
        values_flat = sub[frames:].reshape(-1, HD)
        allowed = window_allowed(
            row_start, block_start + offset, frame_rows, frame_cols, tile_rows, tile_cols, half_win
        )
        allowed = jnp.tile(allowed, (1, frames))
        result = attend(query_block, keys_flat, values_flat, allowed, 1, HD)
        return result.reshape(tile_rows, tile_cols, HD)

    blocks = lax.map(one_block, jnp.arange(heads, dtype=jnp.int32))
    payload = blocks.transpose(1, 0, 2, 3)
    payload = jnp.broadcast_to(payload[:, None], (tile_rows, copies, heads, tile_cols, HD))
    payload = payload.reshape(tile_rows, copies * heads, tile_cols, HD)
    returned = lax.all_to_all(
        payload.astype(jnp.bfloat16), "wt", split_axis=1, concat_axis=1, tiled=True
    ).astype(payload.dtype)
    own = lax.dynamic_slice_in_dim(returned, my_group * heads, heads, 1)
    combined = own.transpose(0, 2, 1, 3).reshape(tile_rows, tile_cols, channels)
    combined = combined + cycle_conv(values_new, conv_weight, conv_bias)
    return combined.astype(jnp.bfloat16)


LOG2E = 1.4426950408889634
NEG = -1e30
VMEM = pl.BlockSpec(memory_space=pltpu.VMEM)
SMEM = pl.BlockSpec(memory_space=pltpu.SMEM)
LIMIT = pltpu.CompilerParams(vmem_limit_bytes=8 * 1024 * 1024)
SMALL = pltpu.CompilerParams(vmem_limit_bytes=4 * 1024 * 1024)


class Window:
    def __init__(self, grid, tile, info_ref, current_ref, sides):
        self.grid_rows, self.grid_cols = grid
        self.tile_rows, self.tile_cols = tile
        self.size = self.tile_rows * self.tile_cols
        self.info, self.current, self.sides = info_ref, current_ref, sides
        self.scale = HD ** (-0.5) * LOG2E
        self.bias_left = jnp.where(info_ref[0] > 0, 0.0, NEG).astype(jnp.float32)
        self.bias_right = jnp.where(info_ref[1] > 0, 0.0, NEG).astype(jnp.float32)
        query = lax.broadcasted_iota(jnp.int32, (self.size, self.size), 0)
        key = lax.broadcasted_iota(jnp.int32, (self.size, self.size), 1)
        self.upper = key // self.tile_cols >= query // self.tile_cols
        self.left = key % self.tile_cols >= query % self.tile_cols
        self.upper_one = self.upper.astype(jnp.float32).astype(jnp.bfloat16)
        self.left_one = self.left.astype(jnp.float32).astype(jnp.bfloat16)

    def slot(self, row, col):
        return self.info[2 + row * self.grid_cols + col]

    def side(self, col):
        return 1 if col < 0 else (2 if col >= self.grid_cols else 0)

    def tile(self, frame, part, row, col):
        ref, base = self.sides[frame][self.side(col)]
        return ref[self.slot(row, col % self.grid_cols), base + part].reshape(self.size, HD)

    def steps(self, col, inner):
        near = [step for step in (-1, 0, 1) if 0 <= col + step < self.grid_cols]
        return near if inner else [step for step in (-1, 0, 1, 2) if step not in near]

    def attend(self, row, col, wanted, before):
        query = self.current[self.slot(row, col), 2].reshape(self.size, HD)
        rows = [r for r in (row - 1, row, row + 1) if 0 <= r < self.grid_rows]
        needed = []
        for frame, step in wanted:
            for key_col in (col - 2, col + 2) if step == 2 else (col + step,):
                needed += [(frame, r, key_col) for r in rows]
        keys = jnp.concatenate([self.tile(frame, 0, r, c) for frame, r, c in needed], axis=0)
        raw = lax.dot_general(query, keys, (((1,), (1,)), ((), ())), preferred_element_type=jnp.float32)
        scores = {}
        for i, (frame, r, c) in enumerate(needed):
            score = raw[:, i * self.size : (i + 1) * self.size]
            if self.side(c) == 1:
                score = score + self.bias_left
            elif self.side(c) == 2:
                score = score + self.bias_right
            scores[frame, r, c] = score
        up, down = row > 0, row + 1 < self.grid_rows

        def level(frame, c):
            return scores[frame, row, c]

        def beside(frame, c):
            above = scores[frame, row - 1, c] if up else NEG
            return jnp.where(self.upper, above, scores[frame, row + 1, c] if down else NEG)

        blocks = []
        for frame, step in wanted:
            for off_row, make in ((False, level), (True, beside)):
                if off_row and not (up or down):
                    continue
                if step == 2:
                    block = jnp.where(self.left, make(frame, col - 2), make(frame, col + 2))
                else:
                    block = make(frame, col + step)
                blocks.append((frame, off_row, step, block))
        top = blocks[0][3]
        for entry in blocks[1:]:
            top = jnp.maximum(top, entry[3])
        top = jnp.max(top, axis=1, keepdims=True)
        if before is not None:
            top = jnp.maximum(top, before[0])
        parts = []
        for frame, off_row, step, block in blocks:
            weights = jnp.exp2((block - top) * self.scale).astype(jnp.bfloat16)
            if off_row and up and down:
                by_row = [(row - 1, weights * self.upper_one), (row + 1, weights * (1 - self.upper_one))]
            elif off_row:
                by_row = [(row + 1 if down else row - 1, weights)]
            else:
                by_row = [(row, weights)]
            for r, part in by_row:
                if step == 2:
                    parts.append((frame, r, col - 2, part * self.left_one))
                    parts.append((frame, r, col + 2, part * (1 - self.left_one)))
                else:
                    parts.append((frame, r, col + step, part))
        values = jnp.concatenate([self.tile(frame, 1, r, c) for frame, r, c, _ in parts], axis=0)
        values = jnp.concatenate([values, jnp.ones_like(values)], axis=1)
        weights = jnp.concatenate([part for _, _, _, part in parts], axis=1)
        total = jnp.dot(weights, values, preferred_element_type=jnp.float32)
        if before is not None:
            total = total + before[1] * jnp.exp2((before[0] - top) * self.scale)
        return top, total

    def enhanced(self, row, col, weight_ref, bias_ref):
        shape = (self.tile_cols, HD)
        sub = lax.broadcasted_iota(jnp.int32, shape, 0)
        taps = [[weight_ref[a, pl.ds(b, 1), :] for b in range(3)] for a in range(3)]
        last = self.tile_cols - 1
        lines = []
        for key_row in range(row * self.tile_rows - 1, (row + 1) * self.tile_rows + 1):
            tile_row, line = key_row // self.tile_rows, key_row % self.tile_rows
            if tile_row < 0 or tile_row >= self.grid_rows:
                lines.append(None)
                continue

            def values(c):
                ref, base = self.sides[1][self.side(c)]
                return ref[self.slot(tile_row, c % self.grid_cols), base + 1, line].astype(jnp.float32)

            here, before, after = values(col), values(col - 1), values(col + 1)
            low = jnp.where(sub == 0, pltpu.roll(before, 1, 0), pltpu.roll(here, 1, 0))
            high = jnp.where(sub == last, pltpu.roll(after, last, 0), pltpu.roll(here, last, 0))
            lines.append((low, here, high))
        sums = []
        for line in range(self.tile_rows):
            total = jnp.broadcast_to(bias_ref[...], shape)
            for a in range(3):
                if lines[line + a] is not None:
                    for b in range(3):
                        total = total + lines[line + a][b] * taps[a][b]
            sums.append(total)
        return jnp.stack(sums, axis=0)


def running(top_ref, sum_ref, index):
    return top_ref[index][:, :1], sum_ref[index]


def own_kernel(grid, tile, info_ref, current_ref, cached_ref, sum_ref, top_ref):
    window = Window(grid, tile, info_ref, current_ref, [[(cached_ref, 0)], [(current_ref, 0)]])
    for row in range(grid[0]):
        for col in range(grid[1]):
            wanted = [(frame, step) for frame in (0, 1) for step in window.steps(col, True)]
            top, total = window.attend(row, col, wanted, None)
            sum_ref[row * grid[1] + col] = total
            top_ref[row * grid[1] + col] = jnp.broadcast_to(top, (window.size, HD))


def cached_kernel(grid, tile, info_ref, current_ref, left_ref, right_ref, sum_in, top_in, sum_ref, top_ref):
    window = Window(grid, tile, info_ref, current_ref, [[None, (left_ref, 0), (right_ref, 0)]])
    for row in range(grid[0]):
        for col in range(grid[1]):
            index = row * grid[1] + col
            wanted = [(0, step) for step in window.steps(col, False)]
            top, total = window.attend(row, col, wanted, running(top_in, sum_in, index))
            sum_ref[index] = total
            top_ref[index] = jnp.broadcast_to(top, (window.size, HD))


def last_kernel(
    grid, tile, info_ref, weight_ref, bias_ref, current_ref, halo_ref, sum_in, top_in, same_ref, beside_ref
):
    window = Window(grid, tile, info_ref, current_ref, [None, [(current_ref, 0), (halo_ref, 0), (halo_ref, 2)]])
    count = grid[0] * grid[1]
    for row in range(grid[0]):
        for col in range(grid[1]):
            index = row * grid[1] + col
            wanted = [(1, step) for step in window.steps(col, False)]
            _, total = window.attend(row, col, wanted, running(top_in, sum_in, index))
            attended = (total[:, :HD] / total[:, HD:]).reshape(tile + (HD,))
            out = (attended + window.enhanced(row, col, weight_ref, bias_ref)).astype(jnp.bfloat16)
            place = info_ref[2 + index]

            @pl.when(place < count // 2)
            def _():
                same_ref[place] = out

            @pl.when(place >= count // 2)
            def _():
                beside_ref[place - count // 2] = out


def lanes(head):
    return pl.ds(pl.multiple_of(head * HD, HD), HD)


def pack_kernel(flips, side, members, me_ref, *refs):
    buffers = refs[len(refs) - len(flips) :]
    for buffer, flip in zip(buffers, flips):
        for other in range(2):
            head = me_ref[0] ^ (flip ^ (side if other else 0))
            for member, (source, lead) in enumerate(members):
                buffer[other, member] = refs[source][lead, :, :, lanes(head)]


def unpack_kernel(flips, side, me_ref, same_ref, beside_ref, *refs):
    out_ref = refs[-1]
    out_ref[:, :, lanes(me_ref[0])] = same_ref[0]
    out_ref[:, :, lanes(me_ref[0] ^ side)] = beside_ref[0]
    for i, flip in enumerate(flips[1:]):
        out_ref[:, :, lanes(me_ref[0] ^ flip)] = refs[i][0]
        out_ref[:, :, lanes(me_ref[0] ^ (flip ^ side))] = refs[i][1]


def head_step(shape, queries, keys_new, values_new, keys_cache, values_cache, conv_weight, conv_bias):
    group_rows, group_cols, far = shape
    tile_rows, tile_cols, channels = queries.shape
    heads = channels // HD
    grid, tile = (group_rows, group_cols), (tile_rows, tile_cols)
    axes = ("ht", "near")
    block = (tile_rows, tile_cols, HD)
    side = group_cols
    flips = [flip for flip in range(heads) if not flip & side]
    me = lax.axis_index("ht") * group_cols + lax.axis_index("near")
    me = me.astype(jnp.int32)
    me_ref = me.reshape(1)

    def swap(x, flip):
        return lax.ppermute(x, axes, [(s, s ^ flip) for s in range(heads)])

    def pack(*arrays):
        members = [(i, lead) for i, array in enumerate(arrays) for lead in range(array.shape[0])]
        return pl.pallas_call(
            functools.partial(pack_kernel, flips, side, members),
            out_shape=[jax.ShapeDtypeStruct((2, len(members)) + block, jnp.bfloat16)] * len(flips),
            in_specs=[SMEM] + [VMEM] * len(arrays),
            out_specs=[VMEM] * len(flips),
            compiler_params=SMALL,
            cost_estimate=pl.CostEstimate(flops=0, bytes_accessed=len(members) << 20, transcendentals=0),
        )(me_ref, *arrays)

    def gather(buffers):
        got = [buffers[0]] + [swap(b, flip) for b, flip in zip(buffers[1:], flips[1:])]
        forward = jnp.stack([b[1] for b in got])
        beside = swap(forward, side)
        return jnp.concatenate([jnp.stack([b[0] for b in got]), beside], axis=0)

    up = [(i, i + 1) for i in range(far - 1)]
    down = [(i + 1, i) for i in range(far - 1)]

    def halo(x):
        return lax.ppermute(x, "far", up), lax.ppermute(x, "far", down)

    pair = jnp.stack([keys_new, values_new])
    new_left, new_right = halo(pair)
    packed_cached = pack(keys_cache, values_cache)
    cached = gather(packed_cached)
    packed_current = pack(keys_new[None], values_new[None], queries[None])
    current = gather(packed_current)
    cached_left, cached_right = halo(cached)
    packed_beyond = pack(new_left, new_right)
    beyond = gather(packed_beyond)
    far_index = lax.axis_index("far")
    flip = me ^ jnp.arange(heads, dtype=jnp.int32)
    beside = (flip // side) % 2
    order = flip % side + flip // (2 * side) * side
    info = jnp.concatenate(
        [
            jnp.stack([far_index > 0, far_index < far - 1]).astype(jnp.int32),
            beside * len(flips) + order,
        ]
    )
    weight = lax.dynamic_slice_in_dim(conv_weight, me * HD, HD, 2)
    bias = lax.dynamic_slice_in_dim(conv_bias.reshape(1, channels), me * HD, HD, 1)
    size = tile_rows * tile_cols
    state = (
        jax.ShapeDtypeStruct((heads, size, 2 * HD), jnp.float32),
        jax.ShapeDtypeStruct((heads, size, HD), jnp.float32),
    )

    def attention(kernel, out_shape, *operands):
        return pl.pallas_call(
            functools.partial(kernel, grid, tile),
            out_shape=out_shape,
            in_specs=[SMEM] + [VMEM] * len(operands),
            out_specs=(VMEM, VMEM),
            compiler_params=LIMIT,
            cost_estimate=pl.CostEstimate(flops=2**31, bytes_accessed=2**22, transcendentals=2**20),
        )(info, *operands)

    sums, tops = attention(own_kernel, state, current, cached)
    sums, tops = attention(cached_kernel, state, current, cached_left, cached_right, sums, tops)
    half = jax.ShapeDtypeStruct((len(flips),) + block, jnp.bfloat16)
    same, other = attention(last_kernel, (half, half), weight, bias, current, beyond, sums, tops)
    received = swap(other, side)
    pairs = [jnp.stack([same[i], received[i]]) for i in range(1, len(flips))]
    got = [swap(pair, flip) for pair, flip in zip(pairs, flips[1:])]
    return pl.pallas_call(
        functools.partial(unpack_kernel, flips, side),
        out_shape=jax.ShapeDtypeStruct(queries.shape, jnp.bfloat16),
        in_specs=[SMEM] + [VMEM] * (len(flips) + 1),
        out_specs=VMEM,
        compiler_params=SMALL,
    )(me_ref, same, received, *got)


def grouping(mesh, heads):
    rows, cols = mesh.shape["ht"], mesh.shape["wt"]
    group_rows = rows
    group_cols = heads // group_rows if heads % group_rows == 0 else 0
    if group_cols != 2 or cols % group_cols:
        return None
    return group_rows, group_cols, cols // group_cols


def solution(mesh):
    def program(queries, *rest):
        heads = queries.shape[2] // HD
        shape = grouping(mesh, heads)
        if shape is None or queries.shape[0] != mesh.shape["ht"] * (WIN // 2) or queries.shape[1] != mesh.shape["wt"] * (WIN // 4):
            placed = (P("ht", "wt", None),) * 3 + (P(None, "ht", "wt", None),) * 2 + (P(), P())
            return jax.shard_map(
                shards, mesh=mesh, in_specs=placed, out_specs=P("ht", "wt", None), check_vma=False
            )(queries, *rest)
        devices = mesh.devices.reshape(shape[0], shape[2], shape[1])
        split = Mesh(devices, ("ht", "far", "near"))
        tile = P("ht", ("far", "near"), None)
        past = P(None, "ht", ("far", "near"), None)
        step = jax.shard_map(
            functools.partial(head_step, shape),
            mesh=split,
            in_specs=(tile, tile, tile, past, past, P(), P()),
            out_specs=tile,
            check_vma=False,
        )
        return step(queries, *rest)

    return program
```

```python
import functools

import jax
import jax.numpy as jnp
from jax import lax
from jax.experimental import pallas as pl
from jax.experimental.pallas import tpu as pltpu
from jax.sharding import Mesh, PartitionSpec as P


HD = 128
WIN = 32


def with_halo(block, sides, width):
    for axis, dim in sides:
        count = lax.axis_size(axis)
        forward = [(i, i + 1) for i in range(count - 1)]
        backward = [(target, source) for source, target in forward]
        low = lax.ppermute(
            lax.slice_in_dim(block, block.shape[dim] - width, None, axis=dim), axis, forward
        )
        high = lax.ppermute(lax.slice_in_dim(block, 0, width, axis=dim), axis, backward)
        block = jnp.concatenate([low, block, high], axis=dim)
    return block


def window_allowed(row_start, col_start, frame_rows, frame_cols, tile_rows, tile_cols, half_win):
    ext_rows = jnp.arange(tile_rows + 2 * half_win, dtype=jnp.int32) - half_win
    ext_cols = jnp.arange(tile_cols + 2 * half_win, dtype=jnp.int32) - half_win
    query_rows = jnp.arange(tile_rows, dtype=jnp.int32)
    query_cols = jnp.arange(tile_cols, dtype=jnp.int32)
    row_delta = ext_rows[None, :] - query_rows[:, None]
    col_delta = ext_cols[None, :] - query_cols[:, None]
    global_rows = row_start + ext_rows
    global_cols = col_start + ext_cols
    row_valid = (
        (row_delta >= -half_win)
        & (row_delta < half_win)
        & ((global_rows >= 0) & (global_rows < frame_rows))[None, :]
    )
    col_valid = (
        (col_delta >= -half_win)
        & (col_delta < half_win)
        & ((global_cols >= 0) & (global_cols < frame_cols))[None, :]
    )
    allowed = row_valid[:, None, :, None] & col_valid[None, :, None, :]
    return allowed.reshape(
        tile_rows * tile_cols, (tile_rows + 2 * half_win) * (tile_cols + 2 * half_win)
    )


def attend(query_rows, keys_flat, values_flat, allowed, heads, head_dim):
    score_scale = head_dim ** (-0.5)

    def one_head(head_index):
        scores = (
            jnp.einsum("qd,kd->qk", query_rows, keys_flat, preferred_element_type=jnp.float32)
            * score_scale
        )
        scores = jnp.where(allowed, scores, -1e30)
        row_top = jnp.max(scores, axis=1, keepdims=True)
        weights_f = jnp.exp(scores - row_top)
        denominator = jnp.sum(weights_f, axis=1, keepdims=True)
        numerator = jnp.dot(
            weights_f.astype(jnp.bfloat16), values_flat, preferred_element_type=jnp.float32
        )
        return numerator / denominator

    outputs = lax.map(one_head, jnp.arange(heads, dtype=jnp.int32))
    return outputs.transpose(1, 0, 2).reshape(query_rows.shape[0], heads * head_dim)


def local_conv(padded, conv_weight, conv_bias, tile_rows, tile_cols):
    enhanced = jnp.zeros((tile_rows, tile_cols, padded.shape[2]), jnp.float32) + conv_bias
    for row_shift in range(3):
        for col_shift in range(3):
            enhanced = (
                enhanced
                + padded[
                    row_shift : row_shift + tile_rows, col_shift : col_shift + tile_cols
                ].astype(jnp.float32)
                * conv_weight[row_shift, col_shift]
            )
    return enhanced


def cycle_conv(values_new, conv_weight, conv_bias):
    tile_rows, tile_cols, _ = values_new.shape
    padded = with_halo(values_new, (("ht", 0), ("wt", 1)), 1)
    return local_conv(padded, conv_weight, conv_bias, tile_rows, tile_cols)


def shards(queries, keys_new, values_new, keys_cache, values_cache, conv_weight, conv_bias):
    tile_rows, tile_cols, channels = queries.shape
    frames = keys_cache.shape[0] + 1
    half_win = WIN // 2
    stacked = jnp.concatenate([keys_cache, keys_new[None], values_cache, values_new[None]], axis=0)
    row_start = lax.axis_index("ht") * tile_rows
    frame_rows = tile_rows * lax.axis_size("ht")
    frame_cols = tile_cols * lax.axis_size("wt")
    heads = channels // HD
    copies = lax.axis_size("wt") // heads
    bundle = jnp.concatenate([stacked, queries[None]], axis=0)
    members = bundle.shape[0]
    spread = bundle.reshape(members, tile_rows, tile_cols, 1, heads, HD)
    spread = jnp.broadcast_to(spread, (members, tile_rows, tile_cols, copies, heads, HD))
    spread = spread.reshape(members, tile_rows, tile_cols, copies * heads, HD)
    strips = lax.all_to_all(spread, "wt", split_axis=3, concat_axis=2, tiled=True)
    strips = strips.reshape(members, tile_rows, frame_cols, HD)
    device_index = lax.axis_index("wt")
    my_group = device_index // heads
    block_width = tile_cols * heads
    block_start = my_group * block_width
    padded_cols = jnp.pad(strips, ((0, 0), (0, 0), (half_win, half_win), (0, 0)))
    window = lax.dynamic_slice_in_dim(padded_cols, block_start, block_width + 2 * half_win, 2)
    query_part = window[2 * frames, :, half_win : half_win + block_width]
    region = with_halo(window[: 2 * frames], (("ht", 1),), half_win)

    def one_block(step):
        offset = step * tile_cols
        query_block = lax.dynamic_slice_in_dim(query_part, offset, tile_cols, 1).reshape(
            tile_rows * tile_cols, HD
        )
        sub = lax.dynamic_slice_in_dim(region, offset, tile_cols + 2 * half_win, 2)
        keys_flat = sub[:frames].reshape(-1, HD)
        values_flat = sub[frames:].reshape(-1, HD)
        allowed = window_allowed(
            row_start, block_start + offset, frame_rows, frame_cols, tile_rows, tile_cols, half_win
        )
        allowed = jnp.tile(allowed, (1, frames))
        result = attend(query_block, keys_flat, values_flat, allowed, 1, HD)
        return result.reshape(tile_rows, tile_cols, HD)

    blocks = lax.map(one_block, jnp.arange(heads, dtype=jnp.int32))
    payload = blocks.transpose(1, 0, 2, 3)
    payload = jnp.broadcast_to(payload[:, None], (tile_rows, copies, heads, tile_cols, HD))
    payload = payload.reshape(tile_rows, copies * heads, tile_cols, HD)
    returned = lax.all_to_all(
        payload.astype(jnp.bfloat16), "wt", split_axis=1, concat_axis=1, tiled=True
    ).astype(payload.dtype)
    own = lax.dynamic_slice_in_dim(returned, my_group * heads, heads, 1)
    combined = own.transpose(0, 2, 1, 3).reshape(tile_rows, tile_cols, channels)
    combined = combined + cycle_conv(values_new, conv_weight, conv_bias)
    return combined.astype(jnp.bfloat16)


LOG2E = 1.4426950408889634
NEG = -1e30
VMEM = pl.BlockSpec(memory_space=pltpu.VMEM)
SMEM = pl.BlockSpec(memory_space=pltpu.SMEM)
LIMIT = pltpu.CompilerParams(vmem_limit_bytes=8 * 1024 * 1024)
SMALL = pltpu.CompilerParams(vmem_limit_bytes=4 * 1024 * 1024)


class Window:
    def __init__(self, grid, tile, info_ref, query_ref, pairs_ref):
        self.grid_rows, self.grid_cols = grid
        self.tile_rows, self.tile_cols = tile
        self.size = self.tile_rows * self.tile_cols
        self.info, self.query, self.pairs = info_ref, query_ref, pairs_ref
        self.scale = HD ** (-0.5) * LOG2E
        query = lax.broadcasted_iota(jnp.int32, (self.size, self.size), 0)
        key = lax.broadcasted_iota(jnp.int32, (self.size, self.size), 1)
        self.upper = key // self.tile_cols >= query // self.tile_cols
        self.left = key % self.tile_cols >= query % self.tile_cols
        self.upper_one = self.upper.astype(jnp.float32).astype(jnp.bfloat16)

    def slot(self, row, col):
        return self.info[2 + row * self.grid_cols + col % self.grid_cols]

    def tile(self, member, row, col):
        return self.pairs[self.slot(row, col), member].reshape(self.size, HD)

    def attend(self, row, col):
        query = self.query[self.slot(row, col), pl.ds(0, self.tile_rows)].reshape(self.size, HD)
        frames = range(self.pairs.shape[1] // 2)
        cols = [c for c in range(self.grid_cols) if abs(c - col) <= 2]
        up, down = row > 0, row + 1 < self.grid_rows
        rows = [r for r in (row - 1, row, row + 1) if 0 <= r < self.grid_rows]
        needed = [(f, r, c) for f in frames for c in cols for r in rows]
        keys = jnp.concatenate([self.tile(2 * f, r, c) for f, r, c in needed], axis=0)
        raw = lax.dot_general(query, keys, (((1,), (1,)), ((), ())), preferred_element_type=jnp.float32)
        scores = {key: raw[:, i * self.size : (i + 1) * self.size] for i, key in enumerate(needed)}
        blocks = []
        for f in frames:
            for c in cols:
                found = [(False, scores[f, row, c])]
                if up or down:
                    above = scores[f, row - 1, c] if up else NEG
                    found.append((True, jnp.where(self.upper, above, scores[f, row + 1, c] if down else NEG)))
                for off_row, block in found:
                    if c - col == 2:
                        block = jnp.where(self.left, NEG, block)
                    elif c - col == -2:
                        block = jnp.where(self.left, block, NEG)
                    blocks.append((f, off_row, c, block))
        top = blocks[0][3]
        for entry in blocks[1:]:
            top = jnp.maximum(top, entry[3])
        top = jnp.max(top, axis=1, keepdims=True)
        parts = []
        for f, off_row, c, block in blocks:
            weights = jnp.exp2((block - top) * self.scale).astype(jnp.bfloat16)
            if off_row and up and down:
                parts.append((f, row - 1, c, weights * self.upper_one))
                parts.append((f, row + 1, c, weights * (1 - self.upper_one)))
            elif off_row:
                parts.append((f, row + 1 if down else row - 1, c, weights))
            else:
                parts.append((f, row, c, weights))
        values = jnp.concatenate([self.tile(2 * f + 1, r, c) for f, r, c, _ in parts], axis=0)
        values = jnp.concatenate([values, jnp.ones_like(values)], axis=1)
        weights = jnp.concatenate([part for _, _, _, part in parts], axis=1)
        total = jnp.dot(weights, values, preferred_element_type=jnp.float32)
        return total[:, :HD] / total[:, HD:], top * self.scale + jnp.log2(total[:, HD:])

    def enhanced(self, row, col, weight_ref, bias_ref, before_ref, after_ref):
        shape = (self.tile_cols, HD)
        sub = lax.broadcasted_iota(jnp.int32, shape, 0)
        taps = [[weight_ref[a, pl.ds(b, 1), :] for b in range(3)] for a in range(3)]
        last = self.tile_cols - 1
        member = self.pairs.shape[1] - 1
        lines = []
        for key_row in range(row * self.tile_rows - 1, (row + 1) * self.tile_rows + 1):
            tile_row, line = key_row // self.tile_rows, key_row % self.tile_rows
            if tile_row < 0 or tile_row >= self.grid_rows:
                lines.append(None)
                continue

            def values(c):
                return self.pairs[self.slot(tile_row, c), member, line].astype(jnp.float32)

            def edge(ref, c):
                packed = ref[self.slot(tile_row, c), self.tile_rows + line // self.tile_cols].astype(jnp.float32)
                return jnp.broadcast_to(packed[line % self.tile_cols : line % self.tile_cols + 1], shape)

            here = values(col)
            before = pltpu.roll(values(col - 1), 1, 0) if col > 0 else edge(before_ref, self.grid_cols - 1)
            after = pltpu.roll(values(col + 1), last, 0) if col + 1 < self.grid_cols else edge(after_ref, 0)
            low = jnp.where(sub == 0, before, pltpu.roll(here, 1, 0))
            high = jnp.where(sub == last, after, pltpu.roll(here, last, 0))
            lines.append((low, here, high))
        sums = []
        for line in range(self.tile_rows):
            total = jnp.broadcast_to(bias_ref[...], shape)
            for a in range(3):
                if lines[line + a] is not None:
                    for b in range(3):
                        total = total + lines[line + a][b] * taps[a][b]
            sums.append(total)
        return jnp.stack(sums, axis=0)


def visit_kernel(grid, tile, first_col, info_ref, query_ref, pairs_ref, out_ref):
    window = Window(grid, tile, info_ref, query_ref, pairs_ref)
    size, count = window.size, grid[0] * grid[1]
    lane = lax.broadcasted_iota(jnp.int32, (size, HD), 1)
    packed = jnp.zeros((size, HD), jnp.float32)
    for row in range(grid[0]):
        for col in range(grid[1]):
            index = row * grid[1] + col
            part, level = window.attend(row, first_col + col)
            out_ref[window.slot(row, col)] = part.reshape(tile + (HD,)).astype(jnp.bfloat16)
            high = level.astype(jnp.bfloat16).astype(jnp.float32)
            middle = (level - high).astype(jnp.bfloat16).astype(jnp.float32)
            for i, piece in enumerate((high, middle, level - high - middle)):
                packed = jnp.where(lane == i * count + index, piece, packed)
    out_ref[count] = packed.reshape(tile + (HD,)).astype(jnp.bfloat16)


def own_kernel(
    grid, tile, info_ref, weight_ref, bias_ref, query_ref, pairs_ref, before_ref, after_ref, part_ref, level_ref, conv_ref
):
    window = Window(grid, tile, info_ref, query_ref, pairs_ref)
    for row in range(grid[0]):
        for col in range(grid[1]):
            index = row * grid[1] + col
            part_ref[index], level_ref[index] = window.attend(row, col)
            conv = window.enhanced(row, col, weight_ref, bias_ref, before_ref, after_ref)
            conv_ref[index] = conv.reshape(window.size, HD)


def join_kernel(grid, tile, info_ref, part_ref, level_ref, conv_ref, left_ref, right_ref, same_ref, beside_ref):
    size, count = tile[0] * tile[1], grid[0] * grid[1]
    present = [info_ref[0] > 0, info_ref[1] > 0]
    visits = (left_ref, right_ref)
    packed = [ref[count].reshape(size, HD).astype(jnp.float32) for ref in visits]
    for index in range(count):
        place = info_ref[2 + index]
        parts, levels = [part_ref[index]], [level_ref[index]]
        for ref, there, pack in zip(visits, present, packed):
            parts.append(ref[place].reshape(size, HD).astype(jnp.float32))
            level = pack[:, index : index + 1]
            for i in (1, 2):
                level = level + pack[:, i * count + index : i * count + index + 1]
            levels.append(jnp.broadcast_to(jnp.where(there, level, NEG), (size, HD)))
        top = jnp.maximum(jnp.maximum(levels[0], levels[1]), levels[2])
        shares = [jnp.exp2(level - top) for level in levels]
        mixed = sum(share * part for share, part in zip(shares, parts)) / sum(shares)
        out = (mixed + conv_ref[index]).reshape(tile + (HD,)).astype(jnp.bfloat16)

        @pl.when(place < count // 2)
        def _():
            same_ref[place] = out

        @pl.when(place >= count // 2)
        def _():
            beside_ref[place - count // 2] = out


def lanes(head):
    return pl.ds(pl.multiple_of(head * HD, HD), HD)


def pack_kernel(flips, side, me_ref, *refs):
    sources, buffers = refs[: len(refs) - len(flips)], refs[len(refs) - len(flips) :]
    for buffer, flip in zip(buffers, flips):
        for other in range(2):
            head = me_ref[0] ^ (flip ^ (side if other else 0))
            for member, source in enumerate(sources):
                buffer[other, member] = source[:, :, lanes(head)]


def query_kernel(flips, side, me_ref, query_ref, values_ref, *buffers):
    tile_rows, tile_cols, _ = query_ref.shape
    sub = lax.broadcasted_iota(jnp.int32, (tile_cols, HD), 0)
    for buffer, flip in zip(buffers, flips):
        for other in range(2):
            head = me_ref[0] ^ (flip ^ (side if other else 0))
            buffer[other, pl.ds(0, tile_rows)] = query_ref[:, :, lanes(head)]
            for start in range(0, tile_rows, tile_cols):
                packed = jnp.zeros((tile_cols, HD), jnp.float32)
                for line in range(tile_cols):
                    values = values_ref[start + line, :, lanes(head)].astype(jnp.float32)
                    edge = jnp.where(me_ref[1] == 0, values[:1], values[tile_cols - 1 :])
                    packed = jnp.where(sub == line, edge, packed)
                buffer[other, tile_rows + start // tile_cols] = packed.astype(jnp.bfloat16)


def unpack_kernel(flips, side, me_ref, same_ref, beside_ref, *refs):
    out_ref = refs[-1]
    out_ref[:, :, lanes(me_ref[0])] = same_ref[0]
    out_ref[:, :, lanes(me_ref[0] ^ side)] = beside_ref[0]
    for i, flip in enumerate(flips[1:]):
        out_ref[:, :, lanes(me_ref[0] ^ flip)] = refs[i][0]
        out_ref[:, :, lanes(me_ref[0] ^ (flip ^ side))] = refs[i][1]


def head_step(shape, queries, keys_new, values_new, keys_cache, values_cache, conv_weight, conv_bias):
    group_rows, group_cols, far = shape
    tile_rows, tile_cols, channels = queries.shape
    heads = channels // HD
    grid, tile = (group_rows, group_cols), (tile_rows, tile_cols)
    size = tile_rows * tile_cols
    axes = ("ht", "near")
    block = (tile_rows, tile_cols, HD)
    side = group_cols
    flips = [flip for flip in range(heads) if not flip & side]
    near = lax.axis_index("near").astype(jnp.int32)
    me = lax.axis_index("ht").astype(jnp.int32) * group_cols + near
    me_ref = jnp.stack([me, near])

    def swap(x, flip):
        return lax.ppermute(x, axes, [(s, s ^ flip) for s in range(heads)])

    def call(kernel, out_shape, params, cost, *operands):
        return pl.pallas_call(
            kernel,
            out_shape=out_shape,
            in_specs=[SMEM] + [VMEM] * (len(operands) - 1),
            out_specs=jax.tree.map(lambda _: VMEM, out_shape),
            compiler_params=params,
            cost_estimate=pl.CostEstimate(flops=cost << 30, bytes_accessed=1 << 20, transcendentals=0),
        )(*operands)

    def gather(buffers):
        got = [buffers[0]] + [swap(b, flip) for b, flip in zip(buffers[1:], flips[1:])]
        forward = jnp.stack([b[1] for b in got])
        beside = swap(forward, side)
        return jnp.concatenate([jnp.stack([b[0] for b in got]), beside], axis=0)

    up = [(i, i + 1) for i in range(far - 1)]
    down = [(i + 1, i) for i in range(far - 1)]
    edges = -(-tile_rows // tile_cols)
    buffer = jax.ShapeDtypeStruct((2, tile_rows + edges, tile_cols, HD), jnp.bfloat16)
    packed_query = call(
        functools.partial(query_kernel, flips, side), [buffer] * len(flips), SMALL, 0, me_ref, queries, values_new
    )
    query = gather(packed_query)
    sources = (keys_cache[0], values_cache[0], keys_new, values_new)
    buffer = jax.ShapeDtypeStruct((2, len(sources)) + block, jnp.bfloat16)
    packed_pairs = call(functools.partial(pack_kernel, flips, side), [buffer] * len(flips), SMALL, 0, me_ref, *sources)
    pairs = gather(packed_pairs)
    query_left = lax.ppermute(query, "far", up)
    query_right = lax.ppermute(query, "far", down)
    far_index = lax.axis_index("far")
    flip = me ^ jnp.arange(heads, dtype=jnp.int32)
    beside = (flip // side) % 2
    order = flip % side + flip // (2 * side) * side
    info = jnp.concatenate(
        [
            jnp.stack([far_index > 0, far_index < far - 1]).astype(jnp.int32),
            beside * len(flips) + order,
        ]
    )
    weight = lax.dynamic_slice_in_dim(conv_weight, me * HD, HD, 2)
    bias = lax.dynamic_slice_in_dim(conv_bias.reshape(1, channels), me * HD, HD, 1)

    def visit(queries, first_col):
        kernel = functools.partial(visit_kernel, grid, tile, first_col)
        return call(kernel, jax.ShapeDtypeStruct((heads + 1,) + block, jnp.bfloat16), LIMIT, 4, info, queries, pairs)

    left_part = visit(query_left, -group_cols)
    from_right = lax.ppermute(left_part, "far", down)
    right_part = visit(query_right, group_cols)
    from_left = lax.ppermute(right_part, "far", up)
    part = jax.ShapeDtypeStruct((heads, size, HD), jnp.float32)
    kernel = functools.partial(own_kernel, grid, tile)
    own = call(kernel, [part] * 3, LIMIT, 4, info, weight, bias, query, pairs, query_left, query_right)
    half = jax.ShapeDtypeStruct((len(flips),) + block, jnp.bfloat16)
    kernel = functools.partial(join_kernel, grid, tile)
    same, other = call(kernel, [half, half], LIMIT, 1, info, *own, from_left, from_right)
    received = swap(other, side)
    got = [swap(jnp.stack([same[i], received[i]]), flips[i]) for i in range(1, len(flips))]
    return call(
        functools.partial(unpack_kernel, flips, side),
        jax.ShapeDtypeStruct(queries.shape, jnp.bfloat16),
        SMALL,
        0,
        me_ref,
        same,
        received,
        *got,
    )


def grouping(mesh, heads):
    rows, cols = mesh.shape["ht"], mesh.shape["wt"]
    group_rows = rows
    group_cols = heads // group_rows if heads % group_rows == 0 else 0
    if group_cols != 2 or cols % group_cols:
        return None
    return group_rows, group_cols, cols // group_cols


def solution(mesh):
    def program(queries, *rest):
        heads = queries.shape[2] // HD
        shape = grouping(mesh, heads)
        if shape is None or queries.shape[0] != mesh.shape["ht"] * (WIN // 2) or queries.shape[1] != mesh.shape["wt"] * (WIN // 4):
            placed = (P("ht", "wt", None),) * 3 + (P(None, "ht", "wt", None),) * 2 + (P(), P())
            return jax.shard_map(
                shards, mesh=mesh, in_specs=placed, out_specs=P("ht", "wt", None), check_vma=False
            )(queries, *rest)
        devices = mesh.devices.reshape(shape[0], shape[2], shape[1])
        split = Mesh(devices, ("ht", "far", "near"))
        tile = P("ht", ("far", "near"), None)
        past = P(None, "ht", ("far", "near"), None)
        step = jax.shard_map(
            functools.partial(head_step, shape),
            mesh=split,
            in_specs=(tile, tile, tile, past, past, P(), P()),
            out_specs=tile,
            check_vma=False,
        )
        return step(queries, *rest)

    return program
```

```python
import functools

import jax
import jax.numpy as jnp
from jax import lax
from jax.experimental import pallas as pl
from jax.experimental.pallas import tpu as pltpu
from jax.sharding import Mesh, PartitionSpec as P


HD = 128
WIN = 32


def with_halo(block, sides, width):
    for axis, dim in sides:
        count = lax.axis_size(axis)
        forward = [(i, i + 1) for i in range(count - 1)]
        backward = [(target, source) for source, target in forward]
        low = lax.ppermute(
            lax.slice_in_dim(block, block.shape[dim] - width, None, axis=dim), axis, forward
        )
        high = lax.ppermute(lax.slice_in_dim(block, 0, width, axis=dim), axis, backward)
        block = jnp.concatenate([low, block, high], axis=dim)
    return block


def window_allowed(row_start, col_start, frame_rows, frame_cols, tile_rows, tile_cols, half_win):
    ext_rows = jnp.arange(tile_rows + 2 * half_win, dtype=jnp.int32) - half_win
    ext_cols = jnp.arange(tile_cols + 2 * half_win, dtype=jnp.int32) - half_win
    query_rows = jnp.arange(tile_rows, dtype=jnp.int32)
    query_cols = jnp.arange(tile_cols, dtype=jnp.int32)
    row_delta = ext_rows[None, :] - query_rows[:, None]
    col_delta = ext_cols[None, :] - query_cols[:, None]
    global_rows = row_start + ext_rows
    global_cols = col_start + ext_cols
    row_valid = (
        (row_delta >= -half_win)
        & (row_delta < half_win)
        & ((global_rows >= 0) & (global_rows < frame_rows))[None, :]
    )
    col_valid = (
        (col_delta >= -half_win)
        & (col_delta < half_win)
        & ((global_cols >= 0) & (global_cols < frame_cols))[None, :]
    )
    allowed = row_valid[:, None, :, None] & col_valid[None, :, None, :]
    return allowed.reshape(
        tile_rows * tile_cols, (tile_rows + 2 * half_win) * (tile_cols + 2 * half_win)
    )


def attend(query_rows, keys_flat, values_flat, allowed, heads, head_dim):
    score_scale = head_dim ** (-0.5)

    def one_head(head_index):
        scores = (
            jnp.einsum("qd,kd->qk", query_rows, keys_flat, preferred_element_type=jnp.float32)
            * score_scale
        )
        scores = jnp.where(allowed, scores, -1e30)
        row_top = jnp.max(scores, axis=1, keepdims=True)
        weights_f = jnp.exp(scores - row_top)
        denominator = jnp.sum(weights_f, axis=1, keepdims=True)
        numerator = jnp.dot(
            weights_f.astype(jnp.bfloat16), values_flat, preferred_element_type=jnp.float32
        )
        return numerator / denominator

    outputs = lax.map(one_head, jnp.arange(heads, dtype=jnp.int32))
    return outputs.transpose(1, 0, 2).reshape(query_rows.shape[0], heads * head_dim)


def local_conv(padded, conv_weight, conv_bias, tile_rows, tile_cols):
    enhanced = jnp.zeros((tile_rows, tile_cols, padded.shape[2]), jnp.float32) + conv_bias
    for row_shift in range(3):
        for col_shift in range(3):
            enhanced = (
                enhanced
                + padded[
                    row_shift : row_shift + tile_rows, col_shift : col_shift + tile_cols
                ].astype(jnp.float32)
                * conv_weight[row_shift, col_shift]
            )
    return enhanced


def cycle_conv(values_new, conv_weight, conv_bias):
    tile_rows, tile_cols, _ = values_new.shape
    padded = with_halo(values_new, (("ht", 0), ("wt", 1)), 1)
    return local_conv(padded, conv_weight, conv_bias, tile_rows, tile_cols)


def shards(queries, keys_new, values_new, keys_cache, values_cache, conv_weight, conv_bias):
    tile_rows, tile_cols, channels = queries.shape
    frames = keys_cache.shape[0] + 1
    half_win = WIN // 2
    stacked = jnp.concatenate([keys_cache, keys_new[None], values_cache, values_new[None]], axis=0)
    row_start = lax.axis_index("ht") * tile_rows
    frame_rows = tile_rows * lax.axis_size("ht")
    frame_cols = tile_cols * lax.axis_size("wt")
    heads = channels // HD
    copies = lax.axis_size("wt") // heads
    bundle = jnp.concatenate([stacked, queries[None]], axis=0)
    members = bundle.shape[0]
    spread = bundle.reshape(members, tile_rows, tile_cols, 1, heads, HD)
    spread = jnp.broadcast_to(spread, (members, tile_rows, tile_cols, copies, heads, HD))
    spread = spread.reshape(members, tile_rows, tile_cols, copies * heads, HD)
    strips = lax.all_to_all(spread, "wt", split_axis=3, concat_axis=2, tiled=True)
    strips = strips.reshape(members, tile_rows, frame_cols, HD)
    device_index = lax.axis_index("wt")
    my_group = device_index // heads
    block_width = tile_cols * heads
    block_start = my_group * block_width
    padded_cols = jnp.pad(strips, ((0, 0), (0, 0), (half_win, half_win), (0, 0)))
    window = lax.dynamic_slice_in_dim(padded_cols, block_start, block_width + 2 * half_win, 2)
    query_part = window[2 * frames, :, half_win : half_win + block_width]
    region = with_halo(window[: 2 * frames], (("ht", 1),), half_win)

    def one_block(step):
        offset = step * tile_cols
        query_block = lax.dynamic_slice_in_dim(query_part, offset, tile_cols, 1).reshape(
            tile_rows * tile_cols, HD
        )
        sub = lax.dynamic_slice_in_dim(region, offset, tile_cols + 2 * half_win, 2)
        keys_flat = sub[:frames].reshape(-1, HD)
        values_flat = sub[frames:].reshape(-1, HD)
        allowed = window_allowed(
            row_start, block_start + offset, frame_rows, frame_cols, tile_rows, tile_cols, half_win
        )
        allowed = jnp.tile(allowed, (1, frames))
        result = attend(query_block, keys_flat, values_flat, allowed, 1, HD)
        return result.reshape(tile_rows, tile_cols, HD)

    blocks = lax.map(one_block, jnp.arange(heads, dtype=jnp.int32))
    payload = blocks.transpose(1, 0, 2, 3)
    payload = jnp.broadcast_to(payload[:, None], (tile_rows, copies, heads, tile_cols, HD))
    payload = payload.reshape(tile_rows, copies * heads, tile_cols, HD)
    returned = lax.all_to_all(
        payload.astype(jnp.bfloat16), "wt", split_axis=1, concat_axis=1, tiled=True
    ).astype(payload.dtype)
    own = lax.dynamic_slice_in_dim(returned, my_group * heads, heads, 1)
    combined = own.transpose(0, 2, 1, 3).reshape(tile_rows, tile_cols, channels)
    combined = combined + cycle_conv(values_new, conv_weight, conv_bias)
    return combined.astype(jnp.bfloat16)


LOG2E = 1.4426950408889634
NEG = -1e30
VMEM = pl.BlockSpec(memory_space=pltpu.VMEM)
SMEM = pl.BlockSpec(memory_space=pltpu.SMEM)
FAR = pl.BlockSpec(memory_space=pltpu.HBM)
LIMIT = pltpu.CompilerParams(vmem_limit_bytes=8 * 1024 * 1024)
SMALL = pltpu.CompilerParams(vmem_limit_bytes=4 * 1024 * 1024)


class Window:
    def __init__(self, grid, tile, info_ref, query_ref, pairs_ref):
        self.grid_rows, self.grid_cols = grid
        self.tile_rows, self.tile_cols = tile
        self.size = self.tile_rows * self.tile_cols
        self.info, self.query, self.pairs = info_ref, query_ref, pairs_ref
        self.scale = HD ** (-0.5) * LOG2E
        query = lax.broadcasted_iota(jnp.int32, (self.size, self.size), 0)
        key = lax.broadcasted_iota(jnp.int32, (self.size, self.size), 1)
        self.upper = key // self.tile_cols >= query // self.tile_cols
        self.left = key % self.tile_cols >= query % self.tile_cols
        self.upper_one = self.upper.astype(jnp.float32).astype(jnp.bfloat16)

    def slot(self, row, col):
        return self.info[2 + row * self.grid_cols + col % self.grid_cols]

    def tile(self, member, row, col):
        return self.pairs[self.slot(row, col), member].reshape(self.size, HD)

    def attend(self, row, col):
        query = self.query[self.slot(row, col), pl.ds(0, self.tile_rows)].reshape(self.size, HD)
        frames = range(self.pairs.shape[1] // 2)
        cols = [c for c in range(self.grid_cols) if abs(c - col) <= 2]
        up, down = row > 0, row + 1 < self.grid_rows
        rows = [r for r in (row - 1, row, row + 1) if 0 <= r < self.grid_rows]
        needed = [(f, r, c) for f in frames for c in cols for r in rows]
        keys = jnp.concatenate([self.tile(2 * f, r, c) for f, r, c in needed], axis=0)
        raw = lax.dot_general(query, keys, (((1,), (1,)), ((), ())), preferred_element_type=jnp.float32)
        scores = {key: raw[:, i * self.size : (i + 1) * self.size] for i, key in enumerate(needed)}
        blocks = []
        for f in frames:
            for c in cols:
                found = [(False, scores[f, row, c])]
                if up or down:
                    above = scores[f, row - 1, c] if up else NEG
                    found.append((True, jnp.where(self.upper, above, scores[f, row + 1, c] if down else NEG)))
                for off_row, block in found:
                    if c - col == 2:
                        block = jnp.where(self.left, NEG, block)
                    elif c - col == -2:
                        block = jnp.where(self.left, block, NEG)
                    blocks.append((f, off_row, c, block))
        top = blocks[0][3]
        for entry in blocks[1:]:
            top = jnp.maximum(top, entry[3])
        top = jnp.max(top, axis=1, keepdims=True)
        parts = []
        for f, off_row, c, block in blocks:
            weights = jnp.exp2((block - top) * self.scale).astype(jnp.bfloat16)
            if off_row and up and down:
                parts.append((f, row - 1, c, weights * self.upper_one))
                parts.append((f, row + 1, c, weights * (1 - self.upper_one)))
            elif off_row:
                parts.append((f, row + 1 if down else row - 1, c, weights))
            else:
                parts.append((f, row, c, weights))
        values = jnp.concatenate([self.tile(2 * f + 1, r, c) for f, r, c, _ in parts], axis=0)
        values = jnp.concatenate([values, jnp.ones_like(values)], axis=1)
        weights = jnp.concatenate([part for _, _, _, part in parts], axis=1)
        total = jnp.dot(weights, values, preferred_element_type=jnp.float32)
        return total[:, :HD] / total[:, HD:], top * self.scale + jnp.log2(total[:, HD:])

    def enhanced(self, row, col, weight_ref, bias_ref, before_ref, after_ref):
        shape = (self.tile_cols, HD)
        sub = lax.broadcasted_iota(jnp.int32, shape, 0)
        taps = [[weight_ref[a, pl.ds(b, 1), :] for b in range(3)] for a in range(3)]
        last = self.tile_cols - 1
        member = self.pairs.shape[1] - 1
        lines = []
        for key_row in range(row * self.tile_rows - 1, (row + 1) * self.tile_rows + 1):
            tile_row, line = key_row // self.tile_rows, key_row % self.tile_rows
            if tile_row < 0 or tile_row >= self.grid_rows:
                lines.append(None)
                continue

            def values(c):
                return self.pairs[self.slot(tile_row, c), member, line].astype(jnp.float32)

            def edge(ref, c):
                packed = ref[self.slot(tile_row, c), self.tile_rows + line // self.tile_cols].astype(jnp.float32)
                return jnp.broadcast_to(packed[line % self.tile_cols : line % self.tile_cols + 1], shape)

            here = values(col)
            before = pltpu.roll(values(col - 1), 1, 0) if col > 0 else edge(before_ref, self.grid_cols - 1)
            after = pltpu.roll(values(col + 1), last, 0) if col + 1 < self.grid_cols else edge(after_ref, 0)
            low = jnp.where(sub == 0, before, pltpu.roll(here, 1, 0))
            high = jnp.where(sub == last, after, pltpu.roll(here, last, 0))
            lines.append((low, here, high))
        sums = []
        for line in range(self.tile_rows):
            total = jnp.broadcast_to(bias_ref[...], shape)
            for a in range(3):
                if lines[line + a] is not None:
                    for b in range(3):
                        total = total + lines[line + a][b] * taps[a][b]
            sums.append(total)
        return jnp.stack(sums, axis=0)


def visit_kernel(grid, tile, first_col, info_ref, query_ref, pairs_ref, out_ref):
    window = Window(grid, tile, info_ref, query_ref, pairs_ref)
    size, count = window.size, grid[0] * grid[1]
    lane = lax.broadcasted_iota(jnp.int32, (size, HD), 1)
    levels = jnp.zeros((size, HD), jnp.float32)
    for row in range(grid[0]):
        for col in range(grid[1]):
            index = row * grid[1] + col
            part, level = window.attend(row, first_col + col)
            out_ref[index] = part.reshape(tile + (HD,)).astype(jnp.bfloat16)
            levels = jnp.where(lane == index, level, levels)
    high = levels.astype(jnp.bfloat16).astype(jnp.float32)
    middle = (levels - high).astype(jnp.bfloat16).astype(jnp.float32)
    packed = high + pltpu.roll(middle, count, 1) + pltpu.roll(levels - high - middle, 2 * count, 1)
    out_ref[count] = packed.reshape(tile + (HD,)).astype(jnp.bfloat16)


def own_kernel(
    grid, tile, info_ref, weight_ref, bias_ref, query_ref, pairs_ref, before_ref, after_ref, part_ref, level_ref, conv_ref
):
    window = Window(grid, tile, info_ref, query_ref, pairs_ref)
    for row in range(grid[0]):
        for col in range(grid[1]):
            index = row * grid[1] + col
            part_ref[index], level_ref[index] = window.attend(row, col)
            conv = window.enhanced(row, col, weight_ref, bias_ref, before_ref, after_ref)
            conv_ref[index] = conv.reshape(window.size, HD)


def join_kernel(grid, tile, info_ref, part_ref, level_ref, conv_ref, left_ref, right_ref, same_ref, beside_ref):
    size, count = tile[0] * tile[1], grid[0] * grid[1]
    present = [info_ref[0] > 0, info_ref[1] > 0]
    visits = (left_ref, right_ref)
    packed = [ref[count].reshape(size, HD).astype(jnp.float32) for ref in visits]
    for index in range(count):
        place = info_ref[2 + index]
        parts, levels = [part_ref[index]], [level_ref[index]]
        for ref, there, pack in zip(visits, present, packed):
            parts.append(ref[index].reshape(size, HD).astype(jnp.float32))
            level = pack[:, index : index + 1]
            for i in (1, 2):
                level = level + pack[:, i * count + index : i * count + index + 1]
            levels.append(jnp.broadcast_to(jnp.where(there, level, NEG), (size, HD)))
        top = jnp.maximum(jnp.maximum(levels[0], levels[1]), levels[2])
        shares = [jnp.exp2(level - top) for level in levels]
        mixed = sum(share * part for share, part in zip(shares, parts)) / sum(shares)
        out = (mixed + conv_ref[index]).reshape(tile + (HD,)).astype(jnp.bfloat16)

        @pl.when(place < count // 2)
        def _():
            same_ref[place] = out

        @pl.when(place >= count // 2)
        def _():
            beside_ref[place - count // 2] = out


def lanes(head):
    return pl.ds(pl.multiple_of(head * HD, HD), HD)


def move(copies, sems):
    started = [pltpu.make_async_copy(source, target, sems.at[i]) for i, (source, target) in enumerate(copies)]
    for copy in started:
        copy.start()
    for copy in started:
        copy.wait()


def pack_kernel(flips, side, me_ref, *refs):
    sources, buffers, sems = refs[: -len(flips) - 1], refs[-len(flips) - 1 : -1], refs[-1]
    copies = []
    for buffer, flip in zip(buffers, flips):
        for other in range(2):
            head = lanes(me_ref[0] ^ (flip ^ (side if other else 0)))
            for member, source in enumerate(sources):
                copies.append((source.at[:, :, head], buffer.at[other, member]))
    move(copies, sems)


def query_kernel(flips, side, me_ref, query_ref, values_ref, *refs):
    buffers, held_ref, sems = refs[:-2], refs[-2], refs[-1]
    tile_rows, tile_cols, _ = query_ref.shape
    places = [(buffer, flip, other) for buffer, flip in zip(buffers, flips) for other in range(2)]
    heads = [lanes(me_ref[0] ^ (flip ^ (side if other else 0))) for _, flip, other in places]
    copies = [(values_ref, held_ref)]
    for (buffer, _, other), head in zip(places, heads):
        copies.append((query_ref.at[:, :, head], buffer.at[other, pl.ds(0, tile_rows)]))
    move(copies, sems)
    sub = lax.broadcasted_iota(jnp.int32, (tile_cols, HD), 0)
    for (buffer, _, other), head in zip(places, heads):
        for start in range(0, tile_rows, tile_cols):
            packed = jnp.zeros((tile_cols, HD), jnp.float32)
            for line in range(tile_cols):
                values = held_ref[start + line, :, head].astype(jnp.float32)
                edge = jnp.where(me_ref[1] == 0, values[:1], values[tile_cols - 1 :])
                packed = jnp.where(sub == line, edge, packed)
            buffer[other, tile_rows + start // tile_cols] = packed.astype(jnp.bfloat16)


def unpack_kernel(flips, side, me_ref, same_ref, beside_ref, *refs):
    out_ref, sems = refs[-2], refs[-1]
    copies = []
    for i, flip in enumerate(flips):
        one, two = (refs[i - 1].at[0], refs[i - 1].at[1]) if i else (same_ref.at[0], beside_ref.at[0])
        copies.append((one, out_ref.at[:, :, lanes(me_ref[0] ^ flip)]))
        copies.append((two, out_ref.at[:, :, lanes(me_ref[0] ^ (flip ^ side))]))
    move(copies, sems)


def head_step(shape, queries, keys_new, values_new, keys_cache, values_cache, conv_weight, conv_bias):
    group_rows, group_cols, far = shape
    tile_rows, tile_cols, channels = queries.shape
    heads = channels // HD
    grid, tile = (group_rows, group_cols), (tile_rows, tile_cols)
    size = tile_rows * tile_cols
    axes = ("ht", "near")
    block = (tile_rows, tile_cols, HD)
    side = group_cols
    flips = [flip for flip in range(heads) if not flip & side]
    near = lax.axis_index("near").astype(jnp.int32)
    me = lax.axis_index("ht").astype(jnp.int32) * group_cols + near
    me_ref = jnp.stack([me, near])

    def swap(x, flip):
        return lax.ppermute(x, axes, [(s, s ^ flip) for s in range(heads)])

    def call(kernel, out_shape, params, cost, *operands, space=(VMEM, VMEM), scratch=()):
        return pl.pallas_call(
            kernel,
            out_shape=out_shape,
            in_specs=[SMEM] + [space[0]] * (len(operands) - 1),
            out_specs=jax.tree.map(lambda _: space[1], out_shape),
            scratch_shapes=scratch,
            compiler_params=params,
            cost_estimate=pl.CostEstimate(flops=cost << 30, bytes_accessed=1 << 20, transcendentals=0),
        )(*operands)

    def stay(x):
        return pltpu.with_memory_space_constraint(x, pltpu.HBM)

    def gather(buffers):
        got = [buffers[0]] + [swap(b, flip) for b, flip in zip(buffers[1:], flips[1:])]
        forward = jnp.stack([b[1] for b in got])
        beside = swap(forward, side)
        return jnp.concatenate([jnp.stack([b[0] for b in got]), beside], axis=0)

    up = [(i, i + 1) for i in range(far - 1)]
    down = [(i + 1, i) for i in range(far - 1)]
    edges = -(-tile_rows // tile_cols)
    buffer = jax.ShapeDtypeStruct((2, tile_rows + edges, tile_cols, HD), jnp.bfloat16)
    packed_query = call(
        functools.partial(query_kernel, flips, side),
        [buffer] * len(flips),
        SMALL,
        0,
        me_ref,
        stay(queries),
        stay(values_new),
        space=(FAR, VMEM),
        scratch=[pltpu.VMEM(values_new.shape, jnp.bfloat16), pltpu.SemaphoreType.DMA((heads + 1,))],
    )
    query = gather(packed_query)
    sources = (keys_cache[0], values_cache[0], keys_new, values_new)
    buffer = jax.ShapeDtypeStruct((2, len(sources)) + block, jnp.bfloat16)
    packed_pairs = call(
        functools.partial(pack_kernel, flips, side),
        [buffer] * len(flips),
        SMALL,
        0,
        me_ref,
        *map(stay, sources),
        space=(FAR, VMEM),
        scratch=[pltpu.SemaphoreType.DMA((heads * len(sources),))],
    )
    pairs = gather(packed_pairs)
    query_left = lax.ppermute(query, "far", up)
    query_right = lax.ppermute(query, "far", down)
    far_index = lax.axis_index("far")
    flip = me ^ jnp.arange(heads, dtype=jnp.int32)
    beside = (flip // side) % 2
    order = flip % side + flip // (2 * side) * side
    info = jnp.concatenate(
        [
            jnp.stack([far_index > 0, far_index < far - 1]).astype(jnp.int32),
            beside * len(flips) + order,
        ]
    )
    weight = lax.dynamic_slice_in_dim(conv_weight, me * HD, HD, 2)
    bias = lax.dynamic_slice_in_dim(conv_bias.reshape(1, channels), me * HD, HD, 1)

    def visit(queries, first_col):
        kernel = functools.partial(visit_kernel, grid, tile, first_col)
        return call(kernel, jax.ShapeDtypeStruct((heads + 1,) + block, jnp.bfloat16), LIMIT, 4, info, queries, pairs)

    left_part = visit(query_left, -group_cols)
    from_right = lax.ppermute(left_part, "far", down)
    right_part = visit(query_right, group_cols)
    from_left = lax.ppermute(right_part, "far", up)
    part = jax.ShapeDtypeStruct((heads, size, HD), jnp.float32)
    kernel = functools.partial(own_kernel, grid, tile)
    own = call(kernel, [part] * 3, LIMIT, 4, info, weight, bias, query, pairs, query_left, query_right)
    half = jax.ShapeDtypeStruct((len(flips),) + block, jnp.bfloat16)
    kernel = functools.partial(join_kernel, grid, tile)
    same, other = call(kernel, [half, half], LIMIT, 1, info, *own, from_left, from_right)
    received = swap(other, side)
    got = []
    for i in range(1, len(flips)):
        got.append(swap(jnp.stack([same[i], received[i]]), flips[i]))
    return call(
        functools.partial(unpack_kernel, flips, side),
        jax.ShapeDtypeStruct(queries.shape, jnp.bfloat16),
        SMALL,
        0,
        me_ref,
        same,
        received,
        *got,
        space=(VMEM, FAR),
        scratch=[pltpu.SemaphoreType.DMA((heads,))],
    )


def grouping(mesh, heads):
    rows, cols = mesh.shape["ht"], mesh.shape["wt"]
    group_rows = rows
    group_cols = heads // group_rows if heads % group_rows == 0 else 0
    if group_cols != 2 or cols % group_cols:
        return None
    return group_rows, group_cols, cols // group_cols


def solution(mesh):
    def program(queries, *rest):
        heads = queries.shape[2] // HD
        shape = grouping(mesh, heads)
        if shape is None or queries.shape[0] != mesh.shape["ht"] * (WIN // 2) or queries.shape[1] != mesh.shape["wt"] * (WIN // 4):
            placed = (P("ht", "wt", None),) * 3 + (P(None, "ht", "wt", None),) * 2 + (P(), P())
            return jax.shard_map(
                shards, mesh=mesh, in_specs=placed, out_specs=P("ht", "wt", None), check_vma=False
            )(queries, *rest)
        devices = mesh.devices.reshape(shape[0], shape[2], shape[1])
        split = Mesh(devices, ("ht", "far", "near"))
        tile = P("ht", ("far", "near"), None)
        past = P(None, "ht", ("far", "near"), None)
        step = jax.shard_map(
            functools.partial(head_step, shape),
            mesh=split,
            in_specs=(tile, tile, tile, past, past, P(), P()),
            out_specs=tile,
            check_vma=False,
        )
        return step(queries, *rest)

    return program
```

```python
import functools

import jax
import jax.numpy as jnp
from jax import lax
from jax.experimental import pallas as pl
from jax.experimental.pallas import tpu as pltpu
from jax.sharding import Mesh, PartitionSpec as P


HD = 128
WIN = 32


def with_halo(block, sides, width):
    for axis, dim in sides:
        count = lax.axis_size(axis)
        forward = [(i, i + 1) for i in range(count - 1)]
        backward = [(target, source) for source, target in forward]
        low = lax.ppermute(
            lax.slice_in_dim(block, block.shape[dim] - width, None, axis=dim), axis, forward
        )
        high = lax.ppermute(lax.slice_in_dim(block, 0, width, axis=dim), axis, backward)
        block = jnp.concatenate([low, block, high], axis=dim)
    return block


def window_allowed(row_start, col_start, frame_rows, frame_cols, tile_rows, tile_cols, half_win):
    ext_rows = jnp.arange(tile_rows + 2 * half_win, dtype=jnp.int32) - half_win
    ext_cols = jnp.arange(tile_cols + 2 * half_win, dtype=jnp.int32) - half_win
    query_rows = jnp.arange(tile_rows, dtype=jnp.int32)
    query_cols = jnp.arange(tile_cols, dtype=jnp.int32)
    row_delta = ext_rows[None, :] - query_rows[:, None]
    col_delta = ext_cols[None, :] - query_cols[:, None]
    global_rows = row_start + ext_rows
    global_cols = col_start + ext_cols
    row_valid = (
        (row_delta >= -half_win)
        & (row_delta < half_win)
        & ((global_rows >= 0) & (global_rows < frame_rows))[None, :]
    )
    col_valid = (
        (col_delta >= -half_win)
        & (col_delta < half_win)
        & ((global_cols >= 0) & (global_cols < frame_cols))[None, :]
    )
    allowed = row_valid[:, None, :, None] & col_valid[None, :, None, :]
    return allowed.reshape(
        tile_rows * tile_cols, (tile_rows + 2 * half_win) * (tile_cols + 2 * half_win)
    )


def attend(query_rows, keys_flat, values_flat, allowed, heads, head_dim):
    score_scale = head_dim ** (-0.5)

    def one_head(head_index):
        scores = (
            jnp.einsum("qd,kd->qk", query_rows, keys_flat, preferred_element_type=jnp.float32)
            * score_scale
        )
        scores = jnp.where(allowed, scores, -1e30)
        row_top = jnp.max(scores, axis=1, keepdims=True)
        weights_f = jnp.exp(scores - row_top)
        denominator = jnp.sum(weights_f, axis=1, keepdims=True)
        numerator = jnp.dot(
            weights_f.astype(jnp.bfloat16), values_flat, preferred_element_type=jnp.float32
        )
        return numerator / denominator

    outputs = lax.map(one_head, jnp.arange(heads, dtype=jnp.int32))
    return outputs.transpose(1, 0, 2).reshape(query_rows.shape[0], heads * head_dim)


def local_conv(padded, conv_weight, conv_bias, tile_rows, tile_cols):
    enhanced = jnp.zeros((tile_rows, tile_cols, padded.shape[2]), jnp.float32) + conv_bias
    for row_shift in range(3):
        for col_shift in range(3):
            enhanced = (
                enhanced
                + padded[
                    row_shift : row_shift + tile_rows, col_shift : col_shift + tile_cols
                ].astype(jnp.float32)
                * conv_weight[row_shift, col_shift]
            )
    return enhanced


def cycle_conv(values_new, conv_weight, conv_bias):
    tile_rows, tile_cols, _ = values_new.shape
    padded = with_halo(values_new, (("ht", 0), ("wt", 1)), 1)
    return local_conv(padded, conv_weight, conv_bias, tile_rows, tile_cols)


def shards(queries, keys_new, values_new, keys_cache, values_cache, conv_weight, conv_bias):
    tile_rows, tile_cols, channels = queries.shape
    frames = keys_cache.shape[0] + 1
    half_win = WIN // 2
    stacked = jnp.concatenate([keys_cache, keys_new[None], values_cache, values_new[None]], axis=0)
    row_start = lax.axis_index("ht") * tile_rows
    frame_rows = tile_rows * lax.axis_size("ht")
    frame_cols = tile_cols * lax.axis_size("wt")
    heads = channels // HD
    copies = lax.axis_size("wt") // heads
    bundle = jnp.concatenate([stacked, queries[None]], axis=0)
    members = bundle.shape[0]
    spread = bundle.reshape(members, tile_rows, tile_cols, 1, heads, HD)
    spread = jnp.broadcast_to(spread, (members, tile_rows, tile_cols, copies, heads, HD))
    spread = spread.reshape(members, tile_rows, tile_cols, copies * heads, HD)
    strips = lax.all_to_all(spread, "wt", split_axis=3, concat_axis=2, tiled=True)
    strips = strips.reshape(members, tile_rows, frame_cols, HD)
    device_index = lax.axis_index("wt")
    my_group = device_index // heads
    block_width = tile_cols * heads
    block_start = my_group * block_width
    padded_cols = jnp.pad(strips, ((0, 0), (0, 0), (half_win, half_win), (0, 0)))
    window = lax.dynamic_slice_in_dim(padded_cols, block_start, block_width + 2 * half_win, 2)
    query_part = window[2 * frames, :, half_win : half_win + block_width]
    region = with_halo(window[: 2 * frames], (("ht", 1),), half_win)

    def one_block(step):
        offset = step * tile_cols
        query_block = lax.dynamic_slice_in_dim(query_part, offset, tile_cols, 1).reshape(
            tile_rows * tile_cols, HD
        )
        sub = lax.dynamic_slice_in_dim(region, offset, tile_cols + 2 * half_win, 2)
        keys_flat = sub[:frames].reshape(-1, HD)
        values_flat = sub[frames:].reshape(-1, HD)
        allowed = window_allowed(
            row_start, block_start + offset, frame_rows, frame_cols, tile_rows, tile_cols, half_win
        )
        allowed = jnp.tile(allowed, (1, frames))
        result = attend(query_block, keys_flat, values_flat, allowed, 1, HD)
        return result.reshape(tile_rows, tile_cols, HD)

    blocks = lax.map(one_block, jnp.arange(heads, dtype=jnp.int32))
    payload = blocks.transpose(1, 0, 2, 3)
    payload = jnp.broadcast_to(payload[:, None], (tile_rows, copies, heads, tile_cols, HD))
    payload = payload.reshape(tile_rows, copies * heads, tile_cols, HD)
    returned = lax.all_to_all(
        payload.astype(jnp.bfloat16), "wt", split_axis=1, concat_axis=1, tiled=True
    ).astype(payload.dtype)
    own = lax.dynamic_slice_in_dim(returned, my_group * heads, heads, 1)
    combined = own.transpose(0, 2, 1, 3).reshape(tile_rows, tile_cols, channels)
    combined = combined + cycle_conv(values_new, conv_weight, conv_bias)
    return combined.astype(jnp.bfloat16)


LOG2E = 1.4426950408889634
NEG = -1e30
VMEM = pl.BlockSpec(memory_space=pltpu.VMEM)
SMEM = pl.BlockSpec(memory_space=pltpu.SMEM)
FAR = pl.BlockSpec(memory_space=pltpu.HBM)
LIMIT = pltpu.CompilerParams(vmem_limit_bytes=8 * 1024 * 1024)
SMALL = pltpu.CompilerParams(vmem_limit_bytes=4 * 1024 * 1024)


class Window:
    def __init__(self, grid, tile, info_ref, query_ref, pairs_ref):
        self.grid_rows, self.grid_cols = grid
        self.tile_rows, self.tile_cols = tile
        self.size = self.tile_rows * self.tile_cols
        self.info, self.query, self.pairs = info_ref, query_ref, pairs_ref
        self.scale = HD ** (-0.5) * LOG2E
        query = lax.broadcasted_iota(jnp.int32, (self.size, self.size), 0)
        key = lax.broadcasted_iota(jnp.int32, (self.size, self.size), 1)
        self.upper = key // self.tile_cols >= query // self.tile_cols
        self.left = key % self.tile_cols >= query % self.tile_cols
        self.upper_one = self.upper.astype(jnp.float32).astype(jnp.bfloat16)

    def slot(self, row, col):
        return self.info[2 + row * self.grid_cols + col % self.grid_cols]

    def tile(self, member, row, col):
        return self.pairs[self.slot(row, col), member].reshape(self.size, HD)

    def attend(self, row, col):
        query = self.query[self.slot(row, col), pl.ds(0, self.tile_rows)].reshape(self.size, HD)
        frames = range(self.pairs.shape[1] // 2)
        cols = [c for c in range(self.grid_cols) if abs(c - col) <= 2]
        up, down = row > 0, row + 1 < self.grid_rows
        rows = [r for r in (row - 1, row, row + 1) if 0 <= r < self.grid_rows]
        needed = [(f, r, c) for f in frames for c in cols for r in rows]
        keys = jnp.concatenate([self.tile(2 * f, r, c) for f, r, c in needed], axis=0)
        raw = lax.dot_general(query, keys, (((1,), (1,)), ((), ())), preferred_element_type=jnp.float32)
        scores = {key: raw[:, i * self.size : (i + 1) * self.size] for i, key in enumerate(needed)}
        blocks = []
        for f in frames:
            for c in cols:
                found = [(False, scores[f, row, c])]
                if up or down:
                    above = scores[f, row - 1, c] if up else NEG
                    found.append((True, jnp.where(self.upper, above, scores[f, row + 1, c] if down else NEG)))
                for off_row, block in found:
                    if c - col == 2:
                        block = jnp.where(self.left, NEG, block)
                    elif c - col == -2:
                        block = jnp.where(self.left, block, NEG)
                    blocks.append((f, off_row, c, block))
        top = blocks[0][3]
        for entry in blocks[1:]:
            top = jnp.maximum(top, entry[3])
        top = jnp.max(top, axis=1, keepdims=True)
        parts = []
        for f, off_row, c, block in blocks:
            weights = jnp.exp2((block - top) * self.scale).astype(jnp.bfloat16)
            if off_row and up and down:
                parts.append((f, row - 1, c, weights * self.upper_one))
                parts.append((f, row + 1, c, weights * (1 - self.upper_one)))
            elif off_row:
                parts.append((f, row + 1 if down else row - 1, c, weights))
            else:
                parts.append((f, row, c, weights))
        values = jnp.concatenate([self.tile(2 * f + 1, r, c) for f, r, c, _ in parts], axis=0)
        values = jnp.concatenate([values, jnp.ones_like(values)], axis=1)
        weights = jnp.concatenate([part for _, _, _, part in parts], axis=1)
        total = jnp.dot(weights, values, preferred_element_type=jnp.float32)
        return total[:, :HD] / total[:, HD:], top * self.scale + jnp.log2(total[:, HD:])

    def enhanced(self, row, col, weight_ref, bias_ref, before_ref, after_ref):
        shape = (self.tile_cols, HD)
        sub = lax.broadcasted_iota(jnp.int32, shape, 0)
        taps = [[weight_ref[a, pl.ds(b, 1), :] for b in range(3)] for a in range(3)]
        last = self.tile_cols - 1
        member = self.pairs.shape[1] - 1
        lines = []
        for key_row in range(row * self.tile_rows - 1, (row + 1) * self.tile_rows + 1):
            tile_row, line = key_row // self.tile_rows, key_row % self.tile_rows
            if tile_row < 0 or tile_row >= self.grid_rows:
                lines.append(None)
                continue

            def values(c):
                return self.pairs[self.slot(tile_row, c), member, line].astype(jnp.float32)

            def edge(ref, c):
                packed = ref[self.slot(tile_row, c), self.tile_rows + line // self.tile_cols].astype(jnp.float32)
                return jnp.broadcast_to(packed[line % self.tile_cols : line % self.tile_cols + 1], shape)

            here = values(col)
            before = pltpu.roll(values(col - 1), 1, 0) if col > 0 else edge(before_ref, self.grid_cols - 1)
            after = pltpu.roll(values(col + 1), last, 0) if col + 1 < self.grid_cols else edge(after_ref, 0)
            low = jnp.where(sub == 0, before, pltpu.roll(here, 1, 0))
            high = jnp.where(sub == last, after, pltpu.roll(here, last, 0))
            lines.append((low, here, high))
        sums = []
        for line in range(self.tile_rows):
            total = jnp.broadcast_to(bias_ref[...], shape)
            for a in range(3):
                if lines[line + a] is not None:
                    for b in range(3):
                        total = total + lines[line + a][b] * taps[a][b]
            sums.append(total)
        return jnp.stack(sums, axis=0)


def visit_kernel(grid, tile, first_col, info_ref, query_ref, pairs_ref, out_ref):
    window = Window(grid, tile, info_ref, query_ref, pairs_ref)
    size, count = window.size, grid[0] * grid[1]
    lane = lax.broadcasted_iota(jnp.int32, (size, HD), 1)
    levels = jnp.zeros((size, HD), jnp.float32)
    for row in range(grid[0]):
        for col in range(grid[1]):
            index = row * grid[1] + col
            part, level = window.attend(row, first_col + col)
            out_ref[index] = part.reshape(tile + (HD,)).astype(jnp.bfloat16)
            levels = jnp.where(lane == index, level, levels)
    high = levels.astype(jnp.bfloat16).astype(jnp.float32)
    middle = (levels - high).astype(jnp.bfloat16).astype(jnp.float32)
    packed = high + pltpu.roll(middle, count, 1) + pltpu.roll(levels - high - middle, 2 * count, 1)
    out_ref[count] = packed.reshape(tile + (HD,)).astype(jnp.bfloat16)


def own_kernel(
    grid, tile, info_ref, weight_ref, bias_ref, query_ref, pairs_ref, before_ref, after_ref, part_ref, level_ref, conv_ref
):
    window = Window(grid, tile, info_ref, query_ref, pairs_ref)
    for row in range(grid[0]):
        for col in range(grid[1]):
            index = row * grid[1] + col
            part_ref[index], level_ref[index] = window.attend(row, col)
            conv = window.enhanced(row, col, weight_ref, bias_ref, before_ref, after_ref)
            conv_ref[index] = conv.reshape(window.size, HD)


def join_kernel(grid, tile, info_ref, part_ref, level_ref, conv_ref, left_ref, right_ref, same_ref, beside_ref):
    size, count = tile[0] * tile[1], grid[0] * grid[1]
    present = [info_ref[0] > 0, info_ref[1] > 0]
    visits = (left_ref, right_ref)
    packed = [ref[count].reshape(size, HD).astype(jnp.float32) for ref in visits]
    for index in range(count):
        place = info_ref[2 + index]
        parts, levels = [part_ref[index]], [level_ref[index]]
        for ref, there, pack in zip(visits, present, packed):
            parts.append(ref[index].reshape(size, HD).astype(jnp.float32))
            level = pack[:, index : index + 1]
            for i in (1, 2):
                level = level + pack[:, i * count + index : i * count + index + 1]
            levels.append(jnp.broadcast_to(jnp.where(there, level, NEG), (size, HD)))
        top = jnp.maximum(jnp.maximum(levels[0], levels[1]), levels[2])
        shares = [jnp.exp2(level - top) for level in levels]
        mixed = sum(share * part for share, part in zip(shares, parts)) / sum(shares)
        out = (mixed + conv_ref[index]).reshape(tile + (HD,)).astype(jnp.bfloat16)

        @pl.when(place < count // 2)
        def _():
            same_ref[place] = out

        @pl.when(place >= count // 2)
        def _():
            beside_ref[place - count // 2] = out


def lanes(head):
    return pl.ds(pl.multiple_of(head * HD, HD), HD)


def pack_kernel(flips, side, me_ref, *refs):
    count = len(flips)
    sources = refs[: -2 * count - 2]
    query_buffers, pair_buffers = refs[-2 * count - 2 : -count - 2], refs[-count - 2 : -2]
    held_ref, sems = refs[-2], refs[-1]
    tile_rows, tile_cols, _ = sources[0].shape
    copies = [pltpu.make_async_copy(x, held_ref.at[i], sems.at[i]) for i, x in enumerate(sources)]
    for copy in copies:
        copy.start()
    heads = [[lanes(me_ref[0] ^ (flip ^ beside)) for beside in (0, side)] for flip in flips]
    copies[0].wait()
    for buffer, pair in zip(query_buffers, heads):
        for other in range(2):
            buffer[other, pl.ds(0, tile_rows)] = held_ref[0, :, :, pair[other]]
    copies[1].wait()
    sub = lax.broadcasted_iota(jnp.int32, (tile_cols, HD), 0)
    for buffer, pair in zip(query_buffers, heads):
        for other in range(2):
            for start in range(0, tile_rows, tile_cols):
                packed = jnp.zeros((tile_cols, HD), jnp.float32)
                for line in range(tile_cols):
                    values = held_ref[1, start + line, :, pair[other]].astype(jnp.float32)
                    edge = jnp.where(me_ref[1] == 0, values[:1], values[tile_cols - 1 :])
                    packed = jnp.where(sub == line, edge, packed)
                buffer[other, tile_rows + start // tile_cols] = packed.astype(jnp.bfloat16)
    for member, source in enumerate((*range(2, len(sources)), 1)):
        if member < len(sources) - 2:
            copies[source].wait()
        for buffer, pair in zip(pair_buffers, heads):
            for other in range(2):
                buffer[other, member] = held_ref[source, :, :, pair[other]]


def unpack_kernel(flips, side, me_ref, same_ref, beside_ref, *refs):
    out_ref = refs[-1]
    out_ref[:, :, lanes(me_ref[0])] = same_ref[0]
    out_ref[:, :, lanes(me_ref[0] ^ side)] = beside_ref[0]
    for i, flip in enumerate(flips[1:]):
        out_ref[:, :, lanes(me_ref[0] ^ flip)] = refs[i][0]
        out_ref[:, :, lanes(me_ref[0] ^ (flip ^ side))] = refs[i][1]


def head_step(shape, queries, keys_new, values_new, keys_cache, values_cache, conv_weight, conv_bias):
    group_rows, group_cols, far = shape
    tile_rows, tile_cols, channels = queries.shape
    heads = channels // HD
    grid, tile = (group_rows, group_cols), (tile_rows, tile_cols)
    size = tile_rows * tile_cols
    axes = ("ht", "near")
    block = (tile_rows, tile_cols, HD)
    side = group_cols
    flips = [flip for flip in range(heads) if not flip & side]
    near = lax.axis_index("near").astype(jnp.int32)
    me = lax.axis_index("ht").astype(jnp.int32) * group_cols + near
    me_ref = jnp.stack([me, near])

    def swap(x, flip):
        return lax.ppermute(x, axes, [(s, s ^ flip) for s in range(heads)])

    def call(kernel, out_shape, params, cost, *operands, space=(VMEM, VMEM), scratch=()):
        return pl.pallas_call(
            kernel,
            out_shape=out_shape,
            in_specs=[SMEM] + [space[0]] * (len(operands) - 1),
            out_specs=jax.tree.map(lambda _: space[1], out_shape),
            scratch_shapes=scratch,
            compiler_params=params,
            cost_estimate=pl.CostEstimate(flops=cost << 30, bytes_accessed=1 << 20, transcendentals=0),
        )(*operands)

    def stay(x):
        return pltpu.with_memory_space_constraint(x, pltpu.HBM)

    def gather(buffers):
        got = [buffers[0]] + [swap(b, flip) for b, flip in zip(buffers[1:], flips[1:])]
        forward = jnp.stack([b[1] for b in got])
        beside = swap(forward, side)
        return jnp.concatenate([jnp.stack([b[0] for b in got]), beside], axis=0)

    up = [(i, i + 1) for i in range(far - 1)]
    down = [(i + 1, i) for i in range(far - 1)]
    edges = -(-tile_rows // tile_cols)
    sources = (queries, values_new, keys_cache[0], values_cache[0], keys_new)
    query_buffer = jax.ShapeDtypeStruct((2, tile_rows + edges, tile_cols, HD), jnp.bfloat16)
    pair_buffer = jax.ShapeDtypeStruct((2, len(sources) - 1) + block, jnp.bfloat16)
    packed = call(
        functools.partial(pack_kernel, flips, side),
        [query_buffer] * len(flips) + [pair_buffer] * len(flips),
        SMALL,
        0,
        me_ref,
        *map(stay, sources),
        space=(FAR, VMEM),
        scratch=[pltpu.VMEM((len(sources),) + queries.shape, jnp.bfloat16), pltpu.SemaphoreType.DMA((len(sources),))],
    )
    query = gather(packed[: len(flips)])
    pairs = gather(packed[len(flips) :])
    query_left = lax.ppermute(query, "far", up)
    query_right = lax.ppermute(query, "far", down)
    far_index = lax.axis_index("far")
    flip = me ^ jnp.arange(heads, dtype=jnp.int32)
    beside = (flip // side) % 2
    order = flip % side + flip // (2 * side) * side
    info = jnp.concatenate(
        [
            jnp.stack([far_index > 0, far_index < far - 1]).astype(jnp.int32),
            beside * len(flips) + order,
        ]
    )
    weight = lax.dynamic_slice_in_dim(conv_weight, me * HD, HD, 2)
    bias = lax.dynamic_slice_in_dim(conv_bias.reshape(1, channels), me * HD, HD, 1)

    def visit(queries, first_col):
        kernel = functools.partial(visit_kernel, grid, tile, first_col)
        return call(kernel, jax.ShapeDtypeStruct((heads + 1,) + block, jnp.bfloat16), LIMIT, 4, info, queries, pairs)

    left_part = visit(query_left, -group_cols)
    from_right = lax.ppermute(left_part, "far", down)
    right_part = visit(query_right, group_cols)
    from_left = lax.ppermute(right_part, "far", up)
    part = jax.ShapeDtypeStruct((heads, size, HD), jnp.float32)
    kernel = functools.partial(own_kernel, grid, tile)
    own = call(kernel, [part] * 3, LIMIT, 4, info, weight, bias, query, pairs, query_left, query_right)
    half = jax.ShapeDtypeStruct((len(flips),) + block, jnp.bfloat16)
    kernel = functools.partial(join_kernel, grid, tile)
    same, other = call(kernel, [half, half], LIMIT, 1, info, *own, from_left, from_right)
    received = swap(other, side)
    got = []
    for i in range(1, len(flips)):
        got.append(swap(jnp.stack([same[i], received[i]]), flips[i]))
    return call(
        functools.partial(unpack_kernel, flips, side),
        jax.ShapeDtypeStruct(queries.shape, jnp.bfloat16),
        SMALL,
        0,
        me_ref,
        same,
        received,
        *got,
    )


def grouping(mesh, heads):
    rows, cols = mesh.shape["ht"], mesh.shape["wt"]
    group_rows = rows
    group_cols = heads // group_rows if heads % group_rows == 0 else 0
    if group_cols != 2 or cols % group_cols:
        return None
    return group_rows, group_cols, cols // group_cols


def solution(mesh):
    def program(queries, *rest):
        heads = queries.shape[2] // HD
        shape = grouping(mesh, heads)
        if shape is None or queries.shape[0] != mesh.shape["ht"] * (WIN // 2) or queries.shape[1] != mesh.shape["wt"] * (WIN // 4):
            placed = (P("ht", "wt", None),) * 3 + (P(None, "ht", "wt", None),) * 2 + (P(), P())
            return jax.shard_map(
                shards, mesh=mesh, in_specs=placed, out_specs=P("ht", "wt", None), check_vma=False
            )(queries, *rest)
        devices = mesh.devices.reshape(shape[0], shape[2], shape[1])
        split = Mesh(devices, ("ht", "far", "near"))
        tile = P("ht", ("far", "near"), None)
        past = P(None, "ht", ("far", "near"), None)
        step = jax.shard_map(
            functools.partial(head_step, shape),
            mesh=split,
            in_specs=(tile, tile, tile, past, past, P(), P()),
            out_specs=tile,
            check_vma=False,
        )
        return step(queries, *rest)

    return program
```

```python
import functools

import jax
import jax.numpy as jnp
from jax import lax
from jax.experimental import pallas as pl
from jax.experimental.pallas import tpu as pltpu
from jax.sharding import Mesh, PartitionSpec as P


HD = 128
WIN = 32


def with_halo(block, sides, width):
    for axis, dim in sides:
        count = lax.axis_size(axis)
        forward = [(i, i + 1) for i in range(count - 1)]
        backward = [(target, source) for source, target in forward]
        low = lax.ppermute(
            lax.slice_in_dim(block, block.shape[dim] - width, None, axis=dim), axis, forward
        )
        high = lax.ppermute(lax.slice_in_dim(block, 0, width, axis=dim), axis, backward)
        block = jnp.concatenate([low, block, high], axis=dim)
    return block


def window_allowed(row_start, col_start, frame_rows, frame_cols, tile_rows, tile_cols, half_win):
    ext_rows = jnp.arange(tile_rows + 2 * half_win, dtype=jnp.int32) - half_win
    ext_cols = jnp.arange(tile_cols + 2 * half_win, dtype=jnp.int32) - half_win
    query_rows = jnp.arange(tile_rows, dtype=jnp.int32)
    query_cols = jnp.arange(tile_cols, dtype=jnp.int32)
    row_delta = ext_rows[None, :] - query_rows[:, None]
    col_delta = ext_cols[None, :] - query_cols[:, None]
    global_rows = row_start + ext_rows
    global_cols = col_start + ext_cols
    row_valid = (
        (row_delta >= -half_win)
        & (row_delta < half_win)
        & ((global_rows >= 0) & (global_rows < frame_rows))[None, :]
    )
    col_valid = (
        (col_delta >= -half_win)
        & (col_delta < half_win)
        & ((global_cols >= 0) & (global_cols < frame_cols))[None, :]
    )
    allowed = row_valid[:, None, :, None] & col_valid[None, :, None, :]
    return allowed.reshape(
        tile_rows * tile_cols, (tile_rows + 2 * half_win) * (tile_cols + 2 * half_win)
    )


def attend(query_rows, keys_flat, values_flat, allowed, heads, head_dim):
    score_scale = head_dim ** (-0.5)

    def one_head(head_index):
        scores = (
            jnp.einsum("qd,kd->qk", query_rows, keys_flat, preferred_element_type=jnp.float32)
            * score_scale
        )
        scores = jnp.where(allowed, scores, -1e30)
        row_top = jnp.max(scores, axis=1, keepdims=True)
        weights_f = jnp.exp(scores - row_top)
        denominator = jnp.sum(weights_f, axis=1, keepdims=True)
        numerator = jnp.dot(
            weights_f.astype(jnp.bfloat16), values_flat, preferred_element_type=jnp.float32
        )
        return numerator / denominator

    outputs = lax.map(one_head, jnp.arange(heads, dtype=jnp.int32))
    return outputs.transpose(1, 0, 2).reshape(query_rows.shape[0], heads * head_dim)


def local_conv(padded, conv_weight, conv_bias, tile_rows, tile_cols):
    enhanced = jnp.zeros((tile_rows, tile_cols, padded.shape[2]), jnp.float32) + conv_bias
    for row_shift in range(3):
        for col_shift in range(3):
            enhanced = (
                enhanced
                + padded[
                    row_shift : row_shift + tile_rows, col_shift : col_shift + tile_cols
                ].astype(jnp.float32)
                * conv_weight[row_shift, col_shift]
            )
    return enhanced


def cycle_conv(values_new, conv_weight, conv_bias):
    tile_rows, tile_cols, _ = values_new.shape
    padded = with_halo(values_new, (("ht", 0), ("wt", 1)), 1)
    return local_conv(padded, conv_weight, conv_bias, tile_rows, tile_cols)


def shards(queries, keys_new, values_new, keys_cache, values_cache, conv_weight, conv_bias):
    tile_rows, tile_cols, channels = queries.shape
    frames = keys_cache.shape[0] + 1
    half_win = WIN // 2
    stacked = jnp.concatenate([keys_cache, keys_new[None], values_cache, values_new[None]], axis=0)
    row_start = lax.axis_index("ht") * tile_rows
    frame_rows = tile_rows * lax.axis_size("ht")
    frame_cols = tile_cols * lax.axis_size("wt")
    heads = channels // HD
    copies = lax.axis_size("wt") // heads
    bundle = jnp.concatenate([stacked, queries[None]], axis=0)
    members = bundle.shape[0]
    spread = bundle.reshape(members, tile_rows, tile_cols, 1, heads, HD)
    spread = jnp.broadcast_to(spread, (members, tile_rows, tile_cols, copies, heads, HD))
    spread = spread.reshape(members, tile_rows, tile_cols, copies * heads, HD)
    strips = lax.all_to_all(spread, "wt", split_axis=3, concat_axis=2, tiled=True)
    strips = strips.reshape(members, tile_rows, frame_cols, HD)
    device_index = lax.axis_index("wt")
    my_group = device_index // heads
    block_width = tile_cols * heads
    block_start = my_group * block_width
    padded_cols = jnp.pad(strips, ((0, 0), (0, 0), (half_win, half_win), (0, 0)))
    window = lax.dynamic_slice_in_dim(padded_cols, block_start, block_width + 2 * half_win, 2)
    query_part = window[2 * frames, :, half_win : half_win + block_width]
    region = with_halo(window[: 2 * frames], (("ht", 1),), half_win)

    def one_block(step):
        offset = step * tile_cols
        query_block = lax.dynamic_slice_in_dim(query_part, offset, tile_cols, 1).reshape(
            tile_rows * tile_cols, HD
        )
        sub = lax.dynamic_slice_in_dim(region, offset, tile_cols + 2 * half_win, 2)
        keys_flat = sub[:frames].reshape(-1, HD)
        values_flat = sub[frames:].reshape(-1, HD)
        allowed = window_allowed(
            row_start, block_start + offset, frame_rows, frame_cols, tile_rows, tile_cols, half_win
        )
        allowed = jnp.tile(allowed, (1, frames))
        result = attend(query_block, keys_flat, values_flat, allowed, 1, HD)
        return result.reshape(tile_rows, tile_cols, HD)

    blocks = lax.map(one_block, jnp.arange(heads, dtype=jnp.int32))
    payload = blocks.transpose(1, 0, 2, 3)
    payload = jnp.broadcast_to(payload[:, None], (tile_rows, copies, heads, tile_cols, HD))
    payload = payload.reshape(tile_rows, copies * heads, tile_cols, HD)
    returned = lax.all_to_all(
        payload.astype(jnp.bfloat16), "wt", split_axis=1, concat_axis=1, tiled=True
    ).astype(payload.dtype)
    own = lax.dynamic_slice_in_dim(returned, my_group * heads, heads, 1)
    combined = own.transpose(0, 2, 1, 3).reshape(tile_rows, tile_cols, channels)
    combined = combined + cycle_conv(values_new, conv_weight, conv_bias)
    return combined.astype(jnp.bfloat16)


LOG2E = 1.4426950408889634
NEG = -1e30
VMEM = pl.BlockSpec(memory_space=pltpu.VMEM)
SMEM = pl.BlockSpec(memory_space=pltpu.SMEM)
FAR = pl.BlockSpec(memory_space=pltpu.HBM)
LIMIT = pltpu.CompilerParams(vmem_limit_bytes=8 * 1024 * 1024)
SMALL = pltpu.CompilerParams(vmem_limit_bytes=4 * 1024 * 1024)


class Window:
    def __init__(self, grid, tile, info_ref, query_ref, pairs_ref):
        self.grid_rows, self.grid_cols = grid
        self.tile_rows, self.tile_cols = tile
        self.size = self.tile_rows * self.tile_cols
        self.info, self.query, self.pairs = info_ref, query_ref, pairs_ref
        self.scale = HD ** (-0.5) * LOG2E
        query = lax.broadcasted_iota(jnp.int32, (self.size, self.size), 0)
        key = lax.broadcasted_iota(jnp.int32, (self.size, self.size), 1)
        self.upper = key // self.tile_cols >= query // self.tile_cols
        self.left = key % self.tile_cols >= query % self.tile_cols
        self.upper_one = self.upper.astype(jnp.float32).astype(jnp.bfloat16)

    def slot(self, row, col):
        return self.info[2 + row * self.grid_cols + col % self.grid_cols]

    def tile(self, member, row, col):
        return self.pairs[self.slot(row, col), member].reshape(self.size, HD)

    def scores(self, row, col):
        query = self.query[self.slot(row, col), pl.ds(0, self.tile_rows)].reshape(self.size, HD)
        frames = range(self.pairs.shape[1] // 2)
        cols = [c for c in range(self.grid_cols) if abs(c - col) <= 2]
        up, down = row > 0, row + 1 < self.grid_rows
        rows = [r for r in (row - 1, row, row + 1) if 0 <= r < self.grid_rows]
        needed = [(f, r, c) for f in frames for c in cols for r in rows]
        keys = jnp.concatenate([self.tile(2 * f, r, c) for f, r, c in needed], axis=0)
        raw = lax.dot_general(query, keys, (((1,), (1,)), ((), ())), preferred_element_type=jnp.float32)
        scores = {key: raw[:, i * self.size : (i + 1) * self.size] for i, key in enumerate(needed)}
        blocks = []
        for f in frames:
            for c in cols:
                found = [(False, scores[f, row, c])]
                if up or down:
                    above = scores[f, row - 1, c] if up else NEG
                    found.append((True, jnp.where(self.upper, above, scores[f, row + 1, c] if down else NEG)))
                for off_row, block in found:
                    if c - col == 2:
                        block = jnp.where(self.left, NEG, block)
                    elif c - col == -2:
                        block = jnp.where(self.left, block, NEG)
                    blocks.append((f, off_row, c, block))
        top = blocks[0][3]
        for entry in blocks[1:]:
            top = jnp.maximum(top, entry[3])
        return row, up and down, down, blocks, jnp.max(top, axis=1, keepdims=True)

    def weigh(self, row, both, down, blocks, top):
        parts = []
        for f, off_row, c, block in blocks:
            weights = jnp.exp2((block - top) * self.scale).astype(jnp.bfloat16)
            if off_row and both:
                parts.append((f, row - 1, c, weights * self.upper_one))
                parts.append((f, row + 1, c, weights * (1 - self.upper_one)))
            elif off_row:
                parts.append((f, row + 1 if down else row - 1, c, weights))
            else:
                parts.append((f, row, c, weights))
        values = jnp.concatenate([self.tile(2 * f + 1, r, c) for f, r, c, _ in parts], axis=0)
        values = jnp.concatenate([values, jnp.ones_like(values)], axis=1)
        weights = jnp.concatenate([part for _, _, _, part in parts], axis=1)
        total = jnp.dot(weights, values, preferred_element_type=jnp.float32)
        return total[:, :HD] / total[:, HD:], top * self.scale + jnp.log2(total[:, HD:])

    def attend_all(self, first_col):
        places = [(row, col) for row in range(self.grid_rows) for col in range(self.grid_cols)]
        held = None
        for place in [*places, None]:
            ready = self.scores(place[0], first_col + place[1]) if place else None
            if held:
                yield (*held[0], *self.weigh(*held[1]))
            held = (place, ready)

    def enhanced(self, row, col, weight_ref, bias_ref, before_ref, after_ref):
        shape = (self.tile_cols, HD)
        sub = lax.broadcasted_iota(jnp.int32, shape, 0)
        taps = [[weight_ref[a, pl.ds(b, 1), :] for b in range(3)] for a in range(3)]
        last = self.tile_cols - 1
        member = self.pairs.shape[1] - 1
        lines = []
        for key_row in range(row * self.tile_rows - 1, (row + 1) * self.tile_rows + 1):
            tile_row, line = key_row // self.tile_rows, key_row % self.tile_rows
            if tile_row < 0 or tile_row >= self.grid_rows:
                lines.append(None)
                continue

            def values(c):
                return self.pairs[self.slot(tile_row, c), member, line].astype(jnp.float32)

            def edge(ref, c):
                packed = ref[self.slot(tile_row, c), self.tile_rows + line // self.tile_cols].astype(jnp.float32)
                return jnp.broadcast_to(packed[line % self.tile_cols : line % self.tile_cols + 1], shape)

            here = values(col)
            before = pltpu.roll(values(col - 1), 1, 0) if col > 0 else edge(before_ref, self.grid_cols - 1)
            after = pltpu.roll(values(col + 1), last, 0) if col + 1 < self.grid_cols else edge(after_ref, 0)
            low = jnp.where(sub == 0, before, pltpu.roll(here, 1, 0))
            high = jnp.where(sub == last, after, pltpu.roll(here, last, 0))
            lines.append((low, here, high))
        sums = []
        for line in range(self.tile_rows):
            total = jnp.broadcast_to(bias_ref[...], shape)
            for a in range(3):
                if lines[line + a] is not None:
                    for b in range(3):
                        total = total + lines[line + a][b] * taps[a][b]
            sums.append(total)
        return jnp.stack(sums, axis=0)


def visit_kernel(grid, tile, first_col, info_ref, query_ref, pairs_ref, out_ref):
    window = Window(grid, tile, info_ref, query_ref, pairs_ref)
    size, count = window.size, grid[0] * grid[1]
    lane = lax.broadcasted_iota(jnp.int32, (size, HD), 1)
    levels = jnp.zeros((size, HD), jnp.float32)
    for row, col, part, level in window.attend_all(first_col):
        index = row * grid[1] + col
        out_ref[index] = part.reshape(tile + (HD,)).astype(jnp.bfloat16)
        levels = jnp.where(lane == index, level, levels)
    high = levels.astype(jnp.bfloat16).astype(jnp.float32)
    middle = (levels - high).astype(jnp.bfloat16).astype(jnp.float32)
    packed = high + pltpu.roll(middle, count, 1) + pltpu.roll(levels - high - middle, 2 * count, 1)
    out_ref[count] = packed.reshape(tile + (HD,)).astype(jnp.bfloat16)


def own_kernel(
    grid, tile, info_ref, weight_ref, bias_ref, query_ref, pairs_ref, before_ref, after_ref, part_ref, level_ref, conv_ref
):
    window = Window(grid, tile, info_ref, query_ref, pairs_ref)
    for row, col, part, level in window.attend_all(0):
        index = row * grid[1] + col
        part_ref[index], level_ref[index] = part, level
        conv = window.enhanced(row, col, weight_ref, bias_ref, before_ref, after_ref)
        conv_ref[index] = conv.reshape(window.size, HD)


def join_kernel(grid, tile, info_ref, part_ref, level_ref, conv_ref, left_ref, right_ref, out_ref):
    size, count = tile[0] * tile[1], grid[0] * grid[1]
    visits = (left_ref, right_ref)
    packed = []
    for i, ref in enumerate(visits):
        pack = ref[count].reshape(size, HD).astype(jnp.float32)
        level = pack + pltpu.roll(pack, HD - count, 1) + pltpu.roll(pack, HD - 2 * count, 1)
        packed.append(jnp.where(info_ref[i] > 0, level, NEG))
    for index in range(count):
        levels = [level_ref[index]]
        parts = [part_ref[index]]
        for ref, pack in zip(visits, packed):
            parts.append(ref[index].reshape(size, HD).astype(jnp.float32))
            levels.append(jnp.broadcast_to(pack[:, index : index + 1], (size, HD)))
        top = jnp.maximum(jnp.maximum(levels[0], levels[1]), levels[2])
        shares = [jnp.exp2(level - top) for level in levels]
        mixed = sum(share * part for share, part in zip(shares, parts)) / sum(shares)
        out_ref[info_ref[2 + index]] = (mixed + conv_ref[index]).reshape(tile + (HD,)).astype(jnp.bfloat16)


def lanes(head):
    return pl.ds(pl.multiple_of(head * HD, HD), HD)


def pack_kernel(flips, side, me_ref, *refs):
    count = len(flips)
    sources = refs[: -2 * count - 2]
    query_buffers, pair_buffers = refs[-2 * count - 2 : -count - 2], refs[-count - 2 : -2]
    held_ref, sems = refs[-2], refs[-1]
    tile_rows, tile_cols, _ = sources[0].shape
    copies = [pltpu.make_async_copy(x, held_ref.at[i], sems.at[i]) for i, x in enumerate(sources)]
    for copy in copies:
        copy.start()
    heads = [[lanes(me_ref[0] ^ (flip ^ beside)) for beside in (0, side)] for flip in flips]
    copies[0].wait()
    for buffer, pair in zip(query_buffers, heads):
        for other in range(2):
            buffer[other, pl.ds(0, tile_rows)] = held_ref[0, :, :, pair[other]]
    copies[1].wait()
    sub = lax.broadcasted_iota(jnp.int32, (tile_cols, HD), 0)
    for buffer, pair in zip(query_buffers, heads):
        for other in range(2):
            for start in range(0, tile_rows, tile_cols):
                packed = jnp.zeros((tile_cols, HD), jnp.float32)
                for line in range(tile_cols):
                    values = held_ref[1, start + line, :, pair[other]].astype(jnp.float32)
                    edge = jnp.where(me_ref[1] == 0, values[:1], values[tile_cols - 1 :])
                    packed = jnp.where(sub == line, edge, packed)
                buffer[other, tile_rows + start // tile_cols] = packed.astype(jnp.bfloat16)
    for member, source in enumerate((*range(2, len(sources)), 1)):
        if member < len(sources) - 2:
            copies[source].wait()
        for buffer, pair in zip(pair_buffers, heads):
            for other in range(2):
                buffer[other, member] = held_ref[source, :, :, pair[other]]


def unpack_kernel(flips, side, me_ref, same_ref, beside_ref, *refs):
    out_ref = refs[-1]
    out_ref[:, :, lanes(me_ref[0])] = same_ref[0]
    out_ref[:, :, lanes(me_ref[0] ^ side)] = beside_ref[0]
    for i, flip in enumerate(flips[1:]):
        out_ref[:, :, lanes(me_ref[0] ^ flip)] = refs[i][0]
        out_ref[:, :, lanes(me_ref[0] ^ (flip ^ side))] = refs[i][1]


def head_step(shape, queries, keys_new, values_new, keys_cache, values_cache, conv_weight, conv_bias):
    group_rows, group_cols, far = shape
    tile_rows, tile_cols, channels = queries.shape
    heads = channels // HD
    grid, tile = (group_rows, group_cols), (tile_rows, tile_cols)
    size = tile_rows * tile_cols
    axes = ("ht", "near")
    block = (tile_rows, tile_cols, HD)
    side = group_cols
    flips = [flip for flip in range(heads) if not flip & side]
    near = lax.axis_index("near").astype(jnp.int32)
    me = lax.axis_index("ht").astype(jnp.int32) * group_cols + near
    me_ref = jnp.stack([me, near])

    def swap(x, flip):
        return lax.ppermute(x, axes, [(s, s ^ flip) for s in range(heads)])

    def call(kernel, out_shape, params, cost, *operands, space=(VMEM, VMEM), scratch=()):
        return pl.pallas_call(
            kernel,
            out_shape=out_shape,
            in_specs=[SMEM] + [space[0]] * (len(operands) - 1),
            out_specs=jax.tree.map(lambda _: space[1], out_shape),
            scratch_shapes=scratch,
            compiler_params=params,
            cost_estimate=pl.CostEstimate(flops=cost << 30, bytes_accessed=1 << 20, transcendentals=0),
        )(*operands)

    def stay(x):
        return pltpu.with_memory_space_constraint(x, pltpu.HBM)

    def gather(buffers):
        got = [buffers[0]] + [swap(b, flip) for b, flip in zip(buffers[1:], flips[1:])]
        forward = jnp.stack([b[1] for b in got])
        beside = swap(forward, side)
        return jnp.concatenate([jnp.stack([b[0] for b in got]), beside], axis=0)

    up = [(i, i + 1) for i in range(far - 1)]
    down = [(i + 1, i) for i in range(far - 1)]
    edges = -(-tile_rows // tile_cols)
    sources = (queries, values_new, keys_cache[0], values_cache[0], keys_new)
    query_buffer = jax.ShapeDtypeStruct((2, tile_rows + edges, tile_cols, HD), jnp.bfloat16)
    pair_buffer = jax.ShapeDtypeStruct((2, len(sources) - 1) + block, jnp.bfloat16)
    packed = call(
        functools.partial(pack_kernel, flips, side),
        [query_buffer] * len(flips) + [pair_buffer] * len(flips),
        SMALL,
        0,
        me_ref,
        *map(stay, sources),
        space=(FAR, VMEM),
        scratch=[pltpu.VMEM((len(sources),) + queries.shape, jnp.bfloat16), pltpu.SemaphoreType.DMA((len(sources),))],
    )
    query = gather(packed[: len(flips)])
    pairs = gather(packed[len(flips) :])
    query_left = lax.ppermute(query, "far", up)
    query_right = lax.ppermute(query, "far", down)
    far_index = lax.axis_index("far")
    flip = me ^ jnp.arange(heads, dtype=jnp.int32)
    beside = (flip // side) % 2
    order = flip % side + flip // (2 * side) * side
    info = jnp.concatenate(
        [
            jnp.stack([far_index > 0, far_index < far - 1]).astype(jnp.int32),
            beside * len(flips) + order,
        ]
    )
    weight = lax.dynamic_slice_in_dim(conv_weight, me * HD, HD, 2)
    bias = lax.dynamic_slice_in_dim(conv_bias.reshape(1, channels), me * HD, HD, 1)

    def visit(queries, first_col):
        kernel = functools.partial(visit_kernel, grid, tile, first_col)
        return call(kernel, jax.ShapeDtypeStruct((heads + 1,) + block, jnp.bfloat16), LIMIT, 4, info, queries, pairs)

    left_part = visit(query_left, -group_cols)
    from_right = lax.ppermute(left_part, "far", down)
    right_part = visit(query_right, group_cols)
    from_left = lax.ppermute(right_part, "far", up)
    part = jax.ShapeDtypeStruct((heads, size, HD), jnp.float32)
    kernel = functools.partial(own_kernel, grid, tile)
    own = call(kernel, [part] * 3, LIMIT, 4, info, weight, bias, query, pairs, query_left, query_right)
    kernel = functools.partial(join_kernel, grid, tile)
    result = jax.ShapeDtypeStruct((heads,) + block, jnp.bfloat16)
    result = call(kernel, result, LIMIT, 1, info, *own, from_left, from_right)
    same, other = result[: len(flips)], result[len(flips) :]
    received = swap(other, side)
    got = []
    for i in range(1, len(flips)):
        got.append(swap(jnp.stack([same[i], received[i]]), flips[i]))
    return call(
        functools.partial(unpack_kernel, flips, side),
        jax.ShapeDtypeStruct(queries.shape, jnp.bfloat16),
        SMALL,
        0,
        me_ref,
        same,
        received,
        *got,
    )


def grouping(mesh, heads):
    rows, cols = mesh.shape["ht"], mesh.shape["wt"]
    group_rows = rows
    group_cols = heads // group_rows if heads % group_rows == 0 else 0
    if group_cols != 2 or cols % group_cols:
        return None
    return group_rows, group_cols, cols // group_cols


def solution(mesh):
    def program(queries, *rest):
        heads = queries.shape[2] // HD
        shape = grouping(mesh, heads)
        if shape is None or queries.shape[0] != mesh.shape["ht"] * (WIN // 2) or queries.shape[1] != mesh.shape["wt"] * (WIN // 4):
            placed = (P("ht", "wt", None),) * 3 + (P(None, "ht", "wt", None),) * 2 + (P(), P())
            return jax.shard_map(
                shards, mesh=mesh, in_specs=placed, out_specs=P("ht", "wt", None), check_vma=False
            )(queries, *rest)
        devices = mesh.devices.reshape(shape[0], shape[2], shape[1])
        split = Mesh(devices, ("ht", "far", "near"))
        tile = P("ht", ("far", "near"), None)
        past = P(None, "ht", ("far", "near"), None)
        step = jax.shard_map(
            functools.partial(head_step, shape),
            mesh=split,
            in_specs=(tile, tile, tile, past, past, P(), P()),
            out_specs=tile,
            check_vma=False,
        )
        return step(queries, *rest)

    return program
```

```python
import functools

import jax
import jax.numpy as jnp
from jax import lax
from jax.experimental import pallas as pl
from jax.experimental.pallas import tpu as pltpu
from jax.sharding import Mesh, PartitionSpec as P


HD = 128
WIN = 32


def with_halo(block, sides, width):
    for axis, dim in sides:
        count = lax.axis_size(axis)
        forward = [(i, i + 1) for i in range(count - 1)]
        backward = [(target, source) for source, target in forward]
        low = lax.ppermute(
            lax.slice_in_dim(block, block.shape[dim] - width, None, axis=dim), axis, forward
        )
        high = lax.ppermute(lax.slice_in_dim(block, 0, width, axis=dim), axis, backward)
        block = jnp.concatenate([low, block, high], axis=dim)
    return block


def window_allowed(row_start, col_start, frame_rows, frame_cols, tile_rows, tile_cols, half_win):
    ext_rows = jnp.arange(tile_rows + 2 * half_win, dtype=jnp.int32) - half_win
    ext_cols = jnp.arange(tile_cols + 2 * half_win, dtype=jnp.int32) - half_win
    query_rows = jnp.arange(tile_rows, dtype=jnp.int32)
    query_cols = jnp.arange(tile_cols, dtype=jnp.int32)
    row_delta = ext_rows[None, :] - query_rows[:, None]
    col_delta = ext_cols[None, :] - query_cols[:, None]
    global_rows = row_start + ext_rows
    global_cols = col_start + ext_cols
    row_valid = (
        (row_delta >= -half_win)
        & (row_delta < half_win)
        & ((global_rows >= 0) & (global_rows < frame_rows))[None, :]
    )
    col_valid = (
        (col_delta >= -half_win)
        & (col_delta < half_win)
        & ((global_cols >= 0) & (global_cols < frame_cols))[None, :]
    )
    allowed = row_valid[:, None, :, None] & col_valid[None, :, None, :]
    return allowed.reshape(
        tile_rows * tile_cols, (tile_rows + 2 * half_win) * (tile_cols + 2 * half_win)
    )


def attend(query_rows, keys_flat, values_flat, allowed, heads, head_dim):
    score_scale = head_dim ** (-0.5)

    def one_head(head_index):
        scores = (
            jnp.einsum("qd,kd->qk", query_rows, keys_flat, preferred_element_type=jnp.float32)
            * score_scale
        )
        scores = jnp.where(allowed, scores, -1e30)
        row_top = jnp.max(scores, axis=1, keepdims=True)
        weights_f = jnp.exp(scores - row_top)
        denominator = jnp.sum(weights_f, axis=1, keepdims=True)
        numerator = jnp.dot(
            weights_f.astype(jnp.bfloat16), values_flat, preferred_element_type=jnp.float32
        )
        return numerator / denominator

    outputs = lax.map(one_head, jnp.arange(heads, dtype=jnp.int32))
    return outputs.transpose(1, 0, 2).reshape(query_rows.shape[0], heads * head_dim)


def local_conv(padded, conv_weight, conv_bias, tile_rows, tile_cols):
    enhanced = jnp.zeros((tile_rows, tile_cols, padded.shape[2]), jnp.float32) + conv_bias
    for row_shift in range(3):
        for col_shift in range(3):
            enhanced = (
                enhanced
                + padded[
                    row_shift : row_shift + tile_rows, col_shift : col_shift + tile_cols
                ].astype(jnp.float32)
                * conv_weight[row_shift, col_shift]
            )
    return enhanced


def cycle_conv(values_new, conv_weight, conv_bias):
    tile_rows, tile_cols, _ = values_new.shape
    padded = with_halo(values_new, (("ht", 0), ("wt", 1)), 1)
    return local_conv(padded, conv_weight, conv_bias, tile_rows, tile_cols)


def shards(queries, keys_new, values_new, keys_cache, values_cache, conv_weight, conv_bias):
    tile_rows, tile_cols, channels = queries.shape
    frames = keys_cache.shape[0] + 1
    half_win = WIN // 2
    stacked = jnp.concatenate([keys_cache, keys_new[None], values_cache, values_new[None]], axis=0)
    row_start = lax.axis_index("ht") * tile_rows
    frame_rows = tile_rows * lax.axis_size("ht")
    frame_cols = tile_cols * lax.axis_size("wt")
    heads = channels // HD
    copies = lax.axis_size("wt") // heads
    bundle = jnp.concatenate([stacked, queries[None]], axis=0)
    members = bundle.shape[0]
    spread = bundle.reshape(members, tile_rows, tile_cols, 1, heads, HD)
    spread = jnp.broadcast_to(spread, (members, tile_rows, tile_cols, copies, heads, HD))
    spread = spread.reshape(members, tile_rows, tile_cols, copies * heads, HD)
    strips = lax.all_to_all(spread, "wt", split_axis=3, concat_axis=2, tiled=True)
    strips = strips.reshape(members, tile_rows, frame_cols, HD)
    device_index = lax.axis_index("wt")
    my_group = device_index // heads
    block_width = tile_cols * heads
    block_start = my_group * block_width
    padded_cols = jnp.pad(strips, ((0, 0), (0, 0), (half_win, half_win), (0, 0)))
    window = lax.dynamic_slice_in_dim(padded_cols, block_start, block_width + 2 * half_win, 2)
    query_part = window[2 * frames, :, half_win : half_win + block_width]
    region = with_halo(window[: 2 * frames], (("ht", 1),), half_win)

    def one_block(step):
        offset = step * tile_cols
        query_block = lax.dynamic_slice_in_dim(query_part, offset, tile_cols, 1).reshape(
            tile_rows * tile_cols, HD
        )
        sub = lax.dynamic_slice_in_dim(region, offset, tile_cols + 2 * half_win, 2)
        keys_flat = sub[:frames].reshape(-1, HD)
        values_flat = sub[frames:].reshape(-1, HD)
        allowed = window_allowed(
            row_start, block_start + offset, frame_rows, frame_cols, tile_rows, tile_cols, half_win
        )
        allowed = jnp.tile(allowed, (1, frames))
        result = attend(query_block, keys_flat, values_flat, allowed, 1, HD)
        return result.reshape(tile_rows, tile_cols, HD)

    blocks = lax.map(one_block, jnp.arange(heads, dtype=jnp.int32))
    payload = blocks.transpose(1, 0, 2, 3)
    payload = jnp.broadcast_to(payload[:, None], (tile_rows, copies, heads, tile_cols, HD))
    payload = payload.reshape(tile_rows, copies * heads, tile_cols, HD)
    returned = lax.all_to_all(
        payload.astype(jnp.bfloat16), "wt", split_axis=1, concat_axis=1, tiled=True
    ).astype(payload.dtype)
    own = lax.dynamic_slice_in_dim(returned, my_group * heads, heads, 1)
    combined = own.transpose(0, 2, 1, 3).reshape(tile_rows, tile_cols, channels)
    combined = combined + cycle_conv(values_new, conv_weight, conv_bias)
    return combined.astype(jnp.bfloat16)


LOG2E = 1.4426950408889634
NEG = -1e30
VMEM = pl.BlockSpec(memory_space=pltpu.VMEM)
SMEM = pl.BlockSpec(memory_space=pltpu.SMEM)
FAR = pl.BlockSpec(memory_space=pltpu.HBM)
LIMIT = pltpu.CompilerParams(vmem_limit_bytes=8 * 1024 * 1024)
SMALL = pltpu.CompilerParams(vmem_limit_bytes=4 * 1024 * 1024)


class Window:
    def __init__(self, grid, tile, info_ref, query_ref, pairs_ref):
        self.grid_rows, self.grid_cols = grid
        self.tile_rows, self.tile_cols = tile
        self.size = self.tile_rows * self.tile_cols
        self.info, self.query, self.pairs = info_ref, query_ref, pairs_ref
        self.scale = HD ** (-0.5) * LOG2E
        query = lax.broadcasted_iota(jnp.int32, (self.size, self.size), 0)
        key = lax.broadcasted_iota(jnp.int32, (self.size, self.size), 1)
        self.upper = key // self.tile_cols >= query // self.tile_cols
        self.left = key % self.tile_cols >= query % self.tile_cols
        self.upper_one = self.upper.astype(jnp.float32).astype(jnp.bfloat16)

    def slot(self, row, col):
        return self.info[3 + row * self.grid_cols + col]

    def tile(self, member, row, col):
        return self.pairs[self.slot(row, col), member].reshape(self.size, HD)

    def scores(self, row, col, cols):
        query = self.query[self.slot(row, col), pl.ds(0, self.tile_rows)].reshape(self.size, HD)
        frames = range(self.pairs.shape[1] // 2)
        up, down = row > 0, row + 1 < self.grid_rows
        rows = [r for r in (row - 1, row, row + 1) if 0 <= r < self.grid_rows]
        needed = [(f, r, i) for f in frames for i in range(len(cols)) for r in rows]
        keys = jnp.concatenate([self.tile(2 * f, r, cols[i][0]) for f, r, i in needed], axis=0)
        raw = lax.dot_general(query, keys, (((1,), (1,)), ((), ())), preferred_element_type=jnp.float32)
        scores = {key: raw[:, i * self.size : (i + 1) * self.size] for i, key in enumerate(needed)}
        blocks = []
        for f in frames:
            for i, (c, allowed) in enumerate(cols):
                found = [(False, scores[f, row, i])]
                if up or down:
                    above = scores[f, row - 1, i] if up else NEG
                    found.append((True, jnp.where(self.upper, above, scores[f, row + 1, i] if down else NEG)))
                for off_row, block in found:
                    if allowed is not None:
                        block = jnp.where(allowed, block, NEG)
                    blocks.append((f, off_row, c, block))
        top = blocks[0][3]
        for entry in blocks[1:]:
            top = jnp.maximum(top, entry[3])
        return row, up and down, down, blocks, jnp.max(top, axis=1, keepdims=True)

    def weigh(self, row, both, down, blocks, top):
        parts = []
        for f, off_row, c, block in blocks:
            weights = jnp.exp2((block - top) * self.scale).astype(jnp.bfloat16)
            if off_row and both:
                parts.append((f, row - 1, c, weights * self.upper_one))
                parts.append((f, row + 1, c, weights * (1 - self.upper_one)))
            elif off_row:
                parts.append((f, row + 1 if down else row - 1, c, weights))
            else:
                parts.append((f, row, c, weights))
        values = jnp.concatenate([self.tile(2 * f + 1, r, c) for f, r, c, _ in parts], axis=0)
        values = jnp.concatenate([values, jnp.ones_like(values)], axis=1)
        weights = jnp.concatenate([part for _, _, _, part in parts], axis=1)
        total = jnp.dot(weights, values, preferred_element_type=jnp.float32)
        return total[:, :HD] / total[:, HD:], top * self.scale + jnp.log2(total[:, HD:])

    def attend(self, tiles):
        held = None
        for place in [*tiles, None]:
            ready = self.scores(*place) if place else None
            if held:
                yield (held[0][0] * self.grid_cols + held[0][1], *self.weigh(*held[1]))
            held = (place, ready)

    def enhanced(self, row, col, weight_ref, bias_ref, beyond):
        shape = (self.tile_cols, HD)
        sub = lax.broadcasted_iota(jnp.int32, shape, 0)
        taps = [[weight_ref[a, pl.ds(b, 1), :] for b in range(3)] for a in range(3)]
        last = self.tile_cols - 1
        member = self.pairs.shape[1] - 1
        lines = []
        for key_row in range(row * self.tile_rows - 1, (row + 1) * self.tile_rows + 1):
            tile_row, line = key_row // self.tile_rows, key_row % self.tile_rows
            if tile_row < 0 or tile_row >= self.grid_rows:
                lines.append(None)
                continue

            def values(c):
                return self.pairs[self.slot(tile_row, c), member, line].astype(jnp.float32)

            def edge(right, c):
                place = self.slot(tile_row, c), self.tile_rows + line // self.tile_cols
                first, second = (ref[place].astype(jnp.float32) for ref in beyond)
                packed = jnp.where(self.info[2] == right, first, second)
                return jnp.broadcast_to(packed[line % self.tile_cols : line % self.tile_cols + 1], shape)

            here = values(col)
            before = pltpu.roll(values(col - 1), 1, 0) if col > 0 else edge(0, self.grid_cols - 1)
            after = pltpu.roll(values(col + 1), last, 0) if col + 1 < self.grid_cols else edge(1, 0)
            low = jnp.where(sub == 0, before, pltpu.roll(here, 1, 0))
            high = jnp.where(sub == last, after, pltpu.roll(here, last, 0))
            lines.append((low, here, high))
        sums = []
        for line in range(self.tile_rows):
            total = jnp.broadcast_to(bias_ref[...], shape)
            for a in range(3):
                if lines[line + a] is not None:
                    for b in range(3):
                        total = total + lines[line + a][b] * taps[a][b]
            sums.append(total)
        return jnp.stack(sums, axis=0)


def visit_kernel(grid, tile, first, info_ref, query_ref, pairs_ref, out_ref):
    window = Window(grid, tile, info_ref, query_ref, pairs_ref)
    near = info_ref[2] if first else 1 - info_ref[2]
    allowed = window.left.astype(jnp.int32) == near
    tiles = []
    for row in range(grid[0]):
        tiles.append((row, 1 - near, [(near, None), (1 - near, allowed)]))
        tiles.append((row, near, [(near, allowed)]))
    size, count = window.size, grid[0] * grid[1]
    lane = lax.broadcasted_iota(jnp.int32, (size, HD), 1)
    levels = jnp.zeros((size, HD), jnp.float32)
    for index, part, level in window.attend(tiles):
        out_ref[index] = part.reshape(tile + (HD,)).astype(jnp.bfloat16)
        levels = jnp.where(lane == index, level, levels)
    high = levels.astype(jnp.bfloat16).astype(jnp.float32)
    middle = (levels - high).astype(jnp.bfloat16).astype(jnp.float32)
    packed = high + pltpu.roll(middle, count, 1) + pltpu.roll(levels - high - middle, 2 * count, 1)
    out_ref[count] = packed.reshape(tile + (HD,)).astype(jnp.bfloat16)


def own_kernel(
    grid, tile, info_ref, weight_ref, bias_ref, query_ref, pairs_ref, first_ref, second_ref, part_ref, level_ref, conv_ref
):
    window = Window(grid, tile, info_ref, query_ref, pairs_ref)
    cols = [(c, None) for c in range(grid[1])]
    tiles = [(row, col, cols) for row in range(grid[0]) for col in range(grid[1])]
    for index, part, level in window.attend(tiles):
        part_ref[index], level_ref[index] = part, level
        row, col = index // grid[1], index % grid[1]
        conv = window.enhanced(row, col, weight_ref, bias_ref, (first_ref, second_ref))
        conv_ref[index] = conv.reshape(window.size, HD)


def join_kernel(grid, tile, info_ref, part_ref, level_ref, conv_ref, first_ref, second_ref, out_ref):
    size, count = tile[0] * tile[1], grid[0] * grid[1]
    visits = (first_ref, second_ref)
    packed = []
    for i, ref in enumerate(visits):
        pack = ref[count].reshape(size, HD).astype(jnp.float32)
        level = pack + pltpu.roll(pack, HD - count, 1) + pltpu.roll(pack, HD - 2 * count, 1)
        packed.append(jnp.where(info_ref[i] > 0, level, NEG))
    for index in range(count):
        levels = [level_ref[index]]
        parts = [part_ref[index]]
        for ref, pack in zip(visits, packed):
            parts.append(ref[index].reshape(size, HD).astype(jnp.float32))
            levels.append(jnp.broadcast_to(pack[:, index : index + 1], (size, HD)))
        top = jnp.maximum(jnp.maximum(levels[0], levels[1]), levels[2])
        shares = [jnp.exp2(level - top) for level in levels]
        mixed = sum(share * part for share, part in zip(shares, parts)) / sum(shares)
        out_ref[info_ref[3 + index]] = (mixed + conv_ref[index]).reshape(tile + (HD,)).astype(jnp.bfloat16)


def lanes(head):
    return pl.ds(pl.multiple_of(head * HD, HD), HD)


def fetch(sources, held_ref, sems):
    copies = [pltpu.make_async_copy(x, held_ref.at[i], sems.at[i]) for i, x in enumerate(sources)]
    for copy in copies:
        copy.start()
    return copies


def pack_kernel(flips, side, me_ref, *refs):
    count = len(flips)
    sources, buffers, held_ref, sems = refs[: -count - 2], refs[-count - 2 : -2], refs[-2], refs[-1]
    for member, copy in enumerate(fetch(sources, held_ref, sems)):
        copy.wait()
        for buffer, flip in zip(buffers, flips):
            for other in range(2):
                head = lanes(me_ref[0] ^ (flip ^ (side if other else 0)))
                buffer[other, member] = held_ref[member, :, :, head]


def query_kernel(flips, side, me_ref, query_ref, values_ref, *refs):
    buffers, held_ref, sems = refs[:-2], refs[-2], refs[-1]
    tile_rows, tile_cols, _ = query_ref.shape
    copies = fetch((query_ref, values_ref), held_ref, sems)
    places = [
        (buffer, other, lanes(me_ref[0] ^ (flip ^ (side if other else 0))))
        for buffer, flip in zip(buffers, flips)
        for other in range(2)
    ]
    copies[0].wait()
    for buffer, other, head in places:
        buffer[other, pl.ds(0, tile_rows)] = held_ref[0, :, :, head]
    copies[1].wait()
    sub = lax.broadcasted_iota(jnp.int32, (tile_cols, HD), 0)
    for buffer, other, head in places:
        for start in range(0, tile_rows, tile_cols):
            packed = jnp.zeros((tile_cols, HD), jnp.float32)
            for line in range(tile_cols):
                values = held_ref[1, start + line, :, head].astype(jnp.float32)
                edge = jnp.where(me_ref[1] == 0, values[:1], values[tile_cols - 1 :])
                packed = jnp.where(sub == line, edge, packed)
            buffer[other, tile_rows + start // tile_cols] = packed.astype(jnp.bfloat16)


def unpack_kernel(flips, side, me_ref, same_ref, beside_ref, *refs):
    out_ref = refs[-1]
    out_ref[:, :, lanes(me_ref[0])] = same_ref[0]
    out_ref[:, :, lanes(me_ref[0] ^ side)] = beside_ref[0]
    for i, flip in enumerate(flips[1:]):
        out_ref[:, :, lanes(me_ref[0] ^ flip)] = refs[i][0]
        out_ref[:, :, lanes(me_ref[0] ^ (flip ^ side))] = refs[i][1]


def head_step(shape, queries, keys_new, values_new, keys_cache, values_cache, conv_weight, conv_bias):
    group_rows, group_cols, far = shape
    tile_rows, tile_cols, channels = queries.shape
    heads = channels // HD
    grid, tile = (group_rows, group_cols), (tile_rows, tile_cols)
    size = tile_rows * tile_cols
    axes = ("ht", "near")
    block = (tile_rows, tile_cols, HD)
    side = group_cols
    flips = [flip for flip in range(heads) if not flip & side]
    near = lax.axis_index("near").astype(jnp.int32)
    me = lax.axis_index("ht").astype(jnp.int32) * group_cols + near
    me_ref = jnp.stack([me, near])

    def swap(x, flip):
        return lax.ppermute(x, axes, [(s, s ^ flip) for s in range(heads)])

    def call(kernel, out_shape, params, cost, *operands, space=(VMEM, VMEM), scratch=()):
        return pl.pallas_call(
            kernel,
            out_shape=out_shape,
            in_specs=[SMEM] + [space[0]] * (len(operands) - 1),
            out_specs=jax.tree.map(lambda _: space[1], out_shape),
            scratch_shapes=scratch,
            compiler_params=params,
            cost_estimate=pl.CostEstimate(flops=cost << 30, bytes_accessed=1 << 20, transcendentals=0),
        )(*operands)

    def stay(x):
        return pltpu.with_memory_space_constraint(x, pltpu.HBM)

    def gather(buffers):
        got = [buffers[0]] + [swap(b, flip) for b, flip in zip(buffers[1:], flips[1:])]
        forward = jnp.stack([b[1] for b in got])
        beside = swap(forward, side)
        return jnp.concatenate([jnp.stack([b[0] for b in got]), beside], axis=0)

    def rounds(start):
        return [pair for i in range(start, far - 1, 2) for pair in ((i, i + 1), (i + 1, i))]

    first, second = rounds(0), rounds(1)
    edges = -(-tile_rows // tile_cols)

    def pack(kernel, buffer, *sources):
        return call(
            functools.partial(kernel, flips, side),
            [jax.ShapeDtypeStruct(buffer, jnp.bfloat16)] * len(flips),
            SMALL,
            0,
            me_ref,
            *map(stay, sources),
            space=(FAR, VMEM),
            scratch=[
                pltpu.VMEM((len(sources),) + queries.shape, jnp.bfloat16),
                pltpu.SemaphoreType.DMA((len(sources),)),
            ],
        )

    packed = pack(query_kernel, (2, tile_rows + edges, tile_cols, HD), queries, values_new)
    query = gather(packed)
    packed = pack(pack_kernel, (2, 4) + block, keys_cache[0], values_cache[0], keys_new, values_new)
    pairs = gather(packed)
    query_second = lax.ppermute(query, "far", second)
    query_first = lax.ppermute(query, "far", first)
    far_index = lax.axis_index("far")
    flip = me ^ jnp.arange(heads, dtype=jnp.int32)
    beside = (flip // side) % 2
    order = flip % side + flip // (2 * side) * side
    even = far_index % 2 == 0
    below, above = far_index > 0, far_index < far - 1
    info = jnp.concatenate(
        [
            jnp.stack([~even | above, jnp.where(even, below, above), even]).astype(jnp.int32),
            beside * len(flips) + order,
        ]
    )
    weight = lax.dynamic_slice_in_dim(conv_weight, me * HD, HD, 2)
    bias = lax.dynamic_slice_in_dim(conv_bias.reshape(1, channels), me * HD, HD, 1)

    def visit(queries, is_first):
        kernel = functools.partial(visit_kernel, grid, tile, is_first)
        return call(kernel, jax.ShapeDtypeStruct((heads + 1,) + block, jnp.bfloat16), LIMIT, 4, info, queries, pairs)

    part = visit(query_second, False)
    home_second = lax.ppermute(part, "far", second)
    part = visit(query_first, True)
    home_first = lax.ppermute(part, "far", first)
    part = jax.ShapeDtypeStruct((heads, size, HD), jnp.float32)
    kernel = functools.partial(own_kernel, grid, tile)
    own = call(kernel, [part] * 3, LIMIT, 4, info, weight, bias, query, pairs, query_first, query_second)
    kernel = functools.partial(join_kernel, grid, tile)
    result = jax.ShapeDtypeStruct((heads,) + block, jnp.bfloat16)
    result = call(kernel, result, LIMIT, 1, info, *own, home_first, home_second)
    same, other = result[: len(flips)], result[len(flips) :]
    received = swap(other, side)
    got = []
    for i in range(1, len(flips)):
        got.append(swap(jnp.stack([same[i], received[i]]), flips[i]))
    return call(
        functools.partial(unpack_kernel, flips, side),
        jax.ShapeDtypeStruct(queries.shape, jnp.bfloat16),
        SMALL,
        0,
        me_ref,
        same,
        received,
        *got,
    )


def grouping(mesh, heads):
    rows, cols = mesh.shape["ht"], mesh.shape["wt"]
    group_rows = rows
    group_cols = heads // group_rows if heads % group_rows == 0 else 0
    if group_cols != 2 or cols % group_cols:
        return None
    return group_rows, group_cols, cols // group_cols


def solution(mesh):
    def program(queries, *rest):
        heads = queries.shape[2] // HD
        shape = grouping(mesh, heads)
        if shape is None or queries.shape[0] != mesh.shape["ht"] * (WIN // 2) or queries.shape[1] != mesh.shape["wt"] * (WIN // 4):
            placed = (P("ht", "wt", None),) * 3 + (P(None, "ht", "wt", None),) * 2 + (P(), P())
            return jax.shard_map(
                shards, mesh=mesh, in_specs=placed, out_specs=P("ht", "wt", None), check_vma=False
            )(queries, *rest)
        devices = mesh.devices.reshape(shape[0], shape[2], shape[1])
        split = Mesh(devices, ("ht", "far", "near"))
        tile = P("ht", ("far", "near"), None)
        past = P(None, "ht", ("far", "near"), None)
        step = jax.shard_map(
            functools.partial(head_step, shape),
            mesh=split,
            in_specs=(tile, tile, tile, past, past, P(), P()),
            out_specs=tile,
            check_vma=False,
        )
        return step(queries, *rest)

    return program
```

```python
import functools

import jax
import jax.numpy as jnp
from jax import lax
from jax.experimental import pallas as pl
from jax.experimental.pallas import tpu as pltpu
from jax.sharding import Mesh, PartitionSpec as P


HD = 128
WIN = 32


def with_halo(block, sides, width):
    for axis, dim in sides:
        count = lax.axis_size(axis)
        forward = [(i, i + 1) for i in range(count - 1)]
        backward = [(target, source) for source, target in forward]
        low = lax.ppermute(
            lax.slice_in_dim(block, block.shape[dim] - width, None, axis=dim), axis, forward
        )
        high = lax.ppermute(lax.slice_in_dim(block, 0, width, axis=dim), axis, backward)
        block = jnp.concatenate([low, block, high], axis=dim)
    return block


def window_allowed(row_start, col_start, frame_rows, frame_cols, tile_rows, tile_cols, half_win):
    ext_rows = jnp.arange(tile_rows + 2 * half_win, dtype=jnp.int32) - half_win
    ext_cols = jnp.arange(tile_cols + 2 * half_win, dtype=jnp.int32) - half_win
    query_rows = jnp.arange(tile_rows, dtype=jnp.int32)
    query_cols = jnp.arange(tile_cols, dtype=jnp.int32)
    row_delta = ext_rows[None, :] - query_rows[:, None]
    col_delta = ext_cols[None, :] - query_cols[:, None]
    global_rows = row_start + ext_rows
    global_cols = col_start + ext_cols
    row_valid = (
        (row_delta >= -half_win)
        & (row_delta < half_win)
        & ((global_rows >= 0) & (global_rows < frame_rows))[None, :]
    )
    col_valid = (
        (col_delta >= -half_win)
        & (col_delta < half_win)
        & ((global_cols >= 0) & (global_cols < frame_cols))[None, :]
    )
    allowed = row_valid[:, None, :, None] & col_valid[None, :, None, :]
    return allowed.reshape(
        tile_rows * tile_cols, (tile_rows + 2 * half_win) * (tile_cols + 2 * half_win)
    )


def attend(query_rows, keys_flat, values_flat, allowed, heads, head_dim):
    score_scale = head_dim ** (-0.5)

    def one_head(head_index):
        scores = (
            jnp.einsum("qd,kd->qk", query_rows, keys_flat, preferred_element_type=jnp.float32)
            * score_scale
        )
        scores = jnp.where(allowed, scores, -1e30)
        row_top = jnp.max(scores, axis=1, keepdims=True)
        weights_f = jnp.exp(scores - row_top)
        denominator = jnp.sum(weights_f, axis=1, keepdims=True)
        numerator = jnp.dot(
            weights_f.astype(jnp.bfloat16), values_flat, preferred_element_type=jnp.float32
        )
        return numerator / denominator

    outputs = lax.map(one_head, jnp.arange(heads, dtype=jnp.int32))
    return outputs.transpose(1, 0, 2).reshape(query_rows.shape[0], heads * head_dim)


def local_conv(padded, conv_weight, conv_bias, tile_rows, tile_cols):
    enhanced = jnp.zeros((tile_rows, tile_cols, padded.shape[2]), jnp.float32) + conv_bias
    for row_shift in range(3):
        for col_shift in range(3):
            enhanced = (
                enhanced
                + padded[
                    row_shift : row_shift + tile_rows, col_shift : col_shift + tile_cols
                ].astype(jnp.float32)
                * conv_weight[row_shift, col_shift]
            )
    return enhanced


def cycle_conv(values_new, conv_weight, conv_bias):
    tile_rows, tile_cols, _ = values_new.shape
    padded = with_halo(values_new, (("ht", 0), ("wt", 1)), 1)
    return local_conv(padded, conv_weight, conv_bias, tile_rows, tile_cols)


def shards(queries, keys_new, values_new, keys_cache, values_cache, conv_weight, conv_bias):
    tile_rows, tile_cols, channels = queries.shape
    frames = keys_cache.shape[0] + 1
    half_win = WIN // 2
    stacked = jnp.concatenate([keys_cache, keys_new[None], values_cache, values_new[None]], axis=0)
    row_start = lax.axis_index("ht") * tile_rows
    frame_rows = tile_rows * lax.axis_size("ht")
    frame_cols = tile_cols * lax.axis_size("wt")
    heads = channels // HD
    copies = lax.axis_size("wt") // heads
    bundle = jnp.concatenate([stacked, queries[None]], axis=0)
    members = bundle.shape[0]
    spread = bundle.reshape(members, tile_rows, tile_cols, 1, heads, HD)
    spread = jnp.broadcast_to(spread, (members, tile_rows, tile_cols, copies, heads, HD))
    spread = spread.reshape(members, tile_rows, tile_cols, copies * heads, HD)
    strips = lax.all_to_all(spread, "wt", split_axis=3, concat_axis=2, tiled=True)
    strips = strips.reshape(members, tile_rows, frame_cols, HD)
    device_index = lax.axis_index("wt")
    my_group = device_index // heads
    block_width = tile_cols * heads
    block_start = my_group * block_width
    padded_cols = jnp.pad(strips, ((0, 0), (0, 0), (half_win, half_win), (0, 0)))
    window = lax.dynamic_slice_in_dim(padded_cols, block_start, block_width + 2 * half_win, 2)
    query_part = window[2 * frames, :, half_win : half_win + block_width]
    region = with_halo(window[: 2 * frames], (("ht", 1),), half_win)

    def one_block(step):
        offset = step * tile_cols
        query_block = lax.dynamic_slice_in_dim(query_part, offset, tile_cols, 1).reshape(
            tile_rows * tile_cols, HD
        )
        sub = lax.dynamic_slice_in_dim(region, offset, tile_cols + 2 * half_win, 2)
        keys_flat = sub[:frames].reshape(-1, HD)
        values_flat = sub[frames:].reshape(-1, HD)
        allowed = window_allowed(
            row_start, block_start + offset, frame_rows, frame_cols, tile_rows, tile_cols, half_win
        )
        allowed = jnp.tile(allowed, (1, frames))
        result = attend(query_block, keys_flat, values_flat, allowed, 1, HD)
        return result.reshape(tile_rows, tile_cols, HD)

    blocks = lax.map(one_block, jnp.arange(heads, dtype=jnp.int32))
    payload = blocks.transpose(1, 0, 2, 3)
    payload = jnp.broadcast_to(payload[:, None], (tile_rows, copies, heads, tile_cols, HD))
    payload = payload.reshape(tile_rows, copies * heads, tile_cols, HD)
    returned = lax.all_to_all(
        payload.astype(jnp.bfloat16), "wt", split_axis=1, concat_axis=1, tiled=True
    ).astype(payload.dtype)
    own = lax.dynamic_slice_in_dim(returned, my_group * heads, heads, 1)
    combined = own.transpose(0, 2, 1, 3).reshape(tile_rows, tile_cols, channels)
    combined = combined + cycle_conv(values_new, conv_weight, conv_bias)
    return combined.astype(jnp.bfloat16)


LOG2E = 1.4426950408889634
NEG = -1e30
VMEM = pl.BlockSpec(memory_space=pltpu.VMEM)
SMEM = pl.BlockSpec(memory_space=pltpu.SMEM)
FAR = pl.BlockSpec(memory_space=pltpu.HBM)
LIMIT = pltpu.CompilerParams(vmem_limit_bytes=8 * 1024 * 1024)
SMALL = pltpu.CompilerParams(vmem_limit_bytes=4 * 1024 * 1024)


class Window:
    def __init__(self, grid, tile, info_ref, query_ref, pairs_ref):
        self.grid_rows, self.grid_cols = grid
        self.tile_rows, self.tile_cols = tile
        self.size = self.tile_rows * self.tile_cols
        self.info, self.query, self.pairs = info_ref, query_ref, pairs_ref
        self.scale = HD ** (-0.5) * LOG2E
        query = lax.broadcasted_iota(jnp.int32, (self.size, self.size), 0)
        key = lax.broadcasted_iota(jnp.int32, (self.size, self.size), 1)
        self.upper = key // self.tile_cols >= query // self.tile_cols
        self.left = key % self.tile_cols >= query % self.tile_cols
        self.upper_one = self.upper.astype(jnp.float32).astype(jnp.bfloat16)

    def slot(self, row, col):
        return self.info[3 + row * self.grid_cols + col]

    def tile(self, member, row, col):
        return self.pairs[self.slot(row, col), member].reshape(self.size, HD)

    def scores(self, row, col, cols):
        query = self.query[self.slot(row, col), pl.ds(0, self.tile_rows)].reshape(self.size, HD)
        frames = range(self.pairs.shape[1] // 2)
        up, down = row > 0, row + 1 < self.grid_rows
        rows = [r for r in (row - 1, row, row + 1) if 0 <= r < self.grid_rows]
        needed = [(f, r, i) for f in frames for i in range(len(cols)) for r in rows]
        keys = jnp.concatenate([self.tile(2 * f, r, cols[i][0]) for f, r, i in needed], axis=0)
        raw = lax.dot_general(query, keys, (((1,), (1,)), ((), ())), preferred_element_type=jnp.float32)
        scores = {key: raw[:, i * self.size : (i + 1) * self.size] for i, key in enumerate(needed)}
        blocks = []
        for f in frames:
            for i, (c, allowed) in enumerate(cols):
                found = [(False, scores[f, row, i])]
                if up or down:
                    above = scores[f, row - 1, i] if up else NEG
                    found.append((True, jnp.where(self.upper, above, scores[f, row + 1, i] if down else NEG)))
                for off_row, block in found:
                    if allowed is not None:
                        block = jnp.where(allowed, block, NEG)
                    blocks.append((f, off_row, c, block))
        top = blocks[0][3]
        for entry in blocks[1:]:
            top = jnp.maximum(top, entry[3])
        return row, up and down, down, blocks, jnp.max(top, axis=1, keepdims=True)

    def weigh(self, row, both, down, blocks, top):
        parts = []
        for f, off_row, c, block in blocks:
            weights = jnp.exp2((block - top) * self.scale).astype(jnp.bfloat16)
            if off_row and both:
                parts.append((f, row - 1, c, weights * self.upper_one))
                parts.append((f, row + 1, c, weights * (1 - self.upper_one)))
            elif off_row:
                parts.append((f, row + 1 if down else row - 1, c, weights))
            else:
                parts.append((f, row, c, weights))
        values = jnp.concatenate([self.tile(2 * f + 1, r, c) for f, r, c, _ in parts], axis=0)
        values = jnp.concatenate([values, jnp.ones_like(values)], axis=1)
        weights = jnp.concatenate([part for _, _, _, part in parts], axis=1)
        total = jnp.dot(weights, values, preferred_element_type=jnp.float32)
        return total[:, :HD] / total[:, HD:], top * self.scale + jnp.log2(total[:, HD:])

    def attend(self, tiles):
        held = None
        for place in [*tiles, None]:
            ready = self.scores(*place) if place else None
            if held:
                yield (held[0][0] * self.grid_cols + held[0][1], *self.weigh(*held[1]))
            held = (place, ready)

    def enhanced(self, row, col, weight_ref, bias_ref, beyond):
        shape = (self.tile_cols, HD)
        sub = lax.broadcasted_iota(jnp.int32, shape, 0)
        taps = [[weight_ref[a, pl.ds(b, 1), :] for b in range(3)] for a in range(3)]
        last = self.tile_cols - 1
        member = self.pairs.shape[1] - 1
        lines = []
        for key_row in range(row * self.tile_rows - 1, (row + 1) * self.tile_rows + 1):
            tile_row, line = key_row // self.tile_rows, key_row % self.tile_rows
            if tile_row < 0 or tile_row >= self.grid_rows:
                lines.append(None)
                continue

            def values(c):
                return self.pairs[self.slot(tile_row, c), member, line].astype(jnp.float32)

            def edge(right, c):
                place = self.slot(tile_row, c), self.tile_rows + line // self.tile_cols
                first, second = (ref[place].astype(jnp.float32) for ref in beyond)
                packed = jnp.where(self.info[2] == right, first, second)
                return jnp.broadcast_to(packed[line % self.tile_cols : line % self.tile_cols + 1], shape)

            here = values(col)
            before = pltpu.roll(values(col - 1), 1, 0) if col > 0 else edge(0, self.grid_cols - 1)
            after = pltpu.roll(values(col + 1), last, 0) if col + 1 < self.grid_cols else edge(1, 0)
            low = jnp.where(sub == 0, before, pltpu.roll(here, 1, 0))
            high = jnp.where(sub == last, after, pltpu.roll(here, last, 0))
            lines.append((low, here, high))
        sums = []
        for line in range(self.tile_rows):
            total = jnp.broadcast_to(bias_ref[...], shape)
            for a in range(3):
                if lines[line + a] is not None:
                    for b in range(3):
                        total = total + lines[line + a][b] * taps[a][b]
            sums.append(total)
        return jnp.stack(sums, axis=0)


def visit_kernel(grid, tile, first, info_ref, query_ref, pairs_ref, out_ref):
    window = Window(grid, tile, info_ref, query_ref, pairs_ref)
    near = info_ref[2] if first else 1 - info_ref[2]
    allowed = window.left.astype(jnp.int32) == near
    tiles = []
    for row in range(grid[0]):
        tiles.append((row, 1 - near, [(near, None), (1 - near, allowed)]))
        tiles.append((row, near, [(near, allowed)]))
    size, count = window.size, grid[0] * grid[1]
    lane = lax.broadcasted_iota(jnp.int32, (size, HD), 1)
    levels = jnp.zeros((size, HD), jnp.float32)
    for index, part, level in window.attend(tiles):
        out_ref[index] = part.reshape(tile + (HD,)).astype(jnp.bfloat16)
        levels = jnp.where(lane == index, level, levels)
    high = levels.astype(jnp.bfloat16).astype(jnp.float32)
    middle = (levels - high).astype(jnp.bfloat16).astype(jnp.float32)
    packed = high + pltpu.roll(middle, count, 1) + pltpu.roll(levels - high - middle, 2 * count, 1)
    out_ref[count] = packed.reshape(tile + (HD,)).astype(jnp.bfloat16)


def own_kernel(
    grid, tile, info_ref, weight_ref, bias_ref, query_ref, pairs_ref, first_ref, second_ref, part_ref, level_ref, conv_ref
):
    window = Window(grid, tile, info_ref, query_ref, pairs_ref)
    cols = [(c, None) for c in range(grid[1])]
    tiles = [(row, col, cols) for row in range(grid[0]) for col in range(grid[1])]
    for index, part, level in window.attend(tiles):
        part_ref[index], level_ref[index] = part, level
        row, col = index // grid[1], index % grid[1]
        conv = window.enhanced(row, col, weight_ref, bias_ref, (first_ref, second_ref))
        conv_ref[index] = conv.reshape(window.size, HD)


def join_kernel(grid, tile, info_ref, part_ref, level_ref, conv_ref, first_ref, second_ref, out_ref):
    size, count = tile[0] * tile[1], grid[0] * grid[1]
    visits = (first_ref, second_ref)
    packed = []
    for i, ref in enumerate(visits):
        pack = ref[count].reshape(size, HD).astype(jnp.float32)
        level = pack + pltpu.roll(pack, HD - count, 1) + pltpu.roll(pack, HD - 2 * count, 1)
        packed.append(jnp.where(info_ref[i] > 0, level, NEG))
    for index in range(count):
        levels = [level_ref[index]]
        parts = [part_ref[index]]
        for ref, pack in zip(visits, packed):
            parts.append(ref[index].reshape(size, HD).astype(jnp.float32))
            levels.append(jnp.broadcast_to(pack[:, index : index + 1], (size, HD)))
        top = jnp.maximum(jnp.maximum(levels[0], levels[1]), levels[2])
        shares = [jnp.exp2(level - top) for level in levels]
        mixed = sum(share * part for share, part in zip(shares, parts)) / sum(shares)
        out_ref[info_ref[3 + index]] = (mixed + conv_ref[index]).reshape(tile + (HD,)).astype(jnp.bfloat16)


def lanes(head):
    return pl.ds(pl.multiple_of(head * HD, HD), HD)


def fetch(sources, held_ref, sems):
    groups = sems.shape[1]
    rows = held_ref.shape[1] // groups
    copies = []
    for i, source in enumerate(sources):
        parts = [pl.ds(j * rows, rows) for j in range(groups)]
        copies.append([pltpu.make_async_copy(source.at[p], held_ref.at[i, p], sems.at[i, j]) for j, p in enumerate(parts)])
        for copy in copies[-1]:
            copy.start()
    return copies


def finish(copies):
    for copy in copies:
        copy.wait()


def pack_kernel(flips, side, me_ref, *refs):
    count = len(flips)
    sources, buffers, held_ref, sems = refs[: -count - 2], refs[-count - 2 : -2], refs[-2], refs[-1]
    for member, copies in enumerate(fetch(sources, held_ref, sems)):
        finish(copies)
        for buffer, flip in zip(buffers, flips):
            for other in range(2):
                head = lanes(me_ref[0] ^ (flip ^ (side if other else 0)))
                buffer[other, member] = held_ref[member, :, :, head]


def query_kernel(flips, side, me_ref, query_ref, values_ref, *refs):
    buffers, held_ref, sems = refs[:-2], refs[-2], refs[-1]
    tile_rows, tile_cols, _ = query_ref.shape
    copies = fetch((query_ref, values_ref), held_ref, sems)
    places = [
        (buffer, other, lanes(me_ref[0] ^ (flip ^ (side if other else 0))))
        for buffer, flip in zip(buffers, flips)
        for other in range(2)
    ]
    finish(copies[0])
    for buffer, other, head in places:
        buffer[other, pl.ds(0, tile_rows)] = held_ref[0, :, :, head]
    finish(copies[1])
    sub = lax.broadcasted_iota(jnp.int32, (tile_cols, HD), 0)
    for buffer, other, head in places:
        for start in range(0, tile_rows, tile_cols):
            packed = jnp.zeros((tile_cols, HD), jnp.float32)
            for line in range(tile_cols):
                values = held_ref[1, start + line, :, head].astype(jnp.float32)
                edge = jnp.where(me_ref[1] == 0, values[:1], values[tile_cols - 1 :])
                packed = jnp.where(sub == line, edge, packed)
            buffer[other, tile_rows + start // tile_cols] = packed.astype(jnp.bfloat16)


def unpack_kernel(flips, me_ref, *refs):
    out_ref = refs[-1]
    for flip, ref in zip(flips, refs):
        out_ref[:, :, lanes(me_ref[0] ^ flip)] = ref[...]


def head_step(shape, queries, keys_new, values_new, keys_cache, values_cache, conv_weight, conv_bias):
    group_rows, group_cols, far = shape
    tile_rows, tile_cols, channels = queries.shape
    heads = channels // HD
    grid, tile = (group_rows, group_cols), (tile_rows, tile_cols)
    size = tile_rows * tile_cols
    axes = ("ht", "near")
    block = (tile_rows, tile_cols, HD)
    side = group_cols
    flips = [flip for flip in range(heads) if not flip & side]
    near = lax.axis_index("near").astype(jnp.int32)
    me = lax.axis_index("ht").astype(jnp.int32) * group_cols + near
    me_ref = jnp.stack([me, near])

    def swap(x, flip):
        return lax.ppermute(x, axes, [(s, s ^ flip) for s in range(heads)])

    def call(kernel, out_shape, params, cost, *operands, space=(VMEM, VMEM), scratch=()):
        return pl.pallas_call(
            kernel,
            out_shape=out_shape,
            in_specs=[SMEM] + [space[0]] * (len(operands) - 1),
            out_specs=jax.tree.map(lambda _: space[1], out_shape),
            scratch_shapes=scratch,
            compiler_params=params,
            cost_estimate=pl.CostEstimate(flops=cost << 30, bytes_accessed=1 << 20, transcendentals=0),
        )(*operands)

    def stay(x):
        return pltpu.with_memory_space_constraint(x, pltpu.HBM)

    def gather(buffers):
        got = [buffers[0]] + [swap(b, flip) for b, flip in zip(buffers[1:], flips[1:])]
        forward = [b[1] for b in got]
        beside = [swap(b, side) for b in forward]
        return jnp.stack([b[0] for b in got] + beside)

    def rounds(start):
        return [pair for i in range(start, far - 1, 2) for pair in ((i, i + 1), (i + 1, i))]

    first, second = rounds(0), rounds(1)
    edges = -(-tile_rows // tile_cols)

    def pack(kernel, buffer, *sources):
        return call(
            functools.partial(kernel, flips, side),
            [jax.ShapeDtypeStruct(buffer, jnp.bfloat16)] * len(flips),
            SMALL,
            0,
            me_ref,
            *map(stay, sources),
            space=(FAR, VMEM),
            scratch=[
                pltpu.VMEM((len(sources),) + queries.shape, jnp.bfloat16),
                pltpu.SemaphoreType.DMA((len(sources), 4)),
            ],
        )

    packed = pack(query_kernel, (2, tile_rows + edges, tile_cols, HD), queries, values_new)
    query = gather(packed)
    packed = pack(pack_kernel, (2, 4) + block, keys_cache[0], values_cache[0], keys_new, values_new)
    pairs = gather(packed)
    query_second = lax.ppermute(query, "far", second)
    query_first = lax.ppermute(query, "far", first)
    far_index = lax.axis_index("far")
    flip = me ^ jnp.arange(heads, dtype=jnp.int32)
    beside = (flip // side) % 2
    order = flip % side + flip // (2 * side) * side
    even = far_index % 2 == 0
    below, above = far_index > 0, far_index < far - 1
    info = jnp.concatenate(
        [
            jnp.stack([~even | above, jnp.where(even, below, above), even]).astype(jnp.int32),
            beside * len(flips) + order,
        ]
    )
    weight = lax.dynamic_slice_in_dim(conv_weight, me * HD, HD, 2)
    bias = lax.dynamic_slice_in_dim(conv_bias.reshape(1, channels), me * HD, HD, 1)

    def visit(queries, is_first):
        kernel = functools.partial(visit_kernel, grid, tile, is_first)
        return call(kernel, jax.ShapeDtypeStruct((heads + 1,) + block, jnp.bfloat16), LIMIT, 4, info, queries, pairs)

    part = visit(query_second, False)
    home_second = lax.ppermute(part, "far", second)
    part = visit(query_first, True)
    home_first = lax.ppermute(part, "far", first)
    part = jax.ShapeDtypeStruct((heads, size, HD), jnp.float32)
    kernel = functools.partial(own_kernel, grid, tile)
    own = call(kernel, [part] * 3, LIMIT, 4, info, weight, bias, query, pairs, query_first, query_second)
    kernel = functools.partial(join_kernel, grid, tile)
    result = jax.ShapeDtypeStruct((heads,) + block, jnp.bfloat16)
    result = call(kernel, result, LIMIT, 1, info, *own, home_first, home_second)
    places = [*flips, *(flip ^ side for flip in flips)]
    got = {0: result[0]}
    for flip in sorted(places[1:], key=lambda flip: (-flip.bit_count(), -flip)):
        got[flip] = swap(result[places.index(flip)], flip)
    return call(
        functools.partial(unpack_kernel, list(got)),
        jax.ShapeDtypeStruct(queries.shape, jnp.bfloat16),
        SMALL,
        0,
        me_ref,
        *got.values(),
    )


def grouping(mesh, heads):
    rows, cols = mesh.shape["ht"], mesh.shape["wt"]
    group_rows = rows
    group_cols = heads // group_rows if heads % group_rows == 0 else 0
    if group_cols != 2 or cols % group_cols:
        return None
    return group_rows, group_cols, cols // group_cols


def solution(mesh):
    def program(queries, *rest):
        heads = queries.shape[2] // HD
        shape = grouping(mesh, heads)
        if shape is None or queries.shape[0] != mesh.shape["ht"] * (WIN // 2) or queries.shape[1] != mesh.shape["wt"] * (WIN // 4):
            placed = (P("ht", "wt", None),) * 3 + (P(None, "ht", "wt", None),) * 2 + (P(), P())
            return jax.shard_map(
                shards, mesh=mesh, in_specs=placed, out_specs=P("ht", "wt", None), check_vma=False
            )(queries, *rest)
        devices = mesh.devices.reshape(shape[0], shape[2], shape[1])
        split = Mesh(devices, ("ht", "far", "near"))
        tile = P("ht", ("far", "near"), None)
        past = P(None, "ht", ("far", "near"), None)
        step = jax.shard_map(
            functools.partial(head_step, shape),
            mesh=split,
            in_specs=(tile, tile, tile, past, past, P(), P()),
            out_specs=tile,
            check_vma=False,
        )
        return step(queries, *rest)

    return program
```

```python
import functools

import jax
import jax.numpy as jnp
from jax import lax
from jax.experimental import pallas as pl
from jax.experimental.pallas import tpu as pltpu
from jax.sharding import Mesh, PartitionSpec as P


HD = 128
WIN = 32


def with_halo(block, sides, width):
    for axis, dim in sides:
        count = lax.axis_size(axis)
        forward = [(i, i + 1) for i in range(count - 1)]
        backward = [(target, source) for source, target in forward]
        low = lax.ppermute(
            lax.slice_in_dim(block, block.shape[dim] - width, None, axis=dim), axis, forward
        )
        high = lax.ppermute(lax.slice_in_dim(block, 0, width, axis=dim), axis, backward)
        block = jnp.concatenate([low, block, high], axis=dim)
    return block


def window_allowed(row_start, col_start, frame_rows, frame_cols, tile_rows, tile_cols, half_win):
    ext_rows = jnp.arange(tile_rows + 2 * half_win, dtype=jnp.int32) - half_win
    ext_cols = jnp.arange(tile_cols + 2 * half_win, dtype=jnp.int32) - half_win
    query_rows = jnp.arange(tile_rows, dtype=jnp.int32)
    query_cols = jnp.arange(tile_cols, dtype=jnp.int32)
    row_delta = ext_rows[None, :] - query_rows[:, None]
    col_delta = ext_cols[None, :] - query_cols[:, None]
    global_rows = row_start + ext_rows
    global_cols = col_start + ext_cols
    row_valid = (
        (row_delta >= -half_win)
        & (row_delta < half_win)
        & ((global_rows >= 0) & (global_rows < frame_rows))[None, :]
    )
    col_valid = (
        (col_delta >= -half_win)
        & (col_delta < half_win)
        & ((global_cols >= 0) & (global_cols < frame_cols))[None, :]
    )
    allowed = row_valid[:, None, :, None] & col_valid[None, :, None, :]
    return allowed.reshape(
        tile_rows * tile_cols, (tile_rows + 2 * half_win) * (tile_cols + 2 * half_win)
    )


def attend(query_rows, keys_flat, values_flat, allowed, heads, head_dim):
    score_scale = head_dim ** (-0.5)

    def one_head(head_index):
        scores = (
            jnp.einsum("qd,kd->qk", query_rows, keys_flat, preferred_element_type=jnp.float32)
            * score_scale
        )
        scores = jnp.where(allowed, scores, -1e30)
        row_top = jnp.max(scores, axis=1, keepdims=True)
        weights_f = jnp.exp(scores - row_top)
        denominator = jnp.sum(weights_f, axis=1, keepdims=True)
        numerator = jnp.dot(
            weights_f.astype(jnp.bfloat16), values_flat, preferred_element_type=jnp.float32
        )
        return numerator / denominator

    outputs = lax.map(one_head, jnp.arange(heads, dtype=jnp.int32))
    return outputs.transpose(1, 0, 2).reshape(query_rows.shape[0], heads * head_dim)


def local_conv(padded, conv_weight, conv_bias, tile_rows, tile_cols):
    enhanced = jnp.zeros((tile_rows, tile_cols, padded.shape[2]), jnp.float32) + conv_bias
    for row_shift in range(3):
        for col_shift in range(3):
            enhanced = (
                enhanced
                + padded[
                    row_shift : row_shift + tile_rows, col_shift : col_shift + tile_cols
                ].astype(jnp.float32)
                * conv_weight[row_shift, col_shift]
            )
    return enhanced


def cycle_conv(values_new, conv_weight, conv_bias):
    tile_rows, tile_cols, _ = values_new.shape
    padded = with_halo(values_new, (("ht", 0), ("wt", 1)), 1)
    return local_conv(padded, conv_weight, conv_bias, tile_rows, tile_cols)


def shards(queries, keys_new, values_new, keys_cache, values_cache, conv_weight, conv_bias):
    tile_rows, tile_cols, channels = queries.shape
    frames = keys_cache.shape[0] + 1
    half_win = WIN // 2
    stacked = jnp.concatenate([keys_cache, keys_new[None], values_cache, values_new[None]], axis=0)
    row_start = lax.axis_index("ht") * tile_rows
    frame_rows = tile_rows * lax.axis_size("ht")
    frame_cols = tile_cols * lax.axis_size("wt")
    heads = channels // HD
    copies = lax.axis_size("wt") // heads
    bundle = jnp.concatenate([stacked, queries[None]], axis=0)
    members = bundle.shape[0]
    spread = bundle.reshape(members, tile_rows, tile_cols, 1, heads, HD)
    spread = jnp.broadcast_to(spread, (members, tile_rows, tile_cols, copies, heads, HD))
    spread = spread.reshape(members, tile_rows, tile_cols, copies * heads, HD)
    strips = lax.all_to_all(spread, "wt", split_axis=3, concat_axis=2, tiled=True)
    strips = strips.reshape(members, tile_rows, frame_cols, HD)
    device_index = lax.axis_index("wt")
    my_group = device_index // heads
    block_width = tile_cols * heads
    block_start = my_group * block_width
    padded_cols = jnp.pad(strips, ((0, 0), (0, 0), (half_win, half_win), (0, 0)))
    window = lax.dynamic_slice_in_dim(padded_cols, block_start, block_width + 2 * half_win, 2)
    query_part = window[2 * frames, :, half_win : half_win + block_width]
    region = with_halo(window[: 2 * frames], (("ht", 1),), half_win)

    def one_block(step):
        offset = step * tile_cols
        query_block = lax.dynamic_slice_in_dim(query_part, offset, tile_cols, 1).reshape(
            tile_rows * tile_cols, HD
        )
        sub = lax.dynamic_slice_in_dim(region, offset, tile_cols + 2 * half_win, 2)
        keys_flat = sub[:frames].reshape(-1, HD)
        values_flat = sub[frames:].reshape(-1, HD)
        allowed = window_allowed(
            row_start, block_start + offset, frame_rows, frame_cols, tile_rows, tile_cols, half_win
        )
        allowed = jnp.tile(allowed, (1, frames))
        result = attend(query_block, keys_flat, values_flat, allowed, 1, HD)
        return result.reshape(tile_rows, tile_cols, HD)

    blocks = lax.map(one_block, jnp.arange(heads, dtype=jnp.int32))
    payload = blocks.transpose(1, 0, 2, 3)
    payload = jnp.broadcast_to(payload[:, None], (tile_rows, copies, heads, tile_cols, HD))
    payload = payload.reshape(tile_rows, copies * heads, tile_cols, HD)
    returned = lax.all_to_all(
        payload.astype(jnp.bfloat16), "wt", split_axis=1, concat_axis=1, tiled=True
    ).astype(payload.dtype)
    own = lax.dynamic_slice_in_dim(returned, my_group * heads, heads, 1)
    combined = own.transpose(0, 2, 1, 3).reshape(tile_rows, tile_cols, channels)
    combined = combined + cycle_conv(values_new, conv_weight, conv_bias)
    return combined.astype(jnp.bfloat16)


LOG2E = 1.4426950408889634
NEG = -1e30
VMEM = pl.BlockSpec(memory_space=pltpu.VMEM)
FAR = pl.BlockSpec(memory_space=pltpu.HBM)
LIMIT = pltpu.CompilerParams(vmem_limit_bytes=8 * 1024 * 1024)
SMALL = pltpu.CompilerParams(vmem_limit_bytes=4 * 1024 * 1024)


def position(group_cols):
    return lax.axis_index("ht") * group_cols + lax.axis_index("near")


def slot_of(group_cols, tile):
    side = group_cols
    flip = position(group_cols) ^ tile
    order = lax.rem(flip, side) + flip // (2 * side) * side
    return lax.rem(flip // side, 2) * (lax.axis_size("ht") * group_cols // 2) + order


def first_is_right():
    return 1 - lax.rem(lax.axis_index("far"), 2)


class Window:
    def __init__(self, grid, tile, query_ref, pairs_ref):
        self.grid_rows, self.grid_cols = grid
        self.tile_rows, self.tile_cols = tile
        self.size = self.tile_rows * self.tile_cols
        self.query, self.pairs = query_ref, pairs_ref
        self.scale = HD ** (-0.5) * LOG2E
        query = lax.broadcasted_iota(jnp.int32, (self.size, self.size), 0)
        key = lax.broadcasted_iota(jnp.int32, (self.size, self.size), 1)
        self.upper = key // self.tile_cols >= query // self.tile_cols
        self.left = key % self.tile_cols >= query % self.tile_cols
        self.upper_one = self.upper.astype(jnp.float32).astype(jnp.bfloat16)

    def slot(self, row, col):
        return slot_of(self.grid_cols, row * self.grid_cols + col)

    def tile(self, member, row, col):
        return self.pairs[self.slot(row, col), member].reshape(self.size, HD)

    def scores(self, row, col, cols):
        query = self.query[self.slot(row, col), pl.ds(0, self.tile_rows)].reshape(self.size, HD)
        frames = range(self.pairs.shape[1] // 2)
        up, down = row > 0, row + 1 < self.grid_rows
        rows = [r for r in (row - 1, row, row + 1) if 0 <= r < self.grid_rows]
        needed = [(f, r, i) for f in frames for i in range(len(cols)) for r in rows]
        keys = jnp.concatenate([self.tile(2 * f, r, cols[i][0]) for f, r, i in needed], axis=0)
        raw = lax.dot_general(query, keys, (((1,), (1,)), ((), ())), preferred_element_type=jnp.float32)
        scores = {key: raw[:, i * self.size : (i + 1) * self.size] for i, key in enumerate(needed)}
        blocks = []
        for f in frames:
            for i, (c, allowed) in enumerate(cols):
                found = [(False, scores[f, row, i])]
                if up or down:
                    above = scores[f, row - 1, i] if up else NEG
                    found.append((True, jnp.where(self.upper, above, scores[f, row + 1, i] if down else NEG)))
                for off_row, block in found:
                    if allowed is not None:
                        block = jnp.where(allowed, block, NEG)
                    blocks.append((f, off_row, c, block))
        top = blocks[0][3]
        for entry in blocks[1:]:
            top = jnp.maximum(top, entry[3])
        return row, up and down, down, blocks, jnp.max(top, axis=1, keepdims=True)

    def weigh(self, row, both, down, blocks, top):
        parts = []
        for f, off_row, c, block in blocks:
            weights = jnp.exp2((block - top) * self.scale).astype(jnp.bfloat16)
            if off_row and both:
                parts.append((f, row - 1, c, weights * self.upper_one))
                parts.append((f, row + 1, c, weights * (1 - self.upper_one)))
            elif off_row:
                parts.append((f, row + 1 if down else row - 1, c, weights))
            else:
                parts.append((f, row, c, weights))
        values = jnp.concatenate([self.tile(2 * f + 1, r, c) for f, r, c, _ in parts], axis=0)
        values = jnp.concatenate([values, jnp.ones_like(values)], axis=1)
        weights = jnp.concatenate([part for _, _, _, part in parts], axis=1)
        total = jnp.dot(weights, values, preferred_element_type=jnp.float32)
        return total[:, :HD] / total[:, HD:], top * self.scale + jnp.log2(total[:, HD:])

    def attend(self, tiles):
        held = None
        for place in [*tiles, None]:
            ready = self.scores(*place) if place else None
            if held:
                yield (held[0][0] * self.grid_cols + held[0][1], *self.weigh(*held[1]))
            held = (place, ready)

    def enhanced(self, row, col, weight_ref, bias_ref, beyond):
        shape = (self.tile_cols, HD)
        sub = lax.broadcasted_iota(jnp.int32, shape, 0)
        taps = [[weight_ref[a, pl.ds(b, 1), :] for b in range(3)] for a in range(3)]
        last = self.tile_cols - 1
        member = self.pairs.shape[1] - 1
        lines = []
        for key_row in range(row * self.tile_rows - 1, (row + 1) * self.tile_rows + 1):
            tile_row, line = key_row // self.tile_rows, key_row % self.tile_rows
            if tile_row < 0 or tile_row >= self.grid_rows:
                lines.append(None)
                continue

            def values(c):
                return self.pairs[self.slot(tile_row, c), member, line].astype(jnp.float32)

            def edge(right, c):
                place = self.slot(tile_row, c), self.tile_rows + line // self.tile_cols
                first, second = (ref[place].astype(jnp.float32) for ref in beyond)
                packed = jnp.where(first_is_right() == right, first, second)
                return jnp.broadcast_to(packed[line % self.tile_cols : line % self.tile_cols + 1], shape)

            here = values(col)
            before = pltpu.roll(values(col - 1), 1, 0) if col > 0 else edge(0, self.grid_cols - 1)
            after = pltpu.roll(values(col + 1), last, 0) if col + 1 < self.grid_cols else edge(1, 0)
            low = jnp.where(sub == 0, before, pltpu.roll(here, 1, 0))
            high = jnp.where(sub == last, after, pltpu.roll(here, last, 0))
            lines.append((low, here, high))
        sums = []
        for line in range(self.tile_rows):
            total = jnp.broadcast_to(bias_ref[...], shape)
            for a in range(3):
                if lines[line + a] is not None:
                    for b in range(3):
                        total = total + lines[line + a][b] * taps[a][b]
            sums.append(total)
        return jnp.stack(sums, axis=0)


def visit_kernel(grid, tile, first, query_ref, pairs_ref, out_ref):
    window = Window(grid, tile, query_ref, pairs_ref)
    near = first_is_right() if first else 1 - first_is_right()
    allowed = window.left.astype(jnp.int32) == near
    tiles = []
    for row in range(grid[0]):
        tiles.append((row, 1 - near, [(near, None), (1 - near, allowed)]))
        tiles.append((row, near, [(near, allowed)]))
    size, count = window.size, grid[0] * grid[1]
    lane = lax.broadcasted_iota(jnp.int32, (size, HD), 1)
    levels = jnp.zeros((size, HD), jnp.float32)
    for index, part, level in window.attend(tiles):
        out_ref[index] = part.reshape(tile + (HD,)).astype(jnp.bfloat16)
        levels = jnp.where(lane == index, level, levels)
    high = levels.astype(jnp.bfloat16).astype(jnp.float32)
    middle = (levels - high).astype(jnp.bfloat16).astype(jnp.float32)
    packed = high + pltpu.roll(middle, count, 1) + pltpu.roll(levels - high - middle, 2 * count, 1)
    out_ref[count] = packed.reshape(tile + (HD,)).astype(jnp.bfloat16)


def own_kernel(
    grid, tile, weight_ref, bias_ref, query_ref, pairs_ref, first_ref, second_ref, part_ref, level_ref, conv_ref
):
    window = Window(grid, tile, query_ref, pairs_ref)
    cols = [(c, None) for c in range(grid[1])]
    tiles = [(row, col, cols) for row in range(grid[0]) for col in range(grid[1])]
    for index, part, level in window.attend(tiles):
        part_ref[index], level_ref[index] = part, level
        row, col = index // grid[1], index % grid[1]
        conv = window.enhanced(row, col, weight_ref, bias_ref, (first_ref, second_ref))
        conv_ref[index] = conv.reshape(window.size, HD)


def join_kernel(grid, tile, far, part_ref, level_ref, conv_ref, first_ref, second_ref, out_ref):
    size, count = tile[0] * tile[1], grid[0] * grid[1]
    visits = (first_ref, second_ref)
    place = lax.axis_index("far")
    even = lax.rem(place, 2) == 0
    present = [~even | (place < far - 1), jnp.where(even, place > 0, place < far - 1)]
    packed = []
    for there, ref in zip(present, visits):
        pack = ref[count].reshape(size, HD).astype(jnp.float32)
        level = pack + pltpu.roll(pack, HD - count, 1) + pltpu.roll(pack, HD - 2 * count, 1)
        packed.append(jnp.where(there, level, NEG))
    for index in range(count):
        levels = [level_ref[index]]
        parts = [part_ref[index]]
        for ref, pack in zip(visits, packed):
            parts.append(ref[index].reshape(size, HD).astype(jnp.float32))
            levels.append(jnp.broadcast_to(pack[:, index : index + 1], (size, HD)))
        top = jnp.maximum(jnp.maximum(levels[0], levels[1]), levels[2])
        shares = [jnp.exp2(level - top) for level in levels]
        mixed = sum(share * part for share, part in zip(shares, parts)) / sum(shares)
        out_ref[slot_of(grid[1], index)] = (mixed + conv_ref[index]).reshape(tile + (HD,)).astype(jnp.bfloat16)


def lanes(head):
    return pl.ds(pl.multiple_of(head * HD, HD), HD)


def fetch(sources, held_ref, sems):
    copies = [pltpu.make_async_copy(x, held_ref.at[i], sems.at[i]) for i, x in enumerate(sources)]
    for copy in copies:
        copy.start()
    return copies


def pack_kernel(flips, side, *refs):
    count = len(flips)
    sources, buffers, held_ref, sems = refs[: -count - 2], refs[-count - 2 : -2], refs[-2], refs[-1]
    for member, copy in enumerate(fetch(sources, held_ref, sems)):
        copy.wait()
        for buffer, flip in zip(buffers, flips):
            for other in range(2):
                head = lanes(position(side) ^ (flip ^ (side if other else 0)))
                buffer[other, member] = held_ref[member, :, :, head]


def query_kernel(flips, side, query_ref, values_ref, *refs):
    buffers, held_ref, sems = refs[:-2], refs[-2], refs[-1]
    tile_rows, tile_cols, _ = query_ref.shape
    copies = fetch((query_ref, values_ref), held_ref, sems)
    places = [
        (buffer, other, lanes(position(side) ^ (flip ^ (side if other else 0))))
        for buffer, flip in zip(buffers, flips)
        for other in range(2)
    ]
    copies[0].wait()
    for buffer, other, head in places:
        buffer[other, pl.ds(0, tile_rows)] = held_ref[0, :, :, head]
    copies[1].wait()
    sub = lax.broadcasted_iota(jnp.int32, (tile_cols, HD), 0)
    for buffer, other, head in places:
        for start in range(0, tile_rows, tile_cols):
            packed = jnp.zeros((tile_cols, HD), jnp.float32)
            for line in range(tile_cols):
                values = held_ref[1, start + line, :, head].astype(jnp.float32)
                edge = jnp.where(lax.axis_index("near") == 0, values[:1], values[tile_cols - 1 :])
                packed = jnp.where(sub == line, edge, packed)
            buffer[other, tile_rows + start // tile_cols] = packed.astype(jnp.bfloat16)


def unpack_kernel(flips, side, same_ref, beside_ref, *refs):
    out_ref = refs[-1]
    out_ref[:, :, lanes(position(side))] = same_ref[0]
    out_ref[:, :, lanes(position(side) ^ side)] = beside_ref[0]
    for i, flip in enumerate(flips[1:]):
        out_ref[:, :, lanes(position(side) ^ flip)] = refs[i][0]
        out_ref[:, :, lanes(position(side) ^ (flip ^ side))] = refs[i][1]


def head_step(shape, queries, keys_new, values_new, keys_cache, values_cache, conv_weight, conv_bias):
    group_rows, group_cols, far = shape
    tile_rows, tile_cols, channels = queries.shape
    heads = channels // HD
    grid, tile = (group_rows, group_cols), (tile_rows, tile_cols)
    size = tile_rows * tile_cols
    axes = ("ht", "near")
    block = (tile_rows, tile_cols, HD)
    side = group_cols
    flips = [flip for flip in range(heads) if not flip & side]
    near = lax.axis_index("near").astype(jnp.int32)
    me = lax.axis_index("ht").astype(jnp.int32) * group_cols + near

    def swap(x, flip):
        return lax.ppermute(x, axes, [(s, s ^ flip) for s in range(heads)])

    def call(kernel, out_shape, params, cost, *operands, space=(VMEM, VMEM), scratch=()):
        return pl.pallas_call(
            kernel,
            out_shape=out_shape,
            in_specs=[space[0]] * len(operands),
            out_specs=jax.tree.map(lambda _: space[1], out_shape),
            scratch_shapes=scratch,
            compiler_params=params,
            cost_estimate=pl.CostEstimate(flops=cost << 30, bytes_accessed=1 << 20, transcendentals=0),
        )(*operands)

    def stay(x):
        return pltpu.with_memory_space_constraint(x, pltpu.HBM)

    def gather(buffers):
        got = [buffers[0]] + [swap(b, flip) for b, flip in zip(buffers[1:], flips[1:])]
        forward = jnp.stack([b[1] for b in got])
        beside = swap(forward, side)
        return jnp.concatenate([jnp.stack([b[0] for b in got]), beside], axis=0)

    def rounds(start):
        return [pair for i in range(start, far - 1, 2) for pair in ((i, i + 1), (i + 1, i))]

    first, second = rounds(0), rounds(1)
    edges = -(-tile_rows // tile_cols)

    def pack(kernel, buffer, *sources):
        return call(
            functools.partial(kernel, flips, side),
            [jax.ShapeDtypeStruct(buffer, jnp.bfloat16)] * len(flips),
            SMALL,
            0,
            *map(stay, sources),
            space=(FAR, VMEM),
            scratch=[
                pltpu.VMEM((len(sources),) + queries.shape, jnp.bfloat16),
                pltpu.SemaphoreType.DMA((len(sources),)),
            ],
        )

    packed = pack(query_kernel, (2, tile_rows + edges, tile_cols, HD), queries, values_new)
    query = gather(packed)
    packed = pack(pack_kernel, (2, 4) + block, keys_cache[0], values_cache[0], keys_new, values_new)
    pairs = gather(packed)
    query_second = lax.ppermute(query, "far", second)
    query_first = lax.ppermute(query, "far", first)
    weight = lax.dynamic_slice_in_dim(conv_weight, me * HD, HD, 2)
    bias = lax.dynamic_slice_in_dim(conv_bias.reshape(1, channels), me * HD, HD, 1)

    def visit(queries, is_first):
        kernel = functools.partial(visit_kernel, grid, tile, is_first)
        return call(kernel, jax.ShapeDtypeStruct((heads + 1,) + block, jnp.bfloat16), LIMIT, 4, queries, pairs)

    part = visit(query_second, False)
    home_second = lax.ppermute(part, "far", second)
    part = visit(query_first, True)
    home_first = lax.ppermute(part, "far", first)
    part = jax.ShapeDtypeStruct((heads, size, HD), jnp.float32)
    kernel = functools.partial(own_kernel, grid, tile)
    own = call(kernel, [part] * 3, LIMIT, 4, weight, bias, query, pairs, query_first, query_second)
    kernel = functools.partial(join_kernel, grid, tile, far)
    result = jax.ShapeDtypeStruct((heads,) + block, jnp.bfloat16)
    result = call(kernel, result, LIMIT, 1, *own, home_first, home_second)
    same, other = result[: len(flips)], result[len(flips) :]
    received = swap(other, side)
    got = []
    for i in range(1, len(flips)):
        got.append(swap(jnp.stack([same[i], received[i]]), flips[i]))
    return call(
        functools.partial(unpack_kernel, flips, side),
        jax.ShapeDtypeStruct(queries.shape, jnp.bfloat16),
        SMALL,
        0,
        same,
        received,
        *got,
    )


def grouping(mesh, heads):
    rows, cols = mesh.shape["ht"], mesh.shape["wt"]
    group_rows = rows
    group_cols = heads // group_rows if heads % group_rows == 0 else 0
    if group_cols != 2 or cols % group_cols:
        return None
    return group_rows, group_cols, cols // group_cols


def solution(mesh):
    def program(queries, *rest):
        heads = queries.shape[2] // HD
        shape = grouping(mesh, heads)
        if shape is None or queries.shape[0] != mesh.shape["ht"] * (WIN // 2) or queries.shape[1] != mesh.shape["wt"] * (WIN // 4):
            placed = (P("ht", "wt", None),) * 3 + (P(None, "ht", "wt", None),) * 2 + (P(), P())
            return jax.shard_map(
                shards, mesh=mesh, in_specs=placed, out_specs=P("ht", "wt", None), check_vma=False
            )(queries, *rest)
        devices = mesh.devices.reshape(shape[0], shape[2], shape[1])
        split = Mesh(devices, ("ht", "far", "near"))
        tile = P("ht", ("far", "near"), None)
        past = P(None, "ht", ("far", "near"), None)
        step = jax.shard_map(
            functools.partial(head_step, shape),
            mesh=split,
            in_specs=(tile, tile, tile, past, past, P(), P()),
            out_specs=tile,
            check_vma=False,
        )
        return step(queries, *rest)

    return program
```

```python
import functools

import jax
import jax.numpy as jnp
from jax import lax
from jax.experimental import pallas as pl
from jax.experimental.pallas import tpu as pltpu
from jax.sharding import Mesh, PartitionSpec as P


HD = 128
WIN = 32


def with_halo(block, sides, width):
    for axis, dim in sides:
        count = lax.axis_size(axis)
        forward = [(i, i + 1) for i in range(count - 1)]
        backward = [(target, source) for source, target in forward]
        low = lax.ppermute(
            lax.slice_in_dim(block, block.shape[dim] - width, None, axis=dim), axis, forward
        )
        high = lax.ppermute(lax.slice_in_dim(block, 0, width, axis=dim), axis, backward)
        block = jnp.concatenate([low, block, high], axis=dim)
    return block


def window_allowed(row_start, col_start, frame_rows, frame_cols, tile_rows, tile_cols, half_win):
    ext_rows = jnp.arange(tile_rows + 2 * half_win, dtype=jnp.int32) - half_win
    ext_cols = jnp.arange(tile_cols + 2 * half_win, dtype=jnp.int32) - half_win
    query_rows = jnp.arange(tile_rows, dtype=jnp.int32)
    query_cols = jnp.arange(tile_cols, dtype=jnp.int32)
    row_delta = ext_rows[None, :] - query_rows[:, None]
    col_delta = ext_cols[None, :] - query_cols[:, None]
    global_rows = row_start + ext_rows
    global_cols = col_start + ext_cols
    row_valid = (
        (row_delta >= -half_win)
        & (row_delta < half_win)
        & ((global_rows >= 0) & (global_rows < frame_rows))[None, :]
    )
    col_valid = (
        (col_delta >= -half_win)
        & (col_delta < half_win)
        & ((global_cols >= 0) & (global_cols < frame_cols))[None, :]
    )
    allowed = row_valid[:, None, :, None] & col_valid[None, :, None, :]
    return allowed.reshape(
        tile_rows * tile_cols, (tile_rows + 2 * half_win) * (tile_cols + 2 * half_win)
    )


def attend(query_rows, keys_flat, values_flat, allowed, heads, head_dim):
    score_scale = head_dim ** (-0.5)

    def one_head(head_index):
        scores = (
            jnp.einsum("qd,kd->qk", query_rows, keys_flat, preferred_element_type=jnp.float32)
            * score_scale
        )
        scores = jnp.where(allowed, scores, -1e30)
        row_top = jnp.max(scores, axis=1, keepdims=True)
        weights_f = jnp.exp(scores - row_top)
        denominator = jnp.sum(weights_f, axis=1, keepdims=True)
        numerator = jnp.dot(
            weights_f.astype(jnp.bfloat16), values_flat, preferred_element_type=jnp.float32
        )
        return numerator / denominator

    outputs = lax.map(one_head, jnp.arange(heads, dtype=jnp.int32))
    return outputs.transpose(1, 0, 2).reshape(query_rows.shape[0], heads * head_dim)


def local_conv(padded, conv_weight, conv_bias, tile_rows, tile_cols):
    enhanced = jnp.zeros((tile_rows, tile_cols, padded.shape[2]), jnp.float32) + conv_bias
    for row_shift in range(3):
        for col_shift in range(3):
            enhanced = (
                enhanced
                + padded[
                    row_shift : row_shift + tile_rows, col_shift : col_shift + tile_cols
                ].astype(jnp.float32)
                * conv_weight[row_shift, col_shift]
            )
    return enhanced


def cycle_conv(values_new, conv_weight, conv_bias):
    tile_rows, tile_cols, _ = values_new.shape
    padded = with_halo(values_new, (("ht", 0), ("wt", 1)), 1)
    return local_conv(padded, conv_weight, conv_bias, tile_rows, tile_cols)


def shards(queries, keys_new, values_new, keys_cache, values_cache, conv_weight, conv_bias):
    tile_rows, tile_cols, channels = queries.shape
    frames = keys_cache.shape[0] + 1
    half_win = WIN // 2
    stacked = jnp.concatenate([keys_cache, keys_new[None], values_cache, values_new[None]], axis=0)
    row_start = lax.axis_index("ht") * tile_rows
    frame_rows = tile_rows * lax.axis_size("ht")
    frame_cols = tile_cols * lax.axis_size("wt")
    heads = channels // HD
    copies = lax.axis_size("wt") // heads
    bundle = jnp.concatenate([stacked, queries[None]], axis=0)
    members = bundle.shape[0]
    spread = bundle.reshape(members, tile_rows, tile_cols, 1, heads, HD)
    spread = jnp.broadcast_to(spread, (members, tile_rows, tile_cols, copies, heads, HD))
    spread = spread.reshape(members, tile_rows, tile_cols, copies * heads, HD)
    strips = lax.all_to_all(spread, "wt", split_axis=3, concat_axis=2, tiled=True)
    strips = strips.reshape(members, tile_rows, frame_cols, HD)
    device_index = lax.axis_index("wt")
    my_group = device_index // heads
    block_width = tile_cols * heads
    block_start = my_group * block_width
    padded_cols = jnp.pad(strips, ((0, 0), (0, 0), (half_win, half_win), (0, 0)))
    window = lax.dynamic_slice_in_dim(padded_cols, block_start, block_width + 2 * half_win, 2)
    query_part = window[2 * frames, :, half_win : half_win + block_width]
    region = with_halo(window[: 2 * frames], (("ht", 1),), half_win)

    def one_block(step):
        offset = step * tile_cols
        query_block = lax.dynamic_slice_in_dim(query_part, offset, tile_cols, 1).reshape(
            tile_rows * tile_cols, HD
        )
        sub = lax.dynamic_slice_in_dim(region, offset, tile_cols + 2 * half_win, 2)
        keys_flat = sub[:frames].reshape(-1, HD)
        values_flat = sub[frames:].reshape(-1, HD)
        allowed = window_allowed(
            row_start, block_start + offset, frame_rows, frame_cols, tile_rows, tile_cols, half_win
        )
        allowed = jnp.tile(allowed, (1, frames))
        result = attend(query_block, keys_flat, values_flat, allowed, 1, HD)
        return result.reshape(tile_rows, tile_cols, HD)

    blocks = lax.map(one_block, jnp.arange(heads, dtype=jnp.int32))
    payload = blocks.transpose(1, 0, 2, 3)
    payload = jnp.broadcast_to(payload[:, None], (tile_rows, copies, heads, tile_cols, HD))
    payload = payload.reshape(tile_rows, copies * heads, tile_cols, HD)
    returned = lax.all_to_all(
        payload.astype(jnp.bfloat16), "wt", split_axis=1, concat_axis=1, tiled=True
    ).astype(payload.dtype)
    own = lax.dynamic_slice_in_dim(returned, my_group * heads, heads, 1)
    combined = own.transpose(0, 2, 1, 3).reshape(tile_rows, tile_cols, channels)
    combined = combined + cycle_conv(values_new, conv_weight, conv_bias)
    return combined.astype(jnp.bfloat16)


LOG2E = 1.4426950408889634
NEG = -1e30
VMEM = pl.BlockSpec(memory_space=pltpu.VMEM)
FAR = pl.BlockSpec(memory_space=pltpu.HBM)
LIMIT = pltpu.CompilerParams(vmem_limit_bytes=8 * 1024 * 1024)
SMALL = pltpu.CompilerParams(vmem_limit_bytes=4 * 1024 * 1024)


def position(group_cols):
    return lax.axis_index("ht") * group_cols + lax.axis_index("near")


def place_of(group_cols, tile):
    side = group_cols
    flip = position(group_cols) ^ tile
    return lax.rem(flip // side, 2), lax.rem(flip, side) + flip // (2 * side) * side


def slot_of(group_cols, tile):
    beside, order = place_of(group_cols, tile)
    return beside * (lax.axis_size("ht") * group_cols // 2) + order


def pair_slot_of(group_cols, tile):
    beside, order = place_of(group_cols, tile)
    return order * 2 + beside


def first_is_right():
    return 1 - lax.rem(lax.axis_index("far"), 2)


class Window:
    def __init__(self, grid, tile, query_ref, pairs_ref):
        self.grid_rows, self.grid_cols = grid
        self.tile_rows, self.tile_cols = tile
        self.size = self.tile_rows * self.tile_cols
        self.query, self.pairs = query_ref, pairs_ref
        self.scale = HD ** (-0.5) * LOG2E
        query = lax.broadcasted_iota(jnp.int32, (self.size, self.size), 0)
        key = lax.broadcasted_iota(jnp.int32, (self.size, self.size), 1)
        self.upper = key // self.tile_cols >= query // self.tile_cols
        self.left = key % self.tile_cols >= query % self.tile_cols
        self.upper_one = self.upper.astype(jnp.float32).astype(jnp.bfloat16)

    def slot(self, row, col):
        return slot_of(self.grid_cols, row * self.grid_cols + col)

    def pair_slot(self, row, col):
        return pair_slot_of(self.grid_cols, row * self.grid_cols + col)

    def tile(self, member, row, col):
        return self.pairs[self.pair_slot(row, col), member].reshape(self.size, HD)

    def scores(self, row, col, cols):
        query = self.query[self.slot(row, col), pl.ds(0, self.tile_rows)].reshape(self.size, HD)
        frames = range(self.pairs.shape[1] // 2)
        up, down = row > 0, row + 1 < self.grid_rows
        rows = [r for r in (row - 1, row, row + 1) if 0 <= r < self.grid_rows]
        needed = [(f, r, i) for f in frames for i in range(len(cols)) for r in rows]
        keys = jnp.concatenate([self.tile(2 * f, r, cols[i][0]) for f, r, i in needed], axis=0)
        raw = lax.dot_general(query, keys, (((1,), (1,)), ((), ())), preferred_element_type=jnp.float32)
        scores = {key: raw[:, i * self.size : (i + 1) * self.size] for i, key in enumerate(needed)}
        blocks = []
        for f in frames:
            for i, (c, allowed) in enumerate(cols):
                found = [(False, scores[f, row, i])]
                if up or down:
                    above = scores[f, row - 1, i] if up else NEG
                    found.append((True, jnp.where(self.upper, above, scores[f, row + 1, i] if down else NEG)))
                for off_row, block in found:
                    if allowed is not None:
                        block = jnp.where(allowed, block, NEG)
                    blocks.append((f, off_row, c, block))
        top = blocks[0][3]
        for entry in blocks[1:]:
            top = jnp.maximum(top, entry[3])
        return row, up and down, down, blocks, jnp.max(top, axis=1, keepdims=True)

    def weigh(self, row, both, down, blocks, top):
        parts = []
        for f, off_row, c, block in blocks:
            weights = jnp.exp2((block - top) * self.scale).astype(jnp.bfloat16)
            if off_row and both:
                parts.append((f, row - 1, c, weights * self.upper_one))
                parts.append((f, row + 1, c, weights * (1 - self.upper_one)))
            elif off_row:
                parts.append((f, row + 1 if down else row - 1, c, weights))
            else:
                parts.append((f, row, c, weights))
        values = jnp.concatenate([self.tile(2 * f + 1, r, c) for f, r, c, _ in parts], axis=0)
        values = jnp.concatenate([values, jnp.ones_like(values)], axis=1)
        weights = jnp.concatenate([part for _, _, _, part in parts], axis=1)
        total = jnp.dot(weights, values, preferred_element_type=jnp.float32)
        return total[:, :HD] / total[:, HD:], top * self.scale + jnp.log2(total[:, HD:])

    def attend(self, tiles):
        held = None
        for place in [*tiles, None]:
            ready = self.scores(*place) if place else None
            if held:
                yield (held[0][0] * self.grid_cols + held[0][1], *self.weigh(*held[1]))
            held = (place, ready)

    def enhanced(self, row, col, weight_ref, bias_ref, beyond):
        shape = (self.tile_cols, HD)
        sub = lax.broadcasted_iota(jnp.int32, shape, 0)
        taps = [[weight_ref[a, pl.ds(b, 1), :] for b in range(3)] for a in range(3)]
        last = self.tile_cols - 1
        member = self.pairs.shape[1] - 1
        lines = []
        for key_row in range(row * self.tile_rows - 1, (row + 1) * self.tile_rows + 1):
            tile_row, line = key_row // self.tile_rows, key_row % self.tile_rows
            if tile_row < 0 or tile_row >= self.grid_rows:
                lines.append(None)
                continue

            def values(c):
                return self.pairs[self.pair_slot(tile_row, c), member, line].astype(jnp.float32)

            def edge(right, c):
                place = self.slot(tile_row, c), self.tile_rows + line // self.tile_cols
                first, second = (ref[place].astype(jnp.float32) for ref in beyond)
                packed = jnp.where(first_is_right() == right, first, second)
                return jnp.broadcast_to(packed[line % self.tile_cols : line % self.tile_cols + 1], shape)

            here = values(col)
            before = pltpu.roll(values(col - 1), 1, 0) if col > 0 else edge(0, self.grid_cols - 1)
            after = pltpu.roll(values(col + 1), last, 0) if col + 1 < self.grid_cols else edge(1, 0)
            low = jnp.where(sub == 0, before, pltpu.roll(here, 1, 0))
            high = jnp.where(sub == last, after, pltpu.roll(here, last, 0))
            lines.append((low, here, high))
        sums = []
        for line in range(self.tile_rows):
            total = jnp.broadcast_to(bias_ref[...], shape)
            for a in range(3):
                if lines[line + a] is not None:
                    for b in range(3):
                        total = total + lines[line + a][b] * taps[a][b]
            sums.append(total)
        return jnp.stack(sums, axis=0)


def visit_kernel(grid, tile, first, query_ref, pairs_ref, out_ref):
    window = Window(grid, tile, query_ref, pairs_ref)
    near = first_is_right() if first else 1 - first_is_right()
    allowed = window.left.astype(jnp.int32) == near
    tiles = []
    for row in range(grid[0]):
        tiles.append((row, 1 - near, [(near, None), (1 - near, allowed)]))
        tiles.append((row, near, [(near, allowed)]))
    size, count = window.size, grid[0] * grid[1]
    lane = lax.broadcasted_iota(jnp.int32, (size, HD), 1)
    levels = jnp.zeros((size, HD), jnp.float32)
    for index, part, level in window.attend(tiles):
        out_ref[index] = part.reshape(tile + (HD,)).astype(jnp.bfloat16)
        levels = jnp.where(lane == index, level, levels)
    high = levels.astype(jnp.bfloat16).astype(jnp.float32)
    middle = (levels - high).astype(jnp.bfloat16).astype(jnp.float32)
    packed = high + pltpu.roll(middle, count, 1) + pltpu.roll(levels - high - middle, 2 * count, 1)
    out_ref[count] = packed.reshape(tile + (HD,)).astype(jnp.bfloat16)


def own_kernel(
    grid, tile, weight_ref, bias_ref, query_ref, pairs_ref, first_ref, second_ref, part_ref, level_ref, conv_ref
):
    window = Window(grid, tile, query_ref, pairs_ref)
    cols = [(c, None) for c in range(grid[1])]
    tiles = [(row, col, cols) for row in range(grid[0]) for col in range(grid[1])]
    for index, part, level in window.attend(tiles):
        part_ref[index], level_ref[index] = part, level
        row, col = index // grid[1], index % grid[1]
        conv = window.enhanced(row, col, weight_ref, bias_ref, (first_ref, second_ref))
        conv_ref[index] = conv.reshape(window.size, HD)


def join_kernel(grid, tile, far, part_ref, level_ref, conv_ref, first_ref, second_ref, out_ref):
    size, count = tile[0] * tile[1], grid[0] * grid[1]
    visits = (first_ref, second_ref)
    place = lax.axis_index("far")
    even = lax.rem(place, 2) == 0
    present = [~even | (place < far - 1), jnp.where(even, place > 0, place < far - 1)]
    packed = []
    for there, ref in zip(present, visits):
        pack = ref[count].reshape(size, HD).astype(jnp.float32)
        level = pack + pltpu.roll(pack, HD - count, 1) + pltpu.roll(pack, HD - 2 * count, 1)
        packed.append(jnp.where(there, level, NEG))
    for index in range(count):
        levels = [level_ref[index]]
        parts = [part_ref[index]]
        for ref, pack in zip(visits, packed):
            parts.append(ref[index].reshape(size, HD).astype(jnp.float32))
            levels.append(jnp.broadcast_to(pack[:, index : index + 1], (size, HD)))
        top = jnp.maximum(jnp.maximum(levels[0], levels[1]), levels[2])
        shares = [jnp.exp2(level - top) for level in levels]
        mixed = sum(share * part for share, part in zip(shares, parts)) / sum(shares)
        out_ref[slot_of(grid[1], index)] = (mixed + conv_ref[index]).reshape(tile + (HD,)).astype(jnp.bfloat16)


def lanes(head):
    return pl.ds(pl.multiple_of(head * HD, HD), HD)


def pack_kernel(flips, side, *refs):
    count = len(flips)
    sources, buffers = refs[: -count - 4], refs[-count - 4 : -4]
    same_ref, beside_ref, held_ref, sems = refs[-4:]
    tile_rows, tile_cols, _ = sources[0].shape
    copies = [pltpu.make_async_copy(x, held_ref.at[i], sems.at[i]) for i, x in enumerate(sources)]
    for copy in copies:
        copy.start()
    heads = [[lanes(position(side) ^ (flip ^ beside)) for beside in (0, side)] for flip in flips]
    copies[0].wait()
    for buffer, pair in zip(buffers, heads):
        for other in range(2):
            buffer[other, pl.ds(0, tile_rows)] = held_ref[0, :, :, pair[other]]
    copies[1].wait()
    sub = lax.broadcasted_iota(jnp.int32, (tile_cols, HD), 0)
    for buffer, pair in zip(buffers, heads):
        for other in range(2):
            for start in range(0, tile_rows, tile_cols):
                packed = jnp.zeros((tile_cols, HD), jnp.float32)
                for line in range(tile_cols):
                    values = held_ref[1, start + line, :, pair[other]].astype(jnp.float32)
                    edge = jnp.where(lax.axis_index("near") == 0, values[:1], values[tile_cols - 1 :])
                    packed = jnp.where(sub == line, edge, packed)
                buffer[other, tile_rows + start // tile_cols] = packed.astype(jnp.bfloat16)
    for member, source in enumerate((*range(2, len(sources)), 1)):
        if source != 1:
            copies[source].wait()
        for i, pair in enumerate(heads):
            same_ref[i, member] = held_ref[source, :, :, pair[0]]
            beside_ref[i, member] = held_ref[source, :, :, pair[1]]


def unpack_kernel(flips, side, same_ref, beside_ref, *refs):
    out_ref = refs[-1]
    out_ref[:, :, lanes(position(side))] = same_ref[0]
    out_ref[:, :, lanes(position(side) ^ side)] = beside_ref[0]
    for i, flip in enumerate(flips[1:]):
        out_ref[:, :, lanes(position(side) ^ flip)] = refs[i][0]
        out_ref[:, :, lanes(position(side) ^ (flip ^ side))] = refs[i][1]


def head_step(shape, queries, keys_new, values_new, keys_cache, values_cache, conv_weight, conv_bias):
    group_rows, group_cols, far = shape
    tile_rows, tile_cols, channels = queries.shape
    heads = channels // HD
    grid, tile = (group_rows, group_cols), (tile_rows, tile_cols)
    size = tile_rows * tile_cols
    axes = ("ht", "near")
    block = (tile_rows, tile_cols, HD)
    side = group_cols
    flips = [flip for flip in range(heads) if not flip & side]
    near = lax.axis_index("near").astype(jnp.int32)
    me = lax.axis_index("ht").astype(jnp.int32) * group_cols + near

    def swap(x, flip):
        return lax.ppermute(x, axes, [(s, s ^ flip) for s in range(heads)])

    def call(kernel, out_shape, params, cost, *operands, space=(VMEM, VMEM), scratch=()):
        return pl.pallas_call(
            kernel,
            out_shape=out_shape,
            in_specs=[space[0]] * len(operands),
            out_specs=jax.tree.map(lambda _: space[1], out_shape),
            scratch_shapes=scratch,
            compiler_params=params,
            cost_estimate=pl.CostEstimate(flops=cost << 30, bytes_accessed=1 << 20, transcendentals=0),
        )(*operands)

    def stay(x):
        return pltpu.with_memory_space_constraint(x, pltpu.HBM)

    def send(buffers):
        got = [buffers[0]]
        for i in range(1, len(flips)):
            got.append(swap(buffers[i], flips[i]))
        return got

    def rounds(start):
        return [pair for i in range(start, far - 1, 2) for pair in ((i, i + 1), (i + 1, i))]

    first, second = rounds(0), rounds(1)
    edges = -(-tile_rows // tile_cols)

    sources = (queries, values_new, keys_cache[0], values_cache[0], keys_new)
    query_buffer = jax.ShapeDtypeStruct((2, tile_rows + edges, tile_cols, HD), jnp.bfloat16)
    pair_buffer = jax.ShapeDtypeStruct((len(flips), len(sources) - 1) + block, jnp.bfloat16)
    packed = call(
        functools.partial(pack_kernel, flips, side),
        [query_buffer] * len(flips) + [pair_buffer] * 2,
        SMALL,
        0,
        *map(stay, sources),
        space=(FAR, VMEM),
        scratch=[pltpu.VMEM((len(sources),) + queries.shape, jnp.bfloat16), pltpu.SemaphoreType.DMA((len(sources),))],
    )
    same, beside = packed[len(flips) :]
    beside = swap(beside, side)
    got = send(packed[: len(flips)])
    both = [jnp.stack([same[i], beside[i]]) for i in range(len(flips))]
    pairs = send(both)
    pairs = jnp.concatenate(pairs, axis=0)
    forward = jnp.stack([b[1] for b in got])
    forward = swap(forward, side)
    query = jnp.concatenate([jnp.stack([b[0] for b in got]), forward], axis=0)
    query_second = lax.ppermute(query, "far", second)
    query_first = lax.ppermute(query, "far", first)
    weight = lax.dynamic_slice_in_dim(conv_weight, me * HD, HD, 2)
    bias = lax.dynamic_slice_in_dim(conv_bias.reshape(1, channels), me * HD, HD, 1)

    def visit(queries, is_first):
        kernel = functools.partial(visit_kernel, grid, tile, is_first)
        return call(kernel, jax.ShapeDtypeStruct((heads + 1,) + block, jnp.bfloat16), LIMIT, 4, queries, pairs)

    part = visit(query_second, False)
    home_second = lax.ppermute(part, "far", second)
    part = visit(query_first, True)
    home_first = lax.ppermute(part, "far", first)
    part = jax.ShapeDtypeStruct((heads, size, HD), jnp.float32)
    kernel = functools.partial(own_kernel, grid, tile)
    own = call(kernel, [part] * 3, LIMIT, 4, weight, bias, query, pairs, query_first, query_second)
    kernel = functools.partial(join_kernel, grid, tile, far)
    result = jax.ShapeDtypeStruct((heads,) + block, jnp.bfloat16)
    result = call(kernel, result, LIMIT, 1, *own, home_first, home_second)
    same, other = result[: len(flips)], result[len(flips) :]
    received = swap(other, side)
    got = []
    for i in range(1, len(flips)):
        got.append(swap(jnp.stack([same[i], received[i]]), flips[i]))
    return call(
        functools.partial(unpack_kernel, flips, side),
        jax.ShapeDtypeStruct(queries.shape, jnp.bfloat16),
        SMALL,
        0,
        same,
        received,
        *got,
    )


def grouping(mesh, heads):
    rows, cols = mesh.shape["ht"], mesh.shape["wt"]
    group_rows = rows
    group_cols = heads // group_rows if heads % group_rows == 0 else 0
    if group_cols != 2 or cols % group_cols:
        return None
    return group_rows, group_cols, cols // group_cols


def solution(mesh):
    def program(queries, *rest):
        heads = queries.shape[2] // HD
        shape = grouping(mesh, heads)
        if shape is None or queries.shape[0] != mesh.shape["ht"] * (WIN // 2) or queries.shape[1] != mesh.shape["wt"] * (WIN // 4):
            placed = (P("ht", "wt", None),) * 3 + (P(None, "ht", "wt", None),) * 2 + (P(), P())
            return jax.shard_map(
                shards, mesh=mesh, in_specs=placed, out_specs=P("ht", "wt", None), check_vma=False
            )(queries, *rest)
        devices = mesh.devices.reshape(shape[0], shape[2], shape[1])
        split = Mesh(devices, ("ht", "far", "near"))
        tile = P("ht", ("far", "near"), None)
        past = P(None, "ht", ("far", "near"), None)
        step = jax.shard_map(
            functools.partial(head_step, shape),
            mesh=split,
            in_specs=(tile, tile, tile, past, past, P(), P()),
            out_specs=tile,
            check_vma=False,
        )
        return step(queries, *rest)

    return program
```

```python
import functools

import jax
import jax.numpy as jnp
from jax import lax
from jax.experimental import pallas as pl
from jax.experimental.pallas import tpu as pltpu
from jax.sharding import Mesh, PartitionSpec as P


HD = 128
WIN = 32


def with_halo(block, sides, width):
    for axis, dim in sides:
        count = lax.axis_size(axis)
        forward = [(i, i + 1) for i in range(count - 1)]
        backward = [(target, source) for source, target in forward]
        low = lax.ppermute(
            lax.slice_in_dim(block, block.shape[dim] - width, None, axis=dim), axis, forward
        )
        high = lax.ppermute(lax.slice_in_dim(block, 0, width, axis=dim), axis, backward)
        block = jnp.concatenate([low, block, high], axis=dim)
    return block


def window_allowed(row_start, col_start, frame_rows, frame_cols, tile_rows, tile_cols, half_win):
    ext_rows = jnp.arange(tile_rows + 2 * half_win, dtype=jnp.int32) - half_win
    ext_cols = jnp.arange(tile_cols + 2 * half_win, dtype=jnp.int32) - half_win
    query_rows = jnp.arange(tile_rows, dtype=jnp.int32)
    query_cols = jnp.arange(tile_cols, dtype=jnp.int32)
    row_delta = ext_rows[None, :] - query_rows[:, None]
    col_delta = ext_cols[None, :] - query_cols[:, None]
    global_rows = row_start + ext_rows
    global_cols = col_start + ext_cols
    row_valid = (
        (row_delta >= -half_win)
        & (row_delta < half_win)
        & ((global_rows >= 0) & (global_rows < frame_rows))[None, :]
    )
    col_valid = (
        (col_delta >= -half_win)
        & (col_delta < half_win)
        & ((global_cols >= 0) & (global_cols < frame_cols))[None, :]
    )
    allowed = row_valid[:, None, :, None] & col_valid[None, :, None, :]
    return allowed.reshape(
        tile_rows * tile_cols, (tile_rows + 2 * half_win) * (tile_cols + 2 * half_win)
    )


def attend(query_rows, keys_flat, values_flat, allowed, heads, head_dim):
    score_scale = head_dim ** (-0.5)

    def one_head(head_index):
        scores = (
            jnp.einsum("qd,kd->qk", query_rows, keys_flat, preferred_element_type=jnp.float32)
            * score_scale
        )
        scores = jnp.where(allowed, scores, -1e30)
        row_top = jnp.max(scores, axis=1, keepdims=True)
        weights_f = jnp.exp(scores - row_top)
        denominator = jnp.sum(weights_f, axis=1, keepdims=True)
        numerator = jnp.dot(
            weights_f.astype(jnp.bfloat16), values_flat, preferred_element_type=jnp.float32
        )
        return numerator / denominator

    outputs = lax.map(one_head, jnp.arange(heads, dtype=jnp.int32))
    return outputs.transpose(1, 0, 2).reshape(query_rows.shape[0], heads * head_dim)


def local_conv(padded, conv_weight, conv_bias, tile_rows, tile_cols):
    enhanced = jnp.zeros((tile_rows, tile_cols, padded.shape[2]), jnp.float32) + conv_bias
    for row_shift in range(3):
        for col_shift in range(3):
            enhanced = (
                enhanced
                + padded[
                    row_shift : row_shift + tile_rows, col_shift : col_shift + tile_cols
                ].astype(jnp.float32)
                * conv_weight[row_shift, col_shift]
            )
    return enhanced


def cycle_conv(values_new, conv_weight, conv_bias):
    tile_rows, tile_cols, _ = values_new.shape
    padded = with_halo(values_new, (("ht", 0), ("wt", 1)), 1)
    return local_conv(padded, conv_weight, conv_bias, tile_rows, tile_cols)


def shards(queries, keys_new, values_new, keys_cache, values_cache, conv_weight, conv_bias):
    tile_rows, tile_cols, channels = queries.shape
    frames = keys_cache.shape[0] + 1
    half_win = WIN // 2
    stacked = jnp.concatenate([keys_cache, keys_new[None], values_cache, values_new[None]], axis=0)
    row_start = lax.axis_index("ht") * tile_rows
    frame_rows = tile_rows * lax.axis_size("ht")
    frame_cols = tile_cols * lax.axis_size("wt")
    heads = channels // HD
    copies = lax.axis_size("wt") // heads
    bundle = jnp.concatenate([stacked, queries[None]], axis=0)
    members = bundle.shape[0]
    spread = bundle.reshape(members, tile_rows, tile_cols, 1, heads, HD)
    spread = jnp.broadcast_to(spread, (members, tile_rows, tile_cols, copies, heads, HD))
    spread = spread.reshape(members, tile_rows, tile_cols, copies * heads, HD)
    strips = lax.all_to_all(spread, "wt", split_axis=3, concat_axis=2, tiled=True)
    strips = strips.reshape(members, tile_rows, frame_cols, HD)
    device_index = lax.axis_index("wt")
    my_group = device_index // heads
    block_width = tile_cols * heads
    block_start = my_group * block_width
    padded_cols = jnp.pad(strips, ((0, 0), (0, 0), (half_win, half_win), (0, 0)))
    window = lax.dynamic_slice_in_dim(padded_cols, block_start, block_width + 2 * half_win, 2)
    query_part = window[2 * frames, :, half_win : half_win + block_width]
    region = with_halo(window[: 2 * frames], (("ht", 1),), half_win)

    def one_block(step):
        offset = step * tile_cols
        query_block = lax.dynamic_slice_in_dim(query_part, offset, tile_cols, 1).reshape(
            tile_rows * tile_cols, HD
        )
        sub = lax.dynamic_slice_in_dim(region, offset, tile_cols + 2 * half_win, 2)
        keys_flat = sub[:frames].reshape(-1, HD)
        values_flat = sub[frames:].reshape(-1, HD)
        allowed = window_allowed(
            row_start, block_start + offset, frame_rows, frame_cols, tile_rows, tile_cols, half_win
        )
        allowed = jnp.tile(allowed, (1, frames))
        result = attend(query_block, keys_flat, values_flat, allowed, 1, HD)
        return result.reshape(tile_rows, tile_cols, HD)

    blocks = lax.map(one_block, jnp.arange(heads, dtype=jnp.int32))
    payload = blocks.transpose(1, 0, 2, 3)
    payload = jnp.broadcast_to(payload[:, None], (tile_rows, copies, heads, tile_cols, HD))
    payload = payload.reshape(tile_rows, copies * heads, tile_cols, HD)
    returned = lax.all_to_all(
        payload.astype(jnp.bfloat16), "wt", split_axis=1, concat_axis=1, tiled=True
    ).astype(payload.dtype)
    own = lax.dynamic_slice_in_dim(returned, my_group * heads, heads, 1)
    combined = own.transpose(0, 2, 1, 3).reshape(tile_rows, tile_cols, channels)
    combined = combined + cycle_conv(values_new, conv_weight, conv_bias)
    return combined.astype(jnp.bfloat16)


LOG2E = 1.4426950408889634
NEG = -1e30
VMEM = pl.BlockSpec(memory_space=pltpu.VMEM)
FAR = pl.BlockSpec(memory_space=pltpu.HBM)
LIMIT = pltpu.CompilerParams(vmem_limit_bytes=8 * 1024 * 1024)
SMALL = pltpu.CompilerParams(vmem_limit_bytes=4 * 1024 * 1024)


def position(group_cols):
    return lax.axis_index("ht") * group_cols + lax.axis_index("near")


def place_of(group_cols, tile):
    side = group_cols
    flip = position(group_cols) ^ tile
    return lax.rem(flip // side, 2), lax.rem(flip, side) + flip // (2 * side) * side


def slot_of(group_cols, tile):
    beside, order = place_of(group_cols, tile)
    return beside * (lax.axis_size("ht") * group_cols // 2) + order


def pair_slot_of(group_cols, tile):
    beside, order = place_of(group_cols, tile)
    return order * 2 + beside


def first_is_right():
    return 1 - lax.rem(lax.axis_index("far"), 2)


class Window:
    def __init__(self, grid, tile, query_ref, pairs_ref):
        self.grid_rows, self.grid_cols = grid
        self.tile_rows, self.tile_cols = tile
        self.size = self.tile_rows * self.tile_cols
        self.query, self.pairs = query_ref, pairs_ref
        self.scale = HD ** (-0.5) * LOG2E
        query = lax.broadcasted_iota(jnp.int32, (self.size, self.size), 0)
        key = lax.broadcasted_iota(jnp.int32, (self.size, self.size), 1)
        self.upper = key // self.tile_cols >= query // self.tile_cols
        self.left = key % self.tile_cols >= query % self.tile_cols
        self.upper_one = self.upper.astype(jnp.float32).astype(jnp.bfloat16)

    def slot(self, row, col):
        return slot_of(self.grid_cols, row * self.grid_cols + col)

    def pair_slot(self, row, col):
        return pair_slot_of(self.grid_cols, row * self.grid_cols + col)

    def tile(self, member, row, col):
        return self.pairs[self.pair_slot(row, col), member].reshape(self.size, HD)

    def scores(self, row, col, cols):
        query = self.query[self.slot(row, col), pl.ds(0, self.tile_rows)].reshape(self.size, HD)
        frames = range(self.pairs.shape[1] // 2)
        up, down = row > 0, row + 1 < self.grid_rows
        rows = [r for r in (row - 1, row, row + 1) if 0 <= r < self.grid_rows]
        needed = [(f, r, i) for f in frames for i in range(len(cols)) for r in rows]
        keys = jnp.concatenate([self.tile(2 * f, r, cols[i][0]) for f, r, i in needed], axis=0)
        raw = lax.dot_general(query, keys, (((1,), (1,)), ((), ())), preferred_element_type=jnp.float32)
        scores = {key: raw[:, i * self.size : (i + 1) * self.size] for i, key in enumerate(needed)}
        blocks = []
        for f in frames:
            for i, (c, allowed) in enumerate(cols):
                found = [(False, scores[f, row, i])]
                if up or down:
                    above = scores[f, row - 1, i] if up else NEG
                    found.append((True, jnp.where(self.upper, above, scores[f, row + 1, i] if down else NEG)))
                for off_row, block in found:
                    if allowed is not None:
                        block = jnp.where(allowed, block, NEG)
                    blocks.append((f, off_row, c, block))
        top = blocks[0][3]
        for entry in blocks[1:]:
            top = jnp.maximum(top, entry[3])
        return row, up and down, down, blocks, jnp.max(top, axis=1, keepdims=True)

    def weigh(self, row, both, down, blocks, top):
        parts = []
        for f, off_row, c, block in blocks:
            weights = jnp.exp2((block - top) * self.scale).astype(jnp.bfloat16)
            if off_row and both:
                parts.append((f, row - 1, c, weights * self.upper_one))
                parts.append((f, row + 1, c, weights * (1 - self.upper_one)))
            elif off_row:
                parts.append((f, row + 1 if down else row - 1, c, weights))
            else:
                parts.append((f, row, c, weights))
        values = jnp.concatenate([self.tile(2 * f + 1, r, c) for f, r, c, _ in parts], axis=0)
        values = jnp.concatenate([values, jnp.ones_like(values)], axis=1)
        weights = jnp.concatenate([part for _, _, _, part in parts], axis=1)
        total = jnp.dot(weights, values, preferred_element_type=jnp.float32)
        return total[:, :HD] / total[:, HD:], top * self.scale + jnp.log2(total[:, HD:])

    def attend(self, tiles):
        held = None
        for place in [*tiles, None]:
            ready = self.scores(*place) if place else None
            if held:
                yield (held[0][0] * self.grid_cols + held[0][1], *self.weigh(*held[1]))
            held = (place, ready)

    def enhanced(self, row, col, weight_ref, bias_ref, beyond):
        shape = (self.tile_cols, HD)
        sub = lax.broadcasted_iota(jnp.int32, shape, 0)
        taps = [[weight_ref[a, pl.ds(b, 1), :] for b in range(3)] for a in range(3)]
        last = self.tile_cols - 1
        member = self.pairs.shape[1] - 1
        lines = []
        for key_row in range(row * self.tile_rows - 1, (row + 1) * self.tile_rows + 1):
            tile_row, line = key_row // self.tile_rows, key_row % self.tile_rows
            if tile_row < 0 or tile_row >= self.grid_rows:
                lines.append(None)
                continue

            def values(c):
                return self.pairs[self.pair_slot(tile_row, c), member, line].astype(jnp.float32)

            def edge(right, c):
                place = self.slot(tile_row, c), self.tile_rows + line // self.tile_cols
                first, second = (ref[place].astype(jnp.float32) for ref in beyond)
                packed = jnp.where(first_is_right() == right, first, second)
                return jnp.broadcast_to(packed[line % self.tile_cols : line % self.tile_cols + 1], shape)

            here = values(col)
            before = pltpu.roll(values(col - 1), 1, 0) if col > 0 else edge(0, self.grid_cols - 1)
            after = pltpu.roll(values(col + 1), last, 0) if col + 1 < self.grid_cols else edge(1, 0)
            low = jnp.where(sub == 0, before, pltpu.roll(here, 1, 0))
            high = jnp.where(sub == last, after, pltpu.roll(here, last, 0))
            lines.append((low, here, high))
        sums = []
        for line in range(self.tile_rows):
            total = jnp.broadcast_to(bias_ref[...], shape)
            for a in range(3):
                if lines[line + a] is not None:
                    for b in range(3):
                        total = total + lines[line + a][b] * taps[a][b]
            sums.append(total)
        return jnp.stack(sums, axis=0)


def visit_kernel(grid, tile, first, query_ref, pairs_ref, out_ref):
    window = Window(grid, tile, query_ref, pairs_ref)
    near = first_is_right() if first else 1 - first_is_right()
    allowed = window.left.astype(jnp.int32) == near
    tiles = []
    for row in range(grid[0]):
        tiles.append((row, 1 - near, [(near, None), (1 - near, allowed)]))
        tiles.append((row, near, [(near, allowed)]))
    size, count = window.size, grid[0] * grid[1]
    lane = lax.broadcasted_iota(jnp.int32, (size, HD), 1)
    levels = jnp.zeros((size, HD), jnp.float32)
    for index, part, level in window.attend(tiles):
        out_ref[index] = part.reshape(tile + (HD,)).astype(jnp.bfloat16)
        levels = jnp.where(lane == index, level, levels)
    high = levels.astype(jnp.bfloat16).astype(jnp.float32)
    middle = (levels - high).astype(jnp.bfloat16).astype(jnp.float32)
    packed = high + pltpu.roll(middle, count, 1) + pltpu.roll(levels - high - middle, 2 * count, 1)
    out_ref[count] = packed.reshape(tile + (HD,)).astype(jnp.bfloat16)


def own_kernel(
    grid, tile, weight_ref, bias_ref, query_ref, pairs_ref, first_ref, second_ref, part_ref, level_ref, conv_ref
):
    window = Window(grid, tile, query_ref, pairs_ref)
    cols = [(c, None) for c in range(grid[1])]
    tiles = [(row, col, cols) for row in range(grid[0]) for col in range(grid[1])]
    for index, part, level in window.attend(tiles):
        part_ref[index], level_ref[index] = part, level
        row, col = index // grid[1], index % grid[1]
        conv = window.enhanced(row, col, weight_ref, bias_ref, (first_ref, second_ref))
        conv_ref[index] = conv.reshape(window.size, HD)


def join_kernel(grid, tile, far, part_ref, level_ref, conv_ref, first_ref, second_ref, out_ref):
    size, count = tile[0] * tile[1], grid[0] * grid[1]
    visits = (first_ref, second_ref)
    place = lax.axis_index("far")
    even = lax.rem(place, 2) == 0
    present = [~even | (place < far - 1), jnp.where(even, place > 0, place < far - 1)]
    packed = []
    for there, ref in zip(present, visits):
        pack = ref[count].reshape(size, HD).astype(jnp.float32)
        level = pack + pltpu.roll(pack, HD - count, 1) + pltpu.roll(pack, HD - 2 * count, 1)
        packed.append(jnp.where(there, level, NEG))
    for index in range(count):
        levels = [level_ref[index]]
        parts = [part_ref[index]]
        for ref, pack in zip(visits, packed):
            parts.append(ref[index].reshape(size, HD).astype(jnp.float32))
            levels.append(jnp.broadcast_to(pack[:, index : index + 1], (size, HD)))
        top = jnp.maximum(jnp.maximum(levels[0], levels[1]), levels[2])
        shares = [jnp.exp2(level - top) for level in levels]
        mixed = sum(share * part for share, part in zip(shares, parts)) / sum(shares)
        out_ref[slot_of(grid[1], index)] = (mixed + conv_ref[index]).reshape(tile + (HD,)).astype(jnp.bfloat16)


def lanes(head):
    return pl.ds(pl.multiple_of(head * HD, HD), HD)


def pack_kernel(flips, side, *refs):
    count = len(flips)
    sources, buffers = refs[: -2 * count - 3], refs[-2 * count - 3 : -count - 3]
    messages, (beside_ref, held_ref, sems) = refs[-count - 3 : -3], refs[-3:]
    tile_rows, tile_cols, _ = sources[0].shape
    copies = [pltpu.make_async_copy(x, held_ref.at[i], sems.at[i]) for i, x in enumerate(sources)]
    for copy in copies:
        copy.start()
    heads = [[lanes(position(side) ^ (flip ^ beside)) for beside in (0, side)] for flip in flips]
    copies[0].wait()
    for buffer, pair in zip(buffers, heads):
        for other in range(2):
            buffer[other, pl.ds(0, tile_rows)] = held_ref[0, :, :, pair[other]]
    copies[1].wait()
    sub = lax.broadcasted_iota(jnp.int32, (tile_cols, HD), 0)
    for buffer, pair in zip(buffers, heads):
        for other in range(2):
            for start in range(0, tile_rows, tile_cols):
                packed = jnp.zeros((tile_cols, HD), jnp.float32)
                for line in range(tile_cols):
                    values = held_ref[1, start + line, :, pair[other]].astype(jnp.float32)
                    edge = jnp.where(lax.axis_index("near") == 0, values[:1], values[tile_cols - 1 :])
                    packed = jnp.where(sub == line, edge, packed)
                buffer[other, tile_rows + start // tile_cols] = packed.astype(jnp.bfloat16)
    for member, source in enumerate((*range(2, len(sources)), 1)):
        if source != 1:
            copies[source].wait()
        for i, pair in enumerate(heads):
            messages[i][0, member] = held_ref[source, :, :, pair[0]]
            beside_ref[i, member] = held_ref[source, :, :, pair[1]]


def split_kernel(*refs):
    mine_ref, other_ref = refs[-2:]
    for i, ref in enumerate(refs[:-2]):
        mine_ref[i] = ref[0]
        other_ref[i] = ref[1]


def unpack_kernel(flips, side, same_ref, beside_ref, *refs):
    out_ref = refs[-1]
    out_ref[:, :, lanes(position(side))] = same_ref[0]
    out_ref[:, :, lanes(position(side) ^ side)] = beside_ref[0]
    for i, flip in enumerate(flips[1:]):
        out_ref[:, :, lanes(position(side) ^ flip)] = refs[i][0]
        out_ref[:, :, lanes(position(side) ^ (flip ^ side))] = refs[i][1]


def head_step(shape, queries, keys_new, values_new, keys_cache, values_cache, conv_weight, conv_bias):
    group_rows, group_cols, far = shape
    tile_rows, tile_cols, channels = queries.shape
    heads = channels // HD
    grid, tile = (group_rows, group_cols), (tile_rows, tile_cols)
    size = tile_rows * tile_cols
    axes = ("ht", "near")
    block = (tile_rows, tile_cols, HD)
    side = group_cols
    flips = [flip for flip in range(heads) if not flip & side]
    near = lax.axis_index("near").astype(jnp.int32)
    me = lax.axis_index("ht").astype(jnp.int32) * group_cols + near

    def swap(x, flip):
        return lax.ppermute(x, axes, [(s, s ^ flip) for s in range(heads)])

    def call(kernel, out_shape, params, cost, *operands, space=(VMEM, VMEM), scratch=()):
        return pl.pallas_call(
            kernel,
            out_shape=out_shape,
            in_specs=[space[0]] * len(operands),
            out_specs=jax.tree.map(lambda _: space[1], out_shape),
            scratch_shapes=scratch,
            compiler_params=params,
            cost_estimate=pl.CostEstimate(flops=cost << 30, bytes_accessed=1 << 20, transcendentals=0),
        )(*operands)

    def stay(x):
        return pltpu.with_memory_space_constraint(x, pltpu.HBM)

    def send(buffers):
        got = [buffers[0]]
        for i in range(1, len(flips)):
            got.append(swap(buffers[i], flips[i]))
        return got

    def rounds(start):
        return [pair for i in range(start, far - 1, 2) for pair in ((i, i + 1), (i + 1, i))]

    first, second = rounds(0), rounds(1)
    edges = -(-tile_rows // tile_cols)

    sources = (queries, values_new, keys_cache[0], values_cache[0], keys_new)
    query_buffer = jax.ShapeDtypeStruct((2, tile_rows + edges, tile_cols, HD), jnp.bfloat16)
    message = jax.ShapeDtypeStruct((2, len(sources) - 1) + block, jnp.bfloat16)
    beside = jax.ShapeDtypeStruct((len(flips), len(sources) - 1) + block, jnp.bfloat16)
    packed = call(
        functools.partial(pack_kernel, flips, side),
        [query_buffer] * len(flips) + [message] * len(flips) + [beside],
        SMALL,
        0,
        *map(stay, sources),
        space=(FAR, VMEM),
        scratch=[pltpu.VMEM((len(sources),) + queries.shape, jnp.bfloat16), pltpu.SemaphoreType.DMA((len(sources),))],
    )
    beside = swap(packed[-1], side)
    got = send(packed[: len(flips)])
    messages = packed[len(flips) : -1]
    both = [lax.dynamic_update_slice_in_dim(m, beside[i : i + 1], 1, 0) for i, m in enumerate(messages)]
    pairs = send(both)
    pairs = jnp.concatenate(pairs, axis=0)
    half = jax.ShapeDtypeStruct((len(flips),) + query_buffer.shape[1:], jnp.bfloat16)
    mine, forward = call(split_kernel, [half, half], SMALL, 0, *got)
    forward = swap(forward, side)
    query = jnp.concatenate([mine, forward], axis=0)
    query_second = lax.ppermute(query, "far", second)
    query_first = lax.ppermute(query, "far", first)
    weight = lax.dynamic_slice_in_dim(conv_weight, me * HD, HD, 2)
    bias = lax.dynamic_slice_in_dim(conv_bias.reshape(1, channels), me * HD, HD, 1)

    def visit(queries, is_first):
        kernel = functools.partial(visit_kernel, grid, tile, is_first)
        return call(kernel, jax.ShapeDtypeStruct((heads + 1,) + block, jnp.bfloat16), LIMIT, 4, queries, pairs)

    part = visit(query_second, False)
    home_second = lax.ppermute(part, "far", second)
    part = visit(query_first, True)
    home_first = lax.ppermute(part, "far", first)
    part = jax.ShapeDtypeStruct((heads, size, HD), jnp.float32)
    kernel = functools.partial(own_kernel, grid, tile)
    own = call(kernel, [part] * 3, LIMIT, 4, weight, bias, query, pairs, query_first, query_second)
    kernel = functools.partial(join_kernel, grid, tile, far)
    result = jax.ShapeDtypeStruct((heads,) + block, jnp.bfloat16)
    result = call(kernel, result, LIMIT, 1, *own, home_first, home_second)
    same, other = result[: len(flips)], result[len(flips) :]
    received = swap(other, side)
    got = []
    for i in range(1, len(flips)):
        got.append(swap(jnp.stack([same[i], received[i]]), flips[i]))
    return call(
        functools.partial(unpack_kernel, flips, side),
        jax.ShapeDtypeStruct(queries.shape, jnp.bfloat16),
        SMALL,
        0,
        same,
        received,
        *got,
    )


def grouping(mesh, heads):
    rows, cols = mesh.shape["ht"], mesh.shape["wt"]
    group_rows = rows
    group_cols = heads // group_rows if heads % group_rows == 0 else 0
    if group_cols != 2 or cols % group_cols:
        return None
    return group_rows, group_cols, cols // group_cols


def solution(mesh):
    def program(queries, *rest):
        heads = queries.shape[2] // HD
        shape = grouping(mesh, heads)
        if shape is None or queries.shape[0] != mesh.shape["ht"] * (WIN // 2) or queries.shape[1] != mesh.shape["wt"] * (WIN // 4):
            placed = (P("ht", "wt", None),) * 3 + (P(None, "ht", "wt", None),) * 2 + (P(), P())
            return jax.shard_map(
                shards, mesh=mesh, in_specs=placed, out_specs=P("ht", "wt", None), check_vma=False
            )(queries, *rest)
        devices = mesh.devices.reshape(shape[0], shape[2], shape[1])
        split = Mesh(devices, ("ht", "far", "near"))
        tile = P("ht", ("far", "near"), None)
        past = P(None, "ht", ("far", "near"), None)
        step = jax.shard_map(
            functools.partial(head_step, shape),
            mesh=split,
            in_specs=(tile, tile, tile, past, past, P(), P()),
            out_specs=tile,
            check_vma=False,
        )
        return step(queries, *rest)

    return program
```

```python
import functools

import jax
import jax.numpy as jnp
from jax import lax
from jax.experimental import pallas as pl
from jax.experimental.pallas import tpu as pltpu
from jax.sharding import Mesh, PartitionSpec as P


HD = 128
WIN = 32


def with_halo(block, sides, width):
    for axis, dim in sides:
        count = lax.axis_size(axis)
        forward = [(i, i + 1) for i in range(count - 1)]
        backward = [(target, source) for source, target in forward]
        low = lax.ppermute(
            lax.slice_in_dim(block, block.shape[dim] - width, None, axis=dim), axis, forward
        )
        high = lax.ppermute(lax.slice_in_dim(block, 0, width, axis=dim), axis, backward)
        block = jnp.concatenate([low, block, high], axis=dim)
    return block


def window_allowed(row_start, col_start, frame_rows, frame_cols, tile_rows, tile_cols, half_win):
    ext_rows = jnp.arange(tile_rows + 2 * half_win, dtype=jnp.int32) - half_win
    ext_cols = jnp.arange(tile_cols + 2 * half_win, dtype=jnp.int32) - half_win
    query_rows = jnp.arange(tile_rows, dtype=jnp.int32)
    query_cols = jnp.arange(tile_cols, dtype=jnp.int32)
    row_delta = ext_rows[None, :] - query_rows[:, None]
    col_delta = ext_cols[None, :] - query_cols[:, None]
    global_rows = row_start + ext_rows
    global_cols = col_start + ext_cols
    row_valid = (
        (row_delta >= -half_win)
        & (row_delta < half_win)
        & ((global_rows >= 0) & (global_rows < frame_rows))[None, :]
    )
    col_valid = (
        (col_delta >= -half_win)
        & (col_delta < half_win)
        & ((global_cols >= 0) & (global_cols < frame_cols))[None, :]
    )
    allowed = row_valid[:, None, :, None] & col_valid[None, :, None, :]
    return allowed.reshape(
        tile_rows * tile_cols, (tile_rows + 2 * half_win) * (tile_cols + 2 * half_win)
    )


def attend(query_rows, keys_flat, values_flat, allowed, heads, head_dim):
    score_scale = head_dim ** (-0.5)

    def one_head(head_index):
        scores = (
            jnp.einsum("qd,kd->qk", query_rows, keys_flat, preferred_element_type=jnp.float32)
            * score_scale
        )
        scores = jnp.where(allowed, scores, -1e30)
        row_top = jnp.max(scores, axis=1, keepdims=True)
        weights_f = jnp.exp(scores - row_top)
        denominator = jnp.sum(weights_f, axis=1, keepdims=True)
        numerator = jnp.dot(
            weights_f.astype(jnp.bfloat16), values_flat, preferred_element_type=jnp.float32
        )
        return numerator / denominator

    outputs = lax.map(one_head, jnp.arange(heads, dtype=jnp.int32))
    return outputs.transpose(1, 0, 2).reshape(query_rows.shape[0], heads * head_dim)


def local_conv(padded, conv_weight, conv_bias, tile_rows, tile_cols):
    enhanced = jnp.zeros((tile_rows, tile_cols, padded.shape[2]), jnp.float32) + conv_bias
    for row_shift in range(3):
        for col_shift in range(3):
            enhanced = (
                enhanced
                + padded[
                    row_shift : row_shift + tile_rows, col_shift : col_shift + tile_cols
                ].astype(jnp.float32)
                * conv_weight[row_shift, col_shift]
            )
    return enhanced


def cycle_conv(values_new, conv_weight, conv_bias):
    tile_rows, tile_cols, _ = values_new.shape
    padded = with_halo(values_new, (("ht", 0), ("wt", 1)), 1)
    return local_conv(padded, conv_weight, conv_bias, tile_rows, tile_cols)


def shards(queries, keys_new, values_new, keys_cache, values_cache, conv_weight, conv_bias):
    tile_rows, tile_cols, channels = queries.shape
    frames = keys_cache.shape[0] + 1
    half_win = WIN // 2
    stacked = jnp.concatenate([keys_cache, keys_new[None], values_cache, values_new[None]], axis=0)
    row_start = lax.axis_index("ht") * tile_rows
    frame_rows = tile_rows * lax.axis_size("ht")
    frame_cols = tile_cols * lax.axis_size("wt")
    heads = channels // HD
    copies = lax.axis_size("wt") // heads
    bundle = jnp.concatenate([stacked, queries[None]], axis=0)
    members = bundle.shape[0]
    spread = bundle.reshape(members, tile_rows, tile_cols, 1, heads, HD)
    spread = jnp.broadcast_to(spread, (members, tile_rows, tile_cols, copies, heads, HD))
    spread = spread.reshape(members, tile_rows, tile_cols, copies * heads, HD)
    strips = lax.all_to_all(spread, "wt", split_axis=3, concat_axis=2, tiled=True)
    strips = strips.reshape(members, tile_rows, frame_cols, HD)
    device_index = lax.axis_index("wt")
    my_group = device_index // heads
    block_width = tile_cols * heads
    block_start = my_group * block_width
    padded_cols = jnp.pad(strips, ((0, 0), (0, 0), (half_win, half_win), (0, 0)))
    window = lax.dynamic_slice_in_dim(padded_cols, block_start, block_width + 2 * half_win, 2)
    query_part = window[2 * frames, :, half_win : half_win + block_width]
    region = with_halo(window[: 2 * frames], (("ht", 1),), half_win)

    def one_block(step):
        offset = step * tile_cols
        query_block = lax.dynamic_slice_in_dim(query_part, offset, tile_cols, 1).reshape(
            tile_rows * tile_cols, HD
        )
        sub = lax.dynamic_slice_in_dim(region, offset, tile_cols + 2 * half_win, 2)
        keys_flat = sub[:frames].reshape(-1, HD)
        values_flat = sub[frames:].reshape(-1, HD)
        allowed = window_allowed(
            row_start, block_start + offset, frame_rows, frame_cols, tile_rows, tile_cols, half_win
        )
        allowed = jnp.tile(allowed, (1, frames))
        result = attend(query_block, keys_flat, values_flat, allowed, 1, HD)
        return result.reshape(tile_rows, tile_cols, HD)

    blocks = lax.map(one_block, jnp.arange(heads, dtype=jnp.int32))
    payload = blocks.transpose(1, 0, 2, 3)
    payload = jnp.broadcast_to(payload[:, None], (tile_rows, copies, heads, tile_cols, HD))
    payload = payload.reshape(tile_rows, copies * heads, tile_cols, HD)
    returned = lax.all_to_all(
        payload.astype(jnp.bfloat16), "wt", split_axis=1, concat_axis=1, tiled=True
    ).astype(payload.dtype)
    own = lax.dynamic_slice_in_dim(returned, my_group * heads, heads, 1)
    combined = own.transpose(0, 2, 1, 3).reshape(tile_rows, tile_cols, channels)
    combined = combined + cycle_conv(values_new, conv_weight, conv_bias)
    return combined.astype(jnp.bfloat16)


LOG2E = 1.4426950408889634
NEG = -1e30
VMEM = pl.BlockSpec(memory_space=pltpu.VMEM)
FAR = pl.BlockSpec(memory_space=pltpu.HBM)
LIMIT = pltpu.CompilerParams(vmem_limit_bytes=8 * 1024 * 1024)
SMALL = pltpu.CompilerParams(vmem_limit_bytes=4 * 1024 * 1024)


def position(group_cols):
    return lax.axis_index("ht") * group_cols + lax.axis_index("near")


def place_of(group_cols, tile):
    side = group_cols
    flip = position(group_cols) ^ tile
    return lax.rem(flip // side, 2), lax.rem(flip, side) + flip // (2 * side) * side


def slot_of(group_cols, tile):
    beside, order = place_of(group_cols, tile)
    return beside * (lax.axis_size("ht") * group_cols // 2) + order


def pair_slot_of(group_cols, tile):
    beside, order = place_of(group_cols, tile)
    return order * 2 + beside


def first_is_right():
    return 1 - lax.rem(lax.axis_index("far"), 2)


class Window:
    def __init__(self, grid, tile, query_ref, pairs_ref):
        self.grid_rows, self.grid_cols = grid
        self.tile_rows, self.tile_cols = tile
        self.size = self.tile_rows * self.tile_cols
        self.query, self.pairs = query_ref, pairs_ref
        self.scale = HD ** (-0.5) * LOG2E
        query = lax.broadcasted_iota(jnp.int32, (self.size, self.size), 0)
        key = lax.broadcasted_iota(jnp.int32, (self.size, self.size), 1)
        self.upper = key // self.tile_cols >= query // self.tile_cols
        self.left = key % self.tile_cols >= query % self.tile_cols
        self.upper_one = self.upper.astype(jnp.float32).astype(jnp.bfloat16)

    def slot(self, row, col):
        return slot_of(self.grid_cols, row * self.grid_cols + col)

    def pair_slot(self, row, col):
        return pair_slot_of(self.grid_cols, row * self.grid_cols + col)

    def tile(self, member, row, col):
        return self.pairs[self.pair_slot(row, col), member].reshape(self.size, HD)

    def scores(self, row, col, cols):
        query = self.query[self.slot(row, col), pl.ds(0, self.tile_rows)].reshape(self.size, HD)
        frames = range(self.pairs.shape[1] // 2)
        up, down = row > 0, row + 1 < self.grid_rows
        rows = [r for r in (row - 1, row, row + 1) if 0 <= r < self.grid_rows]
        needed = [(f, r, i) for f in frames for i in range(len(cols)) for r in rows]
        keys = jnp.concatenate([self.tile(2 * f, r, cols[i][0]) for f, r, i in needed], axis=0)
        raw = lax.dot_general(query, keys, (((1,), (1,)), ((), ())), preferred_element_type=jnp.float32)
        scores = {key: raw[:, i * self.size : (i + 1) * self.size] for i, key in enumerate(needed)}
        blocks = []
        for f in frames:
            for i, (c, allowed) in enumerate(cols):
                found = [(False, scores[f, row, i])]
                if up or down:
                    above = scores[f, row - 1, i] if up else NEG
                    found.append((True, jnp.where(self.upper, above, scores[f, row + 1, i] if down else NEG)))
                for off_row, block in found:
                    if allowed is not None:
                        block = jnp.where(allowed, block, NEG)
                    blocks.append((f, off_row, c, block))
        top = blocks[0][3]
        for entry in blocks[1:]:
            top = jnp.maximum(top, entry[3])
        return row, up and down, down, blocks, jnp.max(top, axis=1, keepdims=True)

    def weigh(self, row, both, down, blocks, top):
        parts = []
        for f, off_row, c, block in blocks:
            weights = jnp.exp2((block - top) * self.scale).astype(jnp.bfloat16)
            if off_row and both:
                parts.append((f, row - 1, c, weights * self.upper_one))
                parts.append((f, row + 1, c, weights * (1 - self.upper_one)))
            elif off_row:
                parts.append((f, row + 1 if down else row - 1, c, weights))
            else:
                parts.append((f, row, c, weights))
        values = jnp.concatenate([self.tile(2 * f + 1, r, c) for f, r, c, _ in parts], axis=0)
        values = jnp.concatenate([values, jnp.ones_like(values)], axis=1)
        weights = jnp.concatenate([part for _, _, _, part in parts], axis=1)
        total = jnp.dot(weights, values, preferred_element_type=jnp.float32)
        return total[:, :HD] / total[:, HD:], top * self.scale + jnp.log2(total[:, HD:])

    def attend(self, tiles):
        held = None
        for place in [*tiles, None]:
            ready = self.scores(*place) if place else None
            if held:
                yield (held[0][0] * self.grid_cols + held[0][1], *self.weigh(*held[1]))
            held = (place, ready)

    def enhanced(self, row, col, weight_ref, bias_ref, beyond):
        shape = (self.tile_cols, HD)
        sub = lax.broadcasted_iota(jnp.int32, shape, 0)
        taps = [[weight_ref[a, pl.ds(b, 1), :] for b in range(3)] for a in range(3)]
        last = self.tile_cols - 1
        member = self.pairs.shape[1] - 1
        lines = []
        for key_row in range(row * self.tile_rows - 1, (row + 1) * self.tile_rows + 1):
            tile_row, line = key_row // self.tile_rows, key_row % self.tile_rows
            if tile_row < 0 or tile_row >= self.grid_rows:
                lines.append(None)
                continue

            def values(c):
                return self.pairs[self.pair_slot(tile_row, c), member, line].astype(jnp.float32)

            def edge(right, c):
                place = self.slot(tile_row, c), self.tile_rows + line // self.tile_cols
                first, second = (ref[place].astype(jnp.float32) for ref in beyond)
                packed = jnp.where(first_is_right() == right, first, second)
                return jnp.broadcast_to(packed[line % self.tile_cols : line % self.tile_cols + 1], shape)

            here = values(col)
            before = pltpu.roll(values(col - 1), 1, 0) if col > 0 else edge(0, self.grid_cols - 1)
            after = pltpu.roll(values(col + 1), last, 0) if col + 1 < self.grid_cols else edge(1, 0)
            low = jnp.where(sub == 0, before, pltpu.roll(here, 1, 0))
            high = jnp.where(sub == last, after, pltpu.roll(here, last, 0))
            lines.append((low, here, high))
        sums = []
        for line in range(self.tile_rows):
            total = jnp.broadcast_to(bias_ref[...], shape)
            for a in range(3):
                if lines[line + a] is not None:
                    for b in range(3):
                        total = total + lines[line + a][b] * taps[a][b]
            sums.append(total)
        return jnp.stack(sums, axis=0)


def visit_kernel(grid, tile, first, query_ref, pairs_ref, out_ref):
    window = Window(grid, tile, query_ref, pairs_ref)
    near = first_is_right() if first else 1 - first_is_right()
    allowed = window.left.astype(jnp.int32) == near
    tiles = []
    for row in range(grid[0]):
        tiles.append((row, 1 - near, [(near, None), (1 - near, allowed)]))
        tiles.append((row, near, [(near, allowed)]))
    size, count = window.size, grid[0] * grid[1]
    half = count // 2
    lane = lax.broadcasted_iota(jnp.int32, (size, HD), 1)
    levels = jnp.zeros((size, HD), jnp.float32)
    for index, part, level in window.attend(tiles):
        beside, order = place_of(grid[1], index)
        place = (1 - beside) * (half + 1) + order
        out_ref[place] = part.reshape(tile + (HD,)).astype(jnp.bfloat16)
        levels = jnp.where(lane == beside * half + order, level, levels)
    high = levels.astype(jnp.bfloat16).astype(jnp.float32)
    middle = (levels - high).astype(jnp.bfloat16).astype(jnp.float32)
    packed = high + pltpu.roll(middle, count, 1) + pltpu.roll(levels - high - middle, 2 * count, 1)
    out_ref[half] = packed.reshape(tile + (HD,)).astype(jnp.bfloat16)


def own_kernel(
    grid, tile, weight_ref, bias_ref, query_ref, pairs_ref, first_ref, second_ref, part_ref, level_ref, conv_ref
):
    window = Window(grid, tile, query_ref, pairs_ref)
    cols = [(c, None) for c in range(grid[1])]
    tiles = [(row, col, cols) for row in range(grid[0]) for col in range(grid[1])]
    for index, part, level in window.attend(tiles):
        part_ref[index], level_ref[index] = part, level
        row, col = index // grid[1], index % grid[1]
        conv = window.enhanced(row, col, weight_ref, bias_ref, (first_ref, second_ref))
        conv_ref[index] = conv.reshape(window.size, HD)


def join_kernel(grid, tile, far, flips, beside, part_ref, level_ref, conv_ref, first_ref, level_first_ref, second_ref, out_ref):
    size, count, side = tile[0] * tile[1], grid[0] * grid[1], grid[1]
    half = count // 2
    place = lax.axis_index("far")
    even = lax.rem(place, 2) == 0
    present = [~even | (place < far - 1), jnp.where(even, place > 0, place < far - 1)]
    packed = []
    for there, ref in zip(present, (level_first_ref, second_ref)):
        pack = ref[half].reshape(size, HD).astype(jnp.float32)
        level = pack + pltpu.roll(pack, HD - count, 1) + pltpu.roll(pack, HD - 2 * count, 1)
        packed.append(jnp.where(there, level, NEG))
    for order, flip in enumerate(flips):
        index = position(side) ^ (flip ^ (side if beside else 0))
        lane = order + (half if beside else 0)
        visits = [first_ref[order], second_ref[order + (0 if beside else half + 1)]]
        levels = [level_ref[index]]
        parts = [part_ref[index]]
        for visit, pack in zip(visits, packed):
            parts.append(visit.reshape(size, HD).astype(jnp.float32))
            levels.append(jnp.broadcast_to(pack[:, lane : lane + 1], (size, HD)))
        top = jnp.maximum(jnp.maximum(levels[0], levels[1]), levels[2])
        shares = [jnp.exp2(level - top) for level in levels]
        mixed = sum(share * part for share, part in zip(shares, parts)) / sum(shares)
        out_ref[order] = (mixed + conv_ref[index]).reshape(tile + (HD,)).astype(jnp.bfloat16)


def lanes(head):
    return pl.ds(pl.multiple_of(head * HD, HD), HD)


def pack_kernel(flips, side, *refs):
    count = len(flips)
    sources, buffers = refs[: -2 * count - 3], refs[-2 * count - 3 : -count - 3]
    messages, (beside_ref, held_ref, sems) = refs[-count - 3 : -3], refs[-3:]
    tile_rows, tile_cols, _ = sources[0].shape
    copies = [pltpu.make_async_copy(x, held_ref.at[i], sems.at[i]) for i, x in enumerate(sources)]
    for copy in copies:
        copy.start()
    heads = [[lanes(position(side) ^ (flip ^ beside)) for beside in (0, side)] for flip in flips]
    copies[0].wait()
    for buffer, pair in zip(buffers, heads):
        for other in range(2):
            buffer[other, pl.ds(0, tile_rows)] = held_ref[0, :, :, pair[other]]
    copies[1].wait()
    sub = lax.broadcasted_iota(jnp.int32, (tile_cols, HD), 0)
    for buffer, pair in zip(buffers, heads):
        for other in range(2):
            for start in range(0, tile_rows, tile_cols):
                packed = jnp.zeros((tile_cols, HD), jnp.float32)
                for line in range(tile_cols):
                    values = held_ref[1, start + line, :, pair[other]].astype(jnp.float32)
                    edge = jnp.where(lax.axis_index("near") == 0, values[:1], values[tile_cols - 1 :])
                    packed = jnp.where(sub == line, edge, packed)
                buffer[other, tile_rows + start // tile_cols] = packed.astype(jnp.bfloat16)
    for member, source in enumerate((*range(2, len(sources)), 1)):
        if source != 1:
            copies[source].wait()
        for i, pair in enumerate(heads):
            messages[i][0, member] = held_ref[source, :, :, pair[0]]
            beside_ref[i, member] = held_ref[source, :, :, pair[1]]


def split_kernel(*refs):
    mine_ref, other_ref = refs[-2:]
    for i, ref in enumerate(refs[:-2]):
        mine_ref[i] = ref[0]
        other_ref[i] = ref[1]


def unpack_kernel(flips, side, same_ref, beside_ref, *refs):
    out_ref = refs[-1]
    out_ref[:, :, lanes(position(side))] = same_ref[0]
    out_ref[:, :, lanes(position(side) ^ side)] = beside_ref[0]
    for i, flip in enumerate(flips[1:]):
        out_ref[:, :, lanes(position(side) ^ flip)] = refs[i][0]
        out_ref[:, :, lanes(position(side) ^ (flip ^ side))] = refs[i][1]


def head_step(shape, queries, keys_new, values_new, keys_cache, values_cache, conv_weight, conv_bias):
    group_rows, group_cols, far = shape
    tile_rows, tile_cols, channels = queries.shape
    heads = channels // HD
    grid, tile = (group_rows, group_cols), (tile_rows, tile_cols)
    size = tile_rows * tile_cols
    axes = ("ht", "near")
    block = (tile_rows, tile_cols, HD)
    side = group_cols
    flips = [flip for flip in range(heads) if not flip & side]
    near = lax.axis_index("near").astype(jnp.int32)
    me = lax.axis_index("ht").astype(jnp.int32) * group_cols + near

    def swap(x, flip):
        return lax.ppermute(x, axes, [(s, s ^ flip) for s in range(heads)])

    def call(kernel, out_shape, params, cost, *operands, space=(VMEM, VMEM), scratch=()):
        return pl.pallas_call(
            kernel,
            out_shape=out_shape,
            in_specs=[space[0]] * len(operands),
            out_specs=jax.tree.map(lambda _: space[1], out_shape),
            scratch_shapes=scratch,
            compiler_params=params,
            cost_estimate=pl.CostEstimate(flops=cost << 30, bytes_accessed=1 << 20, transcendentals=0),
        )(*operands)

    def stay(x):
        return pltpu.with_memory_space_constraint(x, pltpu.HBM)

    def send(buffers):
        got = [buffers[0]]
        for i in range(1, len(flips)):
            got.append(swap(buffers[i], flips[i]))
        return got

    def rounds(start):
        return [pair for i in range(start, far - 1, 2) for pair in ((i, i + 1), (i + 1, i))]

    first, second = rounds(0), rounds(1)
    edges = -(-tile_rows // tile_cols)

    sources = (queries, values_new, keys_cache[0], values_cache[0], keys_new)
    query_buffer = jax.ShapeDtypeStruct((2, tile_rows + edges, tile_cols, HD), jnp.bfloat16)
    message = jax.ShapeDtypeStruct((2, len(sources) - 1) + block, jnp.bfloat16)
    beside = jax.ShapeDtypeStruct((len(flips), len(sources) - 1) + block, jnp.bfloat16)
    packed = call(
        functools.partial(pack_kernel, flips, side),
        [query_buffer] * len(flips) + [message] * len(flips) + [beside],
        SMALL,
        0,
        *map(stay, sources),
        space=(FAR, VMEM),
        scratch=[pltpu.VMEM((len(sources),) + queries.shape, jnp.bfloat16), pltpu.SemaphoreType.DMA((len(sources),))],
    )
    beside = swap(packed[-1], side)
    got = send(packed[: len(flips)])
    messages = packed[len(flips) : -1]
    both = [lax.dynamic_update_slice_in_dim(m, beside[i : i + 1], 1, 0) for i, m in enumerate(messages)]
    pairs = send(both)
    pairs = jnp.concatenate(pairs, axis=0)
    half = jax.ShapeDtypeStruct((len(flips),) + query_buffer.shape[1:], jnp.bfloat16)
    mine, forward = call(split_kernel, [half, half], SMALL, 0, *got)
    forward = swap(forward, side)
    second_a = lax.ppermute(mine, "far", second)
    second_b = lax.ppermute(forward, "far", second)
    query = jnp.concatenate([mine, forward], axis=0)
    query_second = jnp.concatenate([second_a, second_b], axis=0)
    query_first = lax.ppermute(query, "far", first)
    weight = lax.dynamic_slice_in_dim(conv_weight, me * HD, HD, 2)
    bias = lax.dynamic_slice_in_dim(conv_bias.reshape(1, channels), me * HD, HD, 1)

    def visit(queries, is_first):
        kernel = functools.partial(visit_kernel, grid, tile, is_first)
        return call(kernel, jax.ShapeDtypeStruct((heads + 1,) + block, jnp.bfloat16), LIMIT, 4, queries, pairs)

    part = visit(query_second, False)
    home_second = lax.ppermute(part, "far", second)
    part = visit(query_first, True)
    half = len(flips) + 1
    home_first_a = lax.ppermute(part[:half], "far", first)
    home_first_b = lax.ppermute(part[half:], "far", first)
    part = jax.ShapeDtypeStruct((heads, size, HD), jnp.float32)
    kernel = functools.partial(own_kernel, grid, tile)
    own = call(kernel, [part] * 3, LIMIT, 4, weight, bias, query, pairs, query_first, query_second)
    result = jax.ShapeDtypeStruct((len(flips),) + block, jnp.bfloat16)

    def join(beside, tiles):
        kernel = functools.partial(join_kernel, grid, tile, far, flips, beside)
        return call(kernel, result, LIMIT, 1, *own, tiles, home_first_a, home_second)

    other = join(True, home_first_a)
    received = swap(other, side)
    same = join(False, home_first_b)
    got = []
    for i in range(1, len(flips)):
        got.append(swap(jnp.stack([same[i], received[i]]), flips[i]))
    return call(
        functools.partial(unpack_kernel, flips, side),
        jax.ShapeDtypeStruct(queries.shape, jnp.bfloat16),
        SMALL,
        0,
        same,
        received,
        *got,
    )


def grouping(mesh, heads):
    rows, cols = mesh.shape["ht"], mesh.shape["wt"]
    group_rows = rows
    group_cols = heads // group_rows if heads % group_rows == 0 else 0
    if group_cols != 2 or cols % group_cols:
        return None
    return group_rows, group_cols, cols // group_cols


def solution(mesh):
    def program(queries, *rest):
        heads = queries.shape[2] // HD
        shape = grouping(mesh, heads)
        if shape is None or queries.shape[0] != mesh.shape["ht"] * (WIN // 2) or queries.shape[1] != mesh.shape["wt"] * (WIN // 4):
            placed = (P("ht", "wt", None),) * 3 + (P(None, "ht", "wt", None),) * 2 + (P(), P())
            return jax.shard_map(
                shards, mesh=mesh, in_specs=placed, out_specs=P("ht", "wt", None), check_vma=False
            )(queries, *rest)
        devices = mesh.devices.reshape(shape[0], shape[2], shape[1])
        split = Mesh(devices, ("ht", "far", "near"))
        tile = P("ht", ("far", "near"), None)
        past = P(None, "ht", ("far", "near"), None)
        step = jax.shard_map(
            functools.partial(head_step, shape),
            mesh=split,
            in_specs=(tile, tile, tile, past, past, P(), P()),
            out_specs=tile,
            check_vma=False,
        )
        return step(queries, *rest)

    return program
```

```python
import functools

import jax
import jax.numpy as jnp
from jax import lax
from jax.experimental import pallas as pl
from jax.experimental.pallas import tpu as pltpu
from jax.sharding import Mesh, PartitionSpec as P


HD = 128
WIN = 32


def with_halo(block, sides, width):
    for axis, dim in sides:
        count = lax.axis_size(axis)
        forward = [(i, i + 1) for i in range(count - 1)]
        backward = [(target, source) for source, target in forward]
        low = lax.ppermute(
            lax.slice_in_dim(block, block.shape[dim] - width, None, axis=dim), axis, forward
        )
        high = lax.ppermute(lax.slice_in_dim(block, 0, width, axis=dim), axis, backward)
        block = jnp.concatenate([low, block, high], axis=dim)
    return block


def window_allowed(row_start, col_start, frame_rows, frame_cols, tile_rows, tile_cols, half_win):
    ext_rows = jnp.arange(tile_rows + 2 * half_win, dtype=jnp.int32) - half_win
    ext_cols = jnp.arange(tile_cols + 2 * half_win, dtype=jnp.int32) - half_win
    query_rows = jnp.arange(tile_rows, dtype=jnp.int32)
    query_cols = jnp.arange(tile_cols, dtype=jnp.int32)
    row_delta = ext_rows[None, :] - query_rows[:, None]
    col_delta = ext_cols[None, :] - query_cols[:, None]
    global_rows = row_start + ext_rows
    global_cols = col_start + ext_cols
    row_valid = (
        (row_delta >= -half_win)
        & (row_delta < half_win)
        & ((global_rows >= 0) & (global_rows < frame_rows))[None, :]
    )
    col_valid = (
        (col_delta >= -half_win)
        & (col_delta < half_win)
        & ((global_cols >= 0) & (global_cols < frame_cols))[None, :]
    )
    allowed = row_valid[:, None, :, None] & col_valid[None, :, None, :]
    return allowed.reshape(
        tile_rows * tile_cols, (tile_rows + 2 * half_win) * (tile_cols + 2 * half_win)
    )


def attend(query_rows, keys_flat, values_flat, allowed, heads, head_dim):
    score_scale = head_dim ** (-0.5)

    def one_head(head_index):
        scores = (
            jnp.einsum("qd,kd->qk", query_rows, keys_flat, preferred_element_type=jnp.float32)
            * score_scale
        )
        scores = jnp.where(allowed, scores, -1e30)
        row_top = jnp.max(scores, axis=1, keepdims=True)
        weights_f = jnp.exp(scores - row_top)
        denominator = jnp.sum(weights_f, axis=1, keepdims=True)
        numerator = jnp.dot(
            weights_f.astype(jnp.bfloat16), values_flat, preferred_element_type=jnp.float32
        )
        return numerator / denominator

    outputs = lax.map(one_head, jnp.arange(heads, dtype=jnp.int32))
    return outputs.transpose(1, 0, 2).reshape(query_rows.shape[0], heads * head_dim)


def local_conv(padded, conv_weight, conv_bias, tile_rows, tile_cols):
    enhanced = jnp.zeros((tile_rows, tile_cols, padded.shape[2]), jnp.float32) + conv_bias
    for row_shift in range(3):
        for col_shift in range(3):
            enhanced = (
                enhanced
                + padded[
                    row_shift : row_shift + tile_rows, col_shift : col_shift + tile_cols
                ].astype(jnp.float32)
                * conv_weight[row_shift, col_shift]
            )
    return enhanced


def cycle_conv(values_new, conv_weight, conv_bias):
    tile_rows, tile_cols, _ = values_new.shape
    padded = with_halo(values_new, (("ht", 0), ("wt", 1)), 1)
    return local_conv(padded, conv_weight, conv_bias, tile_rows, tile_cols)


def shards(queries, keys_new, values_new, keys_cache, values_cache, conv_weight, conv_bias):
    tile_rows, tile_cols, channels = queries.shape
    frames = keys_cache.shape[0] + 1
    half_win = WIN // 2
    stacked = jnp.concatenate([keys_cache, keys_new[None], values_cache, values_new[None]], axis=0)
    row_start = lax.axis_index("ht") * tile_rows
    frame_rows = tile_rows * lax.axis_size("ht")
    frame_cols = tile_cols * lax.axis_size("wt")
    heads = channels // HD
    copies = lax.axis_size("wt") // heads
    bundle = jnp.concatenate([stacked, queries[None]], axis=0)
    members = bundle.shape[0]
    spread = bundle.reshape(members, tile_rows, tile_cols, 1, heads, HD)
    spread = jnp.broadcast_to(spread, (members, tile_rows, tile_cols, copies, heads, HD))
    spread = spread.reshape(members, tile_rows, tile_cols, copies * heads, HD)
    strips = lax.all_to_all(spread, "wt", split_axis=3, concat_axis=2, tiled=True)
    strips = strips.reshape(members, tile_rows, frame_cols, HD)
    device_index = lax.axis_index("wt")
    my_group = device_index // heads
    block_width = tile_cols * heads
    block_start = my_group * block_width
    padded_cols = jnp.pad(strips, ((0, 0), (0, 0), (half_win, half_win), (0, 0)))
    window = lax.dynamic_slice_in_dim(padded_cols, block_start, block_width + 2 * half_win, 2)
    query_part = window[2 * frames, :, half_win : half_win + block_width]
    region = with_halo(window[: 2 * frames], (("ht", 1),), half_win)

    def one_block(step):
        offset = step * tile_cols
        query_block = lax.dynamic_slice_in_dim(query_part, offset, tile_cols, 1).reshape(
            tile_rows * tile_cols, HD
        )
        sub = lax.dynamic_slice_in_dim(region, offset, tile_cols + 2 * half_win, 2)
        keys_flat = sub[:frames].reshape(-1, HD)
        values_flat = sub[frames:].reshape(-1, HD)
        allowed = window_allowed(
            row_start, block_start + offset, frame_rows, frame_cols, tile_rows, tile_cols, half_win
        )
        allowed = jnp.tile(allowed, (1, frames))
        result = attend(query_block, keys_flat, values_flat, allowed, 1, HD)
        return result.reshape(tile_rows, tile_cols, HD)

    blocks = lax.map(one_block, jnp.arange(heads, dtype=jnp.int32))
    payload = blocks.transpose(1, 0, 2, 3)
    payload = jnp.broadcast_to(payload[:, None], (tile_rows, copies, heads, tile_cols, HD))
    payload = payload.reshape(tile_rows, copies * heads, tile_cols, HD)
    returned = lax.all_to_all(
        payload.astype(jnp.bfloat16), "wt", split_axis=1, concat_axis=1, tiled=True
    ).astype(payload.dtype)
    own = lax.dynamic_slice_in_dim(returned, my_group * heads, heads, 1)
    combined = own.transpose(0, 2, 1, 3).reshape(tile_rows, tile_cols, channels)
    combined = combined + cycle_conv(values_new, conv_weight, conv_bias)
    return combined.astype(jnp.bfloat16)


LOG2E = 1.4426950408889634
NEG = -1e30
VMEM = pl.BlockSpec(memory_space=pltpu.VMEM)
FAR = pl.BlockSpec(memory_space=pltpu.HBM)
LIMIT = pltpu.CompilerParams(vmem_limit_bytes=8 * 1024 * 1024)
SMALL = pltpu.CompilerParams(vmem_limit_bytes=4 * 1024 * 1024)


def position(group_cols):
    return lax.axis_index("ht") * group_cols + lax.axis_index("near")


def place_of(group_cols, tile):
    side = group_cols
    flip = position(group_cols) ^ tile
    return lax.rem(flip // side, 2), lax.rem(flip, side) + flip // (2 * side) * side


def slot_of(group_cols, tile):
    beside, order = place_of(group_cols, tile)
    return beside * (lax.axis_size("ht") * group_cols // 2) + order


def pair_slot_of(group_cols, tile):
    beside, order = place_of(group_cols, tile)
    return order * 2 + beside


def first_is_right():
    return 1 - lax.rem(lax.axis_index("far"), 2)


class Window:
    def __init__(self, grid, tile, query_ref, pairs_ref):
        self.grid_rows, self.grid_cols = grid
        self.tile_rows, self.tile_cols = tile
        self.size = self.tile_rows * self.tile_cols
        self.query, self.pairs = query_ref, pairs_ref
        self.scale = HD ** (-0.5) * LOG2E
        query = lax.broadcasted_iota(jnp.int32, (self.size, self.size), 0)
        key = lax.broadcasted_iota(jnp.int32, (self.size, self.size), 1)
        self.upper = key // self.tile_cols >= query // self.tile_cols
        self.left = key % self.tile_cols >= query % self.tile_cols
        self.upper_one = self.upper.astype(jnp.float32).astype(jnp.bfloat16)

    def slot(self, row, col):
        return slot_of(self.grid_cols, row * self.grid_cols + col)

    def pair_slot(self, row, col):
        return pair_slot_of(self.grid_cols, row * self.grid_cols + col)

    def tile(self, member, row, col):
        return self.pairs[self.pair_slot(row, col), member].reshape(self.size, HD)

    def scores(self, row, col, cols):
        query = self.query[self.slot(row, col), pl.ds(0, self.tile_rows)].reshape(self.size, HD)
        frames = range(self.pairs.shape[1] // 2)
        up, down = row > 0, row + 1 < self.grid_rows
        rows = [r for r in (row - 1, row, row + 1) if 0 <= r < self.grid_rows]
        needed = [(f, r, i) for f in frames for i in range(len(cols)) for r in rows]
        keys = jnp.concatenate([self.tile(2 * f, r, cols[i][0]) for f, r, i in needed], axis=0)
        raw = lax.dot_general(query, keys, (((1,), (1,)), ((), ())), preferred_element_type=jnp.float32)
        scores = {key: raw[:, i * self.size : (i + 1) * self.size] for i, key in enumerate(needed)}
        blocks = []
        for f in frames:
            for i, (c, allowed) in enumerate(cols):
                found = [(False, scores[f, row, i])]
                if up or down:
                    above = scores[f, row - 1, i] if up else NEG
                    found.append((True, jnp.where(self.upper, above, scores[f, row + 1, i] if down else NEG)))
                for off_row, block in found:
                    if allowed is not None:
                        block = jnp.where(allowed, block, NEG)
                    blocks.append((f, off_row, c, block))
        top = blocks[0][3]
        for entry in blocks[1:]:
            top = jnp.maximum(top, entry[3])
        return row, up and down, down, blocks, jnp.max(top, axis=1, keepdims=True)

    def weigh(self, row, both, down, blocks, top):
        parts = []
        for f, off_row, c, block in blocks:
            weights = jnp.exp2((block - top) * self.scale).astype(jnp.bfloat16)
            if off_row and both:
                parts.append((f, row - 1, c, weights * self.upper_one))
                parts.append((f, row + 1, c, weights * (1 - self.upper_one)))
            elif off_row:
                parts.append((f, row + 1 if down else row - 1, c, weights))
            else:
                parts.append((f, row, c, weights))
        values = jnp.concatenate([self.tile(2 * f + 1, r, c) for f, r, c, _ in parts], axis=0)
        values = jnp.concatenate([values, jnp.ones_like(values)], axis=1)
        weights = jnp.concatenate([part for _, _, _, part in parts], axis=1)
        total = jnp.dot(weights, values, preferred_element_type=jnp.float32)
        return total[:, :HD] / total[:, HD:], top * self.scale + jnp.log2(total[:, HD:])

    def attend(self, tiles):
        held = None
        for place in [*tiles, None]:
            ready = self.scores(*place) if place else None
            if held:
                yield (held[0][0] * self.grid_cols + held[0][1], *self.weigh(*held[1]))
            held = (place, ready)

    def enhanced(self, row, col, weight_ref, bias_ref, beyond):
        shape = (self.tile_cols, HD)
        sub = lax.broadcasted_iota(jnp.int32, shape, 0)
        taps = [[weight_ref[a, pl.ds(b, 1), :] for b in range(3)] for a in range(3)]
        last = self.tile_cols - 1
        member = self.pairs.shape[1] - 1
        lines = []
        for key_row in range(row * self.tile_rows - 1, (row + 1) * self.tile_rows + 1):
            tile_row, line = key_row // self.tile_rows, key_row % self.tile_rows
            if tile_row < 0 or tile_row >= self.grid_rows:
                lines.append(None)
                continue

            def values(c):
                return self.pairs[self.pair_slot(tile_row, c), member, line].astype(jnp.float32)

            def edge(right, c):
                back = self.tile_rows // self.tile_cols - line // self.tile_cols
                first, second = (ref[self.slot(tile_row, c), ref.shape[1] - back].astype(jnp.float32) for ref in beyond)
                packed = jnp.where(first_is_right() == right, first, second)
                return jnp.broadcast_to(packed[line % self.tile_cols : line % self.tile_cols + 1], shape)

            here = values(col)
            before = pltpu.roll(values(col - 1), 1, 0) if col > 0 else edge(0, self.grid_cols - 1)
            after = pltpu.roll(values(col + 1), last, 0) if col + 1 < self.grid_cols else edge(1, 0)
            low = jnp.where(sub == 0, before, pltpu.roll(here, 1, 0))
            high = jnp.where(sub == last, after, pltpu.roll(here, last, 0))
            lines.append((low, here, high))
        sums = []
        for line in range(self.tile_rows):
            total = jnp.broadcast_to(bias_ref[...], shape)
            for a in range(3):
                if lines[line + a] is not None:
                    for b in range(3):
                        total = total + lines[line + a][b] * taps[a][b]
            sums.append(total)
        return jnp.stack(sums, axis=0)


def visit_kernel(grid, tile, first, query_ref, pairs_ref, out_ref):
    window = Window(grid, tile, query_ref, pairs_ref)
    near = first_is_right() if first else 1 - first_is_right()
    allowed = window.left.astype(jnp.int32) == near
    tiles = []
    for row in range(grid[0]):
        tiles.append((row, 1 - near, [(near, None), (1 - near, allowed)]))
        tiles.append((row, near, [(near, allowed)]))
    size, count = window.size, grid[0] * grid[1]
    half = count // 2
    lane = lax.broadcasted_iota(jnp.int32, (size, HD), 1)
    levels = jnp.zeros((size, HD), jnp.float32)
    for index, part, level in window.attend(tiles):
        beside, order = place_of(grid[1], index)
        place = (1 - beside) * (half + 1) + order
        out_ref[place] = part.reshape(tile + (HD,)).astype(jnp.bfloat16)
        levels = jnp.where(lane == beside * half + order, level, levels)
    high = levels.astype(jnp.bfloat16).astype(jnp.float32)
    middle = (levels - high).astype(jnp.bfloat16).astype(jnp.float32)
    packed = high + pltpu.roll(middle, count, 1) + pltpu.roll(levels - high - middle, 2 * count, 1)
    out_ref[half] = packed.reshape(tile + (HD,)).astype(jnp.bfloat16)


def own_kernel(
    grid, tile, weight_ref, bias_ref, query_ref, pairs_ref, first_ref, second_ref, part_ref, level_ref, conv_ref
):
    window = Window(grid, tile, query_ref, pairs_ref)
    cols = [(c, None) for c in range(grid[1])]
    tiles = [(row, col, cols) for row in range(grid[0]) for col in range(grid[1])]
    for index, part, level in window.attend(tiles):
        part_ref[index], level_ref[index] = part, level
        row, col = index // grid[1], index % grid[1]
        conv = window.enhanced(row, col, weight_ref, bias_ref, (first_ref, second_ref))
        conv_ref[index] = conv.reshape(window.size, HD)


def join_kernel(grid, tile, far, flips, beside, part_ref, level_ref, conv_ref, first_ref, level_first_ref, second_ref, out_ref):
    size, count, side = tile[0] * tile[1], grid[0] * grid[1], grid[1]
    half = count // 2
    place = lax.axis_index("far")
    even = lax.rem(place, 2) == 0
    present = [~even | (place < far - 1), jnp.where(even, place > 0, place < far - 1)]
    packed = []
    for there, ref in zip(present, (level_first_ref, second_ref)):
        pack = ref[half].reshape(size, HD).astype(jnp.float32)
        level = pack + pltpu.roll(pack, HD - count, 1) + pltpu.roll(pack, HD - 2 * count, 1)
        packed.append(jnp.where(there, level, NEG))
    for order, flip in enumerate(flips):
        index = position(side) ^ (flip ^ (side if beside else 0))
        lane = order + (half if beside else 0)
        visits = [first_ref[order], second_ref[order + (0 if beside else half + 1)]]
        levels = [level_ref[index]]
        parts = [part_ref[index]]
        for visit, pack in zip(visits, packed):
            parts.append(visit.reshape(size, HD).astype(jnp.float32))
            levels.append(jnp.broadcast_to(pack[:, lane : lane + 1], (size, HD)))
        top = jnp.maximum(jnp.maximum(levels[0], levels[1]), levels[2])
        shares = [jnp.exp2(level - top) for level in levels]
        mixed = sum(share * part for share, part in zip(shares, parts)) / sum(shares)
        out_ref[order] = (mixed + conv_ref[index]).reshape(tile + (HD,)).astype(jnp.bfloat16)


def lanes(head):
    return pl.ds(pl.multiple_of(head * HD, HD), HD)


def pack_kernel(flips, side, *refs):
    count = len(flips)
    sources, buffers = refs[: -2 * count - 3], refs[-2 * count - 3 : -count - 3]
    messages, (beside_ref, held_ref, sems) = refs[-count - 3 : -3], refs[-3:]
    tile_rows, tile_cols, _ = sources[0].shape
    copies = [pltpu.make_async_copy(x, held_ref.at[i], sems.at[i]) for i, x in enumerate(sources)]
    for copy in copies:
        copy.start()
    heads = [[lanes(position(side) ^ (flip ^ beside)) for beside in (0, side)] for flip in flips]
    copies[0].wait()
    for buffer, pair in zip(buffers, heads):
        for other in range(2):
            buffer[other, pl.ds(0, tile_rows)] = held_ref[0, :, :, pair[other]]
    copies[1].wait()
    sub = lax.broadcasted_iota(jnp.int32, (tile_cols, HD), 0)
    for buffer, pair in zip(buffers, heads):
        for other in range(2):
            for start in range(0, tile_rows, tile_cols):
                packed = jnp.zeros((tile_cols, HD), jnp.float32)
                for line in range(tile_cols):
                    values = held_ref[1, start + line, :, pair[other]].astype(jnp.float32)
                    edge = jnp.where(lax.axis_index("near") == 0, values[:1], values[tile_cols - 1 :])
                    packed = jnp.where(sub == line, edge, packed)
                buffer[other, tile_rows + start // tile_cols] = packed.astype(jnp.bfloat16)
    for member, source in enumerate((*range(2, len(sources)), 1)):
        if source != 1:
            copies[source].wait()
        for i, pair in enumerate(heads):
            messages[i][0, member] = held_ref[source, :, :, pair[0]]
            beside_ref[i, member] = held_ref[source, :, :, pair[1]]


def split_kernel(*refs):
    mine_ref, other_ref = refs[-2:]
    for i, ref in enumerate(refs[:-2]):
        mine_ref[i] = ref[0]
        other_ref[i] = ref[1]


def unpack_kernel(flips, side, same_ref, beside_ref, *refs):
    out_ref = refs[-1]
    out_ref[:, :, lanes(position(side))] = same_ref[0]
    out_ref[:, :, lanes(position(side) ^ side)] = beside_ref[0]
    for i, flip in enumerate(flips[1:]):
        out_ref[:, :, lanes(position(side) ^ flip)] = refs[i][0]
        out_ref[:, :, lanes(position(side) ^ (flip ^ side))] = refs[i][1]


def head_step(shape, queries, keys_new, values_new, keys_cache, values_cache, conv_weight, conv_bias):
    group_rows, group_cols, far = shape
    tile_rows, tile_cols, channels = queries.shape
    heads = channels // HD
    grid, tile = (group_rows, group_cols), (tile_rows, tile_cols)
    size = tile_rows * tile_cols
    axes = ("ht", "near")
    block = (tile_rows, tile_cols, HD)
    side = group_cols
    flips = [flip for flip in range(heads) if not flip & side]
    near = lax.axis_index("near").astype(jnp.int32)
    me = lax.axis_index("ht").astype(jnp.int32) * group_cols + near

    def swap(x, flip):
        return lax.ppermute(x, axes, [(s, s ^ flip) for s in range(heads)])

    def call(kernel, out_shape, params, cost, *operands, space=(VMEM, VMEM), scratch=()):
        return pl.pallas_call(
            kernel,
            out_shape=out_shape,
            in_specs=[space[0]] * len(operands),
            out_specs=jax.tree.map(lambda _: space[1], out_shape),
            scratch_shapes=scratch,
            compiler_params=params,
            cost_estimate=pl.CostEstimate(flops=cost << 30, bytes_accessed=1 << 20, transcendentals=0),
        )(*operands)

    def stay(x):
        return pltpu.with_memory_space_constraint(x, pltpu.HBM)

    def send(buffers):
        got = [buffers[0]]
        for i in range(1, len(flips)):
            got.append(swap(buffers[i], flips[i]))
        return got

    def rounds(start):
        return [pair for i in range(start, far - 1, 2) for pair in ((i, i + 1), (i + 1, i))]

    first, second = rounds(0), rounds(1)
    edges = -(-tile_rows // tile_cols)

    sources = (queries, values_new, keys_cache[0], values_cache[0], keys_new)
    query_buffer = jax.ShapeDtypeStruct((2, tile_rows + edges, tile_cols, HD), jnp.bfloat16)
    message = jax.ShapeDtypeStruct((2, len(sources) - 1) + block, jnp.bfloat16)
    beside = jax.ShapeDtypeStruct((len(flips), len(sources) - 1) + block, jnp.bfloat16)
    packed = call(
        functools.partial(pack_kernel, flips, side),
        [query_buffer] * len(flips) + [message] * len(flips) + [beside],
        SMALL,
        0,
        *map(stay, sources),
        space=(FAR, VMEM),
        scratch=[pltpu.VMEM((len(sources),) + queries.shape, jnp.bfloat16), pltpu.SemaphoreType.DMA((len(sources),))],
    )
    beside = swap(packed[-1], side)
    got = send(packed[: len(flips)])
    messages = packed[len(flips) : -1]
    both = [lax.dynamic_update_slice_in_dim(m, beside[i : i + 1], 1, 0) for i, m in enumerate(messages)]
    pairs = send(both)
    pairs = jnp.concatenate(pairs, axis=0)
    half = jax.ShapeDtypeStruct((len(flips),) + query_buffer.shape[1:], jnp.bfloat16)
    mine, forward = call(split_kernel, [half, half], SMALL, 0, *got)
    forward = swap(forward, side)
    second_a = lax.ppermute(mine[:, :tile_rows], "far", second)
    second_b = lax.ppermute(forward[:, :tile_rows], "far", second)
    query = jnp.concatenate([mine, forward], axis=0)
    edges_second = lax.ppermute(query[:, tile_rows:], "far", second)
    query_second = jnp.concatenate([second_a, second_b], axis=0)
    query_first = lax.ppermute(query, "far", first)
    weight = lax.dynamic_slice_in_dim(conv_weight, me * HD, HD, 2)
    bias = lax.dynamic_slice_in_dim(conv_bias.reshape(1, channels), me * HD, HD, 1)

    def visit(queries, is_first):
        kernel = functools.partial(visit_kernel, grid, tile, is_first)
        return call(kernel, jax.ShapeDtypeStruct((heads + 1,) + block, jnp.bfloat16), LIMIT, 4, queries, pairs)

    part = visit(query_second, False)
    home_second = lax.ppermute(part, "far", second)
    part = visit(query_first, True)
    half = len(flips) + 1
    home_first_a = lax.ppermute(part[:half], "far", first)
    home_first_b = lax.ppermute(part[half:], "far", first)
    part = jax.ShapeDtypeStruct((heads, size, HD), jnp.float32)
    kernel = functools.partial(own_kernel, grid, tile)
    own = call(kernel, [part] * 3, LIMIT, 4, weight, bias, query, pairs, query_first, edges_second)
    result = jax.ShapeDtypeStruct((len(flips),) + block, jnp.bfloat16)

    def join(beside, tiles):
        kernel = functools.partial(join_kernel, grid, tile, far, flips, beside)
        return call(kernel, result, LIMIT, 1, *own, tiles, home_first_a, home_second)

    other = join(True, home_first_a)
    received = swap(other, side)
    same = join(False, home_first_b)
    got = []
    for i in range(1, len(flips)):
        got.append(swap(jnp.stack([same[i], received[i]]), flips[i]))
    return call(
        functools.partial(unpack_kernel, flips, side),
        jax.ShapeDtypeStruct(queries.shape, jnp.bfloat16),
        SMALL,
        0,
        same,
        received,
        *got,
    )


def grouping(mesh, heads):
    rows, cols = mesh.shape["ht"], mesh.shape["wt"]
    group_rows = rows
    group_cols = heads // group_rows if heads % group_rows == 0 else 0
    if group_cols != 2 or cols % group_cols:
        return None
    return group_rows, group_cols, cols // group_cols


def solution(mesh):
    def program(queries, *rest):
        heads = queries.shape[2] // HD
        shape = grouping(mesh, heads)
        if shape is None or queries.shape[0] != mesh.shape["ht"] * (WIN // 2) or queries.shape[1] != mesh.shape["wt"] * (WIN // 4):
            placed = (P("ht", "wt", None),) * 3 + (P(None, "ht", "wt", None),) * 2 + (P(), P())
            return jax.shard_map(
                shards, mesh=mesh, in_specs=placed, out_specs=P("ht", "wt", None), check_vma=False
            )(queries, *rest)
        devices = mesh.devices.reshape(shape[0], shape[2], shape[1])
        split = Mesh(devices, ("ht", "far", "near"))
        tile = P("ht", ("far", "near"), None)
        past = P(None, "ht", ("far", "near"), None)
        step = jax.shard_map(
            functools.partial(head_step, shape),
            mesh=split,
            in_specs=(tile, tile, tile, past, past, P(), P()),
            out_specs=tile,
            check_vma=False,
        )
        return step(queries, *rest)

    return program
```
